32 devices in a mesh: dp: 8 (over z, x), mp: 4 (over y, core).
Axes of the slice: x: 2, y: 2, z: 4, core: 2. Of those that a mesh axis runs over, the one named last changes fastest.
Arguments:
- tokens: bfloat16 [32768, 768], P('dp'), may hold values from -6 to 6
- segment: int32 [32768], P('dp'), may hold values from 0 to 8, as said below
- ln1_gain: bfloat16 [768], P('mp'), may hold values from 0.5 to 1.5
- ln1_bias: bfloat16 [768], P('mp'), may hold values from -2 to 2
- w_qkv: bfloat16 [3, 768, 768], P(None, None, 'mp'), may hold values from -0.21875 to 0.21875
- b_qv: bfloat16 [2, 768], P(None, 'mp'), may hold values from -2 to 2
- w_out: bfloat16 [768, 768], P('mp'), may hold values from -0.875 to 0.875
- b_out: bfloat16 [768], P('mp'), may hold values from -2 to 2
- ln2_gain: bfloat16 [768], P('mp'), may hold values from 0.5 to 1.5
- ln2_bias: bfloat16 [768], P('mp'), may hold values from -2 to 2
- w_up: bfloat16 [768, 3072], P(None, 'mp'), may hold values from -0.21875 to 0.21875
- b_up: bfloat16 [3072], P('mp'), may hold values from -3 to 3
- w_down: bfloat16 [3072, 768], P('mp'), may hold values from -0.109375 to 0.109375
- b_down: bfloat16 [768], P('mp'), may hold values from -2 to 2
- cotangent: bfloat16 [32768, 768], P(('dp', 'mp')), may hold values from -6 to 6
Outputs:
- output: bfloat16 [32768, 768], P(('dp', 'mp'))
- grad_x: float32 [32768, 768], P(('dp', 'mp'))
- grad_ln1_gain: float32 [768], P('mp')
- grad_ln1_bias: float32 [768], P('mp')
- grad_w_qkv: float32 [3, 768, 768], P(None, None, 'mp')
- grad_b_qv: float32 [2, 768], P(None, 'mp')
- grad_w_out: float32 [768, 768], P('mp')
- grad_b_out: float32 [768], P('mp')
- grad_ln2_gain: float32 [768], P('mp')
- grad_ln2_bias: float32 [768], P('mp')
- grad_w_up: float32 [768, 3072], P(None, 'mp')
- grad_b_up: float32 [3072], P('mp')
- grad_w_down: float32 [3072, 768], P('mp')
- grad_b_down: float32 [768], P('mp')
The draws below stay inside these ranges and needn't reach their ends.
Inputs may be any that keep to these rules, and one draw needn't show every extreme that they name: `segment`: within each aligned sequence of 512 rows the numbers never fall except to 0; 0 marks padding rows, which stand at the end of a sequence.
All inputs are finite; a program needn't handle non-finite values.
Results may differ from the reference program's by a relative error of at most 0.018.
Values may be sent and summed in bfloat16 or wider, within the bound.
A program may use at most 256 MiB of HBM per device.

```python
import jax
import jax.numpy as jnp
from jax import lax

D = 768
HEADS = 12
FF = 3072
HD = 64
LEN = 512
SEQ_DEV = 8
TOKENS = 32768


def draw_segment(key, part):
    count = TOKENS // LEN
    cut_key, pad_key = jax.random.split(jax.random.fold_in(key, 17))
    cuts = jax.random.randint(cut_key, (count, 7), 1, LEN)
    pads = jax.random.randint(pad_key, (count, 1), 0, LEN // 6 + 1)
    places = jnp.arange(LEN, dtype=jnp.int32)[None, :]
    numbers = 1 + jnp.sum((cuts[:, :, None] <= places[:, None, :]).astype(jnp.int32), axis=1)
    numbers = jnp.where(places >= LEN - pads, 0, numbers)
    return numbers.reshape(TOKENS).astype(jnp.int32)


def steps_of(rng, extent, cuts, low, largest):
    loudness, own = 1.0, jax.random.fold_in(rng, 6)
    for dim, parts in cuts:
        draws = jnp.exp(jax.random.uniform(jax.random.fold_in(own, dim), (parts,), jnp.float32, low / len(cuts), largest / len(cuts)))
        loudness = loudness * jnp.repeat(draws, extent[dim] // parts).reshape([-1 if axis == dim else 1 for axis in range(len(extent))])
    return loudness


def gaussian(stream_key, shape, deviation, most, cuts=(), kind=jnp.bfloat16):
    loudness = steps_of(stream_key, shape, cuts, -0.22, 0.18) if cuts else 1.0
    values = jax.random.normal(stream_key, shape, jnp.float32) * deviation * loudness
    return jnp.minimum(jnp.maximum(values, -most), most).astype(kind)


def setup_inputs(seed: int = 0) -> dict:
    splits = jax.random.split(jax.random.key(seed), 16)
    tokens = gaussian(splits[0], (TOKENS, D), 1.0, 6.0, ((0, 8),))
    segment = draw_segment(jax.random.fold_in(splits[15], 71), 0)
    ln1_gain = jnp.clip(1.0 + 0.1 * jax.random.normal(splits[2], (D,), jnp.float32), 0.5, 1.5).astype(jnp.bfloat16)
    ln1_bias = gaussian(splits[3], (D,), 0.3, 2.0, ((0, 4),))
    w_qkv = gaussian(splits[4], (3, D, D), D ** -0.5, 0.21875, ((2, 4),))
    b_qv = gaussian(splits[5], (2, D), 0.3, 2.0, ((1, 4),))
    w_out = gaussian(splits[6], (D, D), (D // 16) ** -0.5, 0.875, ((0, 4),))
    b_out = gaussian(splits[7], (D,), 0.3, 2.0, ((0, 4),))
    ln2_gain = jnp.clip(1.0 + 0.1 * jax.random.normal(splits[8], (D,), jnp.float32), 0.5, 1.5).astype(jnp.bfloat16)
    ln2_bias = gaussian(splits[9], (D,), 0.3, 2.0, ((0, 4),))
    w_up = gaussian(splits[10], (D, FF), D ** -0.5, 0.21875, ((1, 4),))
    b_up = gaussian(splits[11], (FF,), 0.5, 3.0, ((0, 4),))
    w_down = gaussian(splits[12], (FF, D), FF ** -0.5, 0.109375, ((0, 4),))
    b_down = gaussian(splits[13], (D,), 0.3, 2.0, ((0, 4),))
    cotangent = gaussian(splits[14], (TOKENS, D), 1.0, 6.0, ((0, 32),))
    return {"tokens": tokens, "segment": segment, "ln1_gain": ln1_gain, "ln1_bias": ln1_bias, "w_qkv": w_qkv, "b_qv": b_qv, "w_out": w_out, "b_out": b_out, "ln2_gain": ln2_gain, "ln2_bias": ln2_bias, "w_up": w_up, "b_up": b_up, "w_down": w_down, "b_down": b_down, "cotangent": cotangent}


@jax.custom_vjp
def low(v):
    return lax.optimization_barrier(v.astype(jnp.bfloat16)).astype(jnp.float32)

@jax.custom_vjp
def low_back(v):
    return v

def low_keep(v):
    return (low(v), None)

def low_pass(kept, grad):
    return (grad,)

def back_keep(v):
    return (v, None)

def back_low(kept, grad):
    return (low(grad),)
low.defvjp(low_keep, low_pass)
low_back.defvjp(back_keep, back_low)

def exact_dot(left, right):
    return jnp.dot(left, right, precision=lax.Precision.HIGHEST, preferred_element_type=jnp.float32)

def layer_norm(values, norm_gain, norm_shift):
    centered = values - lax.optimization_barrier(jnp.mean(values, axis=-1, keepdims=True))
    spread = lax.optimization_barrier(jnp.mean(centered * centered, axis=-1, keepdims=True))
    return centered * lax.rsqrt(spread + 1e-06) * norm_gain + norm_shift

def attend_sequence(entries):
    query_heads, key_heads, value_heads, segment = entries
    score_scale = HD ** (-0.5)
    scores = jnp.einsum('qhd,khd->hqk', query_heads, key_heads, precision=lax.Precision.HIGHEST) * score_scale
    scores = low_back(scores)
    places = jnp.arange(LEN, dtype=jnp.int32)
    allowed = (segment[:, None] == segment[None, :]) & (segment[None, :] != 0) | (places[:, None] == places[None, :])
    masked = jnp.where(allowed[None], scores, -1e+30)
    row_max = lax.optimization_barrier(jnp.max(masked, axis=-1, keepdims=True))
    expo_scores = jnp.exp(masked - row_max)
    attn_probs = expo_scores / lax.optimization_barrier(jnp.sum(expo_scores, axis=-1, keepdims=True))
    return jnp.einsum('hqk,khd->qhd', low(attn_probs), value_heads, precision=lax.Precision.HIGHEST)

def forward(inputs, segment, ln1_gain, ln1_bias, w_qkv, b_qv, w_out, b_out, ln2_gain, ln2_bias, w_up, b_up, w_down, b_down):
    row_count = inputs.shape[0]
    sequences = row_count // LEN
    normed = low(layer_norm(inputs, ln1_gain, ln1_bias))
    query = low_back(low(exact_dot(normed, w_qkv[0]) + b_qv[0]))
    key_rows = low_back(low(exact_dot(normed, w_qkv[1])))
    value_rows = low_back(low(exact_dot(normed, w_qkv[2]) + b_qv[1]))
    shaped = (sequences, LEN, HEADS, HD)
    attended = lax.map(jax.checkpoint(attend_sequence), (query.reshape(shaped), key_rows.reshape(shaped), value_rows.reshape(shaped), segment.reshape(sequences, LEN)))
    attended = low_back(low(attended.reshape(row_count, D)))
    hidden = inputs + low_back(exact_dot(attended, w_out)) + b_out
    normed_two = low(layer_norm(hidden, ln2_gain, ln2_bias))
    up_proj = low_back(exact_dot(normed_two, w_up) + b_up)
    active = low(jax.nn.gelu(up_proj, approximate=False))
    return hidden + exact_dot(active, w_down) + b_down

def reference(tokens, segment, ln1_gain, ln1_bias, w_qkv, b_qv, w_out, b_out, ln2_gain, ln2_bias, w_up, b_up, w_down, b_down, cotangent):
    params = tuple((member.astype(jnp.float32) for member in (ln1_gain, ln1_bias, w_qkv, b_qv, w_out, b_out, ln2_gain, ln2_bias, w_up, b_up, w_down, b_down)))
    group_rows = SEQ_DEV * LEN
    groups = TOKENS // group_rows
    stacked = (tokens.reshape(groups, group_rows, D), segment.reshape(groups, group_rows), cotangent.reshape(groups, group_rows, D))

    def group_step(running, entries):
        group_tokens, group_segment, group_cot = entries

        def local_layer(inputs, *weights):
            return forward(inputs, group_segment, *weights)
        result, pull_back = jax.vjp(local_layer, group_tokens.astype(jnp.float32), *params)
        gradients = pull_back(group_cot.astype(jnp.float32))
        running = tuple((summed + addend for summed, addend in zip(running, gradients[1:])))
        return (running, (result.astype(jnp.bfloat16), gradients[0]))
    initial = tuple((jnp.zeros(member.shape, jnp.float32) for member in params))
    totals, (outputs, input_grads) = lax.scan(group_step, initial, stacked)
    return (outputs.reshape(TOKENS, D), input_grads.reshape(TOKENS, D), totals[0], totals[1], totals[2], totals[3], totals[4], totals[5], totals[6], totals[7], totals[8], totals[9], totals[10], totals[11])
```

```python
import jax
import jax.numpy as jnp
from jax import lax
from jax.experimental import pallas as pl
from jax.experimental.pallas import tpu as pltpu
from jax.sharding import PartitionSpec as P

HD = 64
LEN = 512
F32 = jnp.float32
BF16 = jnp.bfloat16
VMEM_LIMIT = 64 * 1024 * 1024 - 128 * 1024


def nn(left, right):
    return jnp.dot(left, right, preferred_element_type=F32)


def nt(left, right):
    return lax.dot_general(left, right, (((1,), (1,)), ((), ())), preferred_element_type=F32)


def tn(left, right):
    return lax.dot_general(left, right, (((0,), (0,)), ((), ())), preferred_element_type=F32)


def rows_of(index, count):
    return pl.ds(pl.multiple_of(index * count, count), count)


def normal_of(values):
    centered = values - jnp.mean(values, axis=-1, keepdims=True)
    spread = jnp.mean(centered * centered, axis=-1, keepdims=True)
    inverse = lax.rsqrt(spread + 1e-06)
    return centered * inverse, inverse


def norm_input_back(normal, inverse, scaled):
    inner = jnp.mean(scaled * normal, axis=-1, keepdims=True)
    return inverse * (scaled - jnp.mean(scaled, axis=-1, keepdims=True) - normal * inner)


def column_sum(values):
    return jnp.sum(values, axis=0, keepdims=True)


def each(count, body):
    lax.fori_loop(0, count, lambda i, carry: (body(i), carry)[1], 0)


def mask_bias(bias, seg_col, seg_row, sequence):
    rows = rows_of(sequence, LEN)
    one = seg_col[rows, :]
    other = seg_row[pl.ds(sequence, 1), :]
    row_ids = lax.broadcasted_iota(jnp.int32, (LEN, LEN), 0)
    col_ids = lax.broadcasted_iota(jnp.int32, (LEN, LEN), 1)
    allowed = ((one == other) & (other != 0)) | (row_ids == col_ids)
    bias[...] = jnp.where(allowed, 0.0, -1e30)


def forward_kernel(
    x, seg_col, seg_row, wqkv, w_out, g1, b1, bqv, b_out, g2, b2,
    normed, qs, ks, vs, stats, attended, hidden, n2, bias,
):
    count = x.shape[0]
    tile = 256
    sequences = count // LEN
    pairs = x.shape[1] // 128

    def ln_one(i):
        r = rows_of(i, tile)
        normal, _ = normal_of(x[r, :].astype(F32))
        normed[r, :] = (normal * g1[...] + b1[...]).astype(BF16)

    each(count // tile, ln_one)

    def project(i):
        r = rows_of(i, LEN)
        value = normed[r, :]
        qs[r, :] = ((nt(value, wqkv[0]) + bqv[0:1, :]).astype(BF16).astype(F32) * (HD**-0.5)).astype(BF16)
        ks[r, :] = nt(value, wqkv[1]).astype(BF16)
        vs[r, :] = (nt(value, wqkv[2]) + bqv[1:2, :]).astype(BF16)

    each(count // LEN, project)
    lane = lax.broadcasted_iota(jnp.int32, (LEN, 128), 1)
    first = lane < HD

    def sequence_step(s):
        mask_bias(bias, seg_col, seg_row, s)
        r = rows_of(s, LEN)
        stats[r, :] = jnp.zeros((LEN, 128), F32)

        def pair_step(p):
            c = rows_of(p, 128)
            q2, k2, v2 = qs[r, c], ks[r, c], vs[r, c]
            results = []
            kept = stats[r, :]
            for half in range(2):
                mine = first if half == 0 else ~first
                scores = nt(jnp.where(mine, q2, jnp.zeros_like(q2)), k2) + bias[...]
                top = jnp.max(scores, axis=-1, keepdims=True)
                expo = jnp.exp(scores - top)
                total = jnp.sum(expo, axis=-1, keepdims=True)
                results.append(nn(expo.astype(BF16), v2) * (1.0 / total))
                kept = jnp.where(lane == 2 * p + half, top + jnp.log(total), kept)
            stats[r, :] = kept
            attended[r, c] = jnp.where(first, results[0], results[1]).astype(BF16)

        each(pairs, pair_step)

    each(sequences, sequence_step)

    def out_step(i):
        r = rows_of(i, tile)
        value = x[r, :].astype(F32) + nn(attended[r, :], w_out[...]) + b_out[...]
        hidden[r, :] = value
        normal, _ = normal_of(value)
        n2[r, :] = (normal * g2[...] + b2[...]).astype(BF16)

    each(count // tile, out_step)


def feed_kernel(
    n2, cot, w_up, w_down, b_up, b_down, hidden, attended, w_out, g2,
    out, grad_hidden, grad_att, gw_down, gw_up, gw_out, vec,
    act, gup,
):
    count, width = n2.shape
    groups = w_up.shape[0]
    piece = 256
    per_group = w_up.shape[2] // piece
    vec[...] = jnp.zeros_like(vec)

    def chunk(j):
        m, part = j // per_group, j % per_group
        c = rows_of(part, piece)
        whole = rows_of(j, piece)
        wu, wd = w_up[m, :, c], w_down[m, c, :]
        bias = b_up[pl.ds(m, 1), c]

        def rows_step(i):
            r = rows_of(i, LEN)
            up = nn(n2[r, :], wu) + bias
            half_cdf = 0.5 * (1.0 + lax.erf(up * (0.5**0.5)))
            slope = half_cdf + up * (jnp.exp(-0.5 * up * up) * 0.3989422804014327)
            act[r, whole] = (up * half_cdf).astype(BF16)
            grad = (nt(cot[r, :], wd) * slope).astype(BF16)
            gup[r, whole] = grad
            vec[pl.ds(8 + m, 1), c] += column_sum(grad.astype(F32))

        each(count // LEN, rows_step)
        gw_down[m, c, :] = tn(act[:, whole], cot[...]).astype(BF16)
        gw_up[m, :, c] = tn(n2[...], gup[:, whole]).astype(BF16)

    each(groups * per_group, chunk)
    tile = 256

    def rows_step(i):
        r = rows_of(i, tile)
        incoming = jnp.zeros((tile, width), F32)
        result = hidden[r, :] + b_down[...]
        for m in range(groups):
            c = pl.ds(m * width, width)
            incoming += nt(gup[r, c], w_up[m])
            result += nn(act[r, c], w_down[m])
        out[r, :] = result.astype(BF16)
        normal, inverse = normal_of(hidden[r, :])
        wide = cot[r, :].astype(F32)
        grad = wide + norm_input_back(normal, inverse, incoming * g2[...])
        grad_hidden[r, :] = grad
        vec[4:5, :] += column_sum(grad)
        vec[5:6, :] += column_sum(incoming * normal)
        vec[6:7, :] += column_sum(incoming)
        vec[7:8, :] += column_sum(wide)
        grad_att[r, :] = nt(grad.astype(BF16), w_out[...]).astype(BF16)

    each(count // tile, rows_step)
    gw_out[...] = tn(attended[...], grad_hidden[...].astype(BF16)).astype(BF16)


def backward_kernel(
    x, seg_col, seg_row, normed, qs, ks, vs, stats, grad_att, grad_hidden, wqkv, g1,
    grad_x, gw_qkv, vec, bias, stat_rows, dq, dk, dv,
):
    count, width = x.shape
    sequences = count // LEN
    pairs = width // 128
    vec[...] = jnp.zeros_like(vec)
    lane = lax.broadcasted_iota(jnp.int32, (LEN, 128), 1)
    first = lane < HD

    def sequence_step(s):
        mask_bias(bias, seg_col, seg_row, s)
        r = rows_of(s, LEN)
        stat_rows[...] = stats[r, :].T

        def pair_step(p):
            c = rows_of(p, 128)
            q2, k2, v2, d2 = qs[r, c], ks[r, c], vs[r, c], grad_att[r, c]
            rq, rk, rv = 0.0, 0.0, 0.0
            for half in range(2):
                mine = first if half == 0 else ~first
                qm = jnp.where(mine, q2, jnp.zeros_like(q2))
                km = jnp.where(mine, k2, jnp.zeros_like(k2))
                dm = jnp.where(mine, d2, jnp.zeros_like(d2))
                probs = jnp.exp(nt(k2, qm) + bias[...] - stat_rows[pl.ds(2 * p + half, 1), :])
                grad_probs = nt(v2, dm)
                inner = jnp.sum(probs * grad_probs, axis=0, keepdims=True)
                grad_scores = (probs * (grad_probs - inner)).astype(BF16)
                rv += nn(probs.astype(BF16), dm)
                rk += nn(grad_scores, qm)
                rq += tn(grad_scores, km)
            dq[r, c] = (rq * (HD**-0.5)).astype(BF16)
            dk[r, c] = rk.astype(BF16)
            dv[r, c] = rv.astype(BF16)

        each(pairs, pair_step)

    each(sequences, sequence_step)
    for k, grad in enumerate((dq, dk, dv)):

        def weight_step(j, k=k, grad=grad):
            c = rows_of(j, 256)
            gw_qkv[k, c, :] = tn(grad[:, c], normed[...]).astype(BF16)

        each(width // 256, weight_step)
    tile = 256

    def rows_step(i):
        r = rows_of(i, tile)
        q, k, v = dq[r, :], dk[r, :], dv[r, :]
        incoming = nn(q, wqkv[0]) + nn(k, wqkv[1]) + nn(v, wqkv[2])
        normal, inverse = normal_of(x[r, :].astype(F32))
        grad_x[r, :] = grad_hidden[r, :] + norm_input_back(normal, inverse, incoming * g1[...])
        vec[0:1, :] += column_sum(incoming * normal)
        vec[1:2, :] += column_sum(incoming)
        vec[2:3, :] += column_sum(q.astype(F32))
        vec[3:4, :] += column_sum(v.astype(F32))

    each(count // tile, rows_step)


def local_call(kernel, outs, scratch, *args):
    spec = pl.BlockSpec(memory_space=pltpu.VMEM)
    return pl.pallas_call(
        kernel,
        out_shape=outs,
        in_specs=[spec] * len(args),
        out_specs=[spec] * len(outs),
        scratch_shapes=scratch,
        compiler_params=pltpu.CompilerParams(vmem_limit_bytes=VMEM_LIMIT),
    )(*args)


def gathered(value):
    return lax.all_gather(value, "mp", axis=0)


def per_device(
    tokens, segment, ln1_gain, ln1_bias, w_qkv, b_qv, w_out, b_out, ln2_gain, ln2_bias, w_up, b_up, w_down, b_down,
    cotangent,
):
    mp = lax.axis_size("mp")
    me = lax.axis_index("mp")
    width = tokens.shape[1]
    count = tokens.shape[0] // mp
    part = width // mp
    feed = w_up.shape[1]
    x = lax.dynamic_slice_in_dim(tokens, me * count, count, 0)
    seg = lax.dynamic_slice_in_dim(segment, me * count, count, 0)
    seg_col = seg.reshape(count, 1)
    seg_row = seg.reshape(count // LEN, LEN)
    small = jnp.concatenate([ln1_gain, ln1_bias, b_qv[0], b_qv[1], b_out, ln2_gain, ln2_bias, b_down, b_up])
    small = gathered(small.reshape(1, -1)).reshape(mp, -1)
    vectors = small[:, : 8 * part].reshape(mp, 8, part).transpose(1, 0, 2).reshape(8, width).astype(F32)
    b_up_full = small[:, 8 * part :].astype(F32)
    wqkv = gathered(w_qkv.swapaxes(1, 2)).transpose(1, 0, 2, 3).reshape(3, width, width)
    full_out = gathered(w_out).reshape(width, width)
    full_up = gathered(w_up)
    full_down = gathered(w_down)
    g1, b1, bqv, bo, g2, b2, bd = (
        vectors[0:1], vectors[1:2], vectors[2:4], vectors[4:5], vectors[5:6], vectors[6:7], vectors[7:8],
    )
    wide = jax.ShapeDtypeStruct((count, width), F32)
    narrow = jax.ShapeDtypeStruct((count, width), BF16)
    weight = jax.ShapeDtypeStruct((mp, feed, width), BF16)
    mask = pltpu.VMEM((LEN, LEN), F32)
    normed, qs, ks, vs, stats, attended, hidden, n2 = local_call(
        forward_kernel,
        [narrow] * 4 + [jax.ShapeDtypeStruct((count, 128), F32), narrow, wide, narrow],
        [mask],
        x, seg_col, seg_row, wqkv, full_out, g1, b1, bqv, bo, g2, b2,
    )
    output, grad_hidden, grad_att, gw_down, gw_up, gw_out, vec_a = local_call(
        feed_kernel,
        [narrow, wide, narrow, weight, weight, jax.ShapeDtypeStruct((width, width), BF16),
         jax.ShapeDtypeStruct((16, width), F32)],
        [pltpu.VMEM((count, mp * feed), BF16), pltpu.VMEM((count, mp * feed), BF16)],
        n2, cotangent, full_up, full_down, b_up_full, bd, hidden, attended, full_out, g2,
    )
    grad_x, gw_qkv, vec_b = local_call(
        backward_kernel,
        [wide, jax.ShapeDtypeStruct((3, width, width), BF16), jax.ShapeDtypeStruct((16, width), F32)],
        [mask, pltpu.VMEM((128, LEN), F32)] + [pltpu.VMEM((count, width), BF16)] * 3,
        x, seg_col, seg_row, normed, qs, ks, vs, stats, grad_att, grad_hidden, wqkv, g1,
    )
    packed = jnp.concatenate(
        [gw_down, gw_up, gw_out.reshape(mp, part, width),
         gw_qkv.reshape(3, mp, part, width).transpose(1, 0, 2, 3).reshape(mp, 3 * part, width)],
        axis=1,
    )
    share = lax.psum_scatter(packed, "mp", scatter_dimension=0, tiled=False)
    share = lax.psum(share, "dp").astype(F32)
    vec = lax.psum(vec_a + vec_b, ("dp", "mp"))
    eight = lax.dynamic_slice_in_dim(vec[:8], me * part, part, 1)
    grad_b_up = lax.dynamic_slice_in_dim(vec[8 : 8 + mp], me, 1, 0).reshape(-1)
    two = 2 * feed
    g_qkv = share[two + part :].reshape(3, part, width).swapaxes(1, 2)
    return (
        output, grad_x, eight[0], eight[1], g_qkv, eight[2:4], share[two : two + part], eight[4], eight[5], eight[6],
        share[feed:two], grad_b_up, share[:feed], eight[7],
    )


def solution(mesh):
    rows = P(("dp", "mp"), None)
    return jax.shard_map(
        per_device,
        mesh=mesh,
        in_specs=(
            P("dp", None), P("dp"), P("mp"), P("mp"), P(None, None, "mp"), P(None, "mp"), P("mp", None), P("mp"),
            P("mp"), P("mp"), P(None, "mp"), P("mp"), P("mp", None), P("mp"), rows,
        ),
        out_specs=(
            rows, rows, P("mp"), P("mp"), P(None, None, "mp"), P(None, "mp"), P("mp", None), P("mp"), P("mp"), P("mp"),
            P(None, "mp"), P("mp"), P("mp", None), P("mp"),
        ),
        check_vma=False,
    )
```

```python
import functools

import jax
import jax.numpy as jnp
from jax import lax
from jax.experimental import pallas as pl
from jax.experimental.pallas import tpu as pltpu
from jax.sharding import PartitionSpec as P

HD = 64
LEN = 512
PIECE = 256
TILE = 256
F32 = jnp.float32
BF16 = jnp.bfloat16
MESH = pl.DeviceIdType.MESH
VMEM_LIMIT = 67043328
HBM = pl.BlockSpec(memory_space=pl.ANY)
VMEM = pl.BlockSpec(memory_space=pltpu.VMEM)


def nn(left, right):
    return jnp.dot(left, right, preferred_element_type=F32)


def nt(left, right):
    return lax.dot_general(left, right, (((1,), (1,)), ((), ())), preferred_element_type=F32)


def tn(left, right):
    return lax.dot_general(left, right, (((0,), (0,)), ((), ())), preferred_element_type=F32)


def ds(start, size, step=None):
    if isinstance(start, int):
        return pl.ds(start, size)
    return pl.ds(pl.multiple_of(start, step or size), size)


def rows_of(index, count):
    return ds(index * count, count)


def normal_of(values):
    centered = values - jnp.mean(values, axis=-1, keepdims=True)
    spread = jnp.mean(centered * centered, axis=-1, keepdims=True)
    inverse = lax.rsqrt(spread + 1e-06)
    return centered * inverse, inverse


def norm_input_back(normal, inverse, scaled):
    inner = jnp.mean(scaled * normal, axis=-1, keepdims=True)
    return inverse * (scaled - jnp.mean(scaled, axis=-1, keepdims=True) - normal * inner)


def column_sum(values):
    return jnp.sum(values, axis=0, keepdims=True)


def each(count, body):
    lax.fori_loop(0, count, lambda i, carry: (body(i), carry)[1], 0)


def at_steps(index, table):
    for step, actions in table.items():

        @pl.when(index == step)
        def _(actions=actions):
            for action in actions:
                action()


def add_into(target, *sources):
    rows = target.shape[0]
    tile = 64 if rows % 64 == 0 else 48

    def step(i):
        r = rows_of(i, tile)
        value = target[r, :].astype(F32)
        for source in sources:
            value += source[r, :].astype(F32)
        target[r, :] = value.astype(BF16)

    each(rows // tile, step)


def layer_kernel(
    dp, small_own, qkv_own, out_own, up_own, down_own, tokens, cot_hbm, segment,
    output, grad_x, feed_out, proj_out, qkv_out, vec_out, act_hbm, hidden_hbm,
    small, wqkv, w_out, w_up, w_down, x, cot, normed, qs, ks, vs, attended, n2, stats, hid, gup, act, bias,
    stat_rows, vec, vec_recv, fp, fcr, fyr, fxr, fzr, fer, op, ocr, oyr, oxr, ozr, oer, qp, qcr, qyr, qxr, qzr, qer,
    ag_local, ag_send, ag_recv, small_send, small_recv, local, act_sem, tile_a, tile_b, unit_send, unit_recv,
    vec_send, vec_got, credit, ready,
):
    me, d = lax.axis_index("mp"), lax.axis_index("dp")
    y, c = me // 2, me % 2
    count, width = x.shape
    part = width // 4
    half = width // 2
    sequences = count // LEN
    xb, zb = d % 2, (d // 2) % 2

    def across(bit):
        return d + bit - 2 * bit * ((d // bit) % 2)

    partner, above = (d, me + 1 - 2 * c), (d, me + 2 - 4 * y)
    diagonal = (d, 3 - me)
    side, level = (across(1), me), (across(2), me)
    far = [(across(bit), me) for bit in [1 << i for i in range(2, 12)] if bit < dp]
    peers = [partner, above, diagonal, side, level] + far
    barrier = pltpu.get_barrier_semaphore()
    for peer in peers:
        pl.semaphore_signal(barrier, inc=1, device_id=peer, device_id_type=MESH)
    pl.semaphore_wait(barrier, len(peers))

    def remote(source, target, send, recv, device):
        return pltpu.make_async_remote_copy(
            src_ref=source, dst_ref=target, send_sem=send, recv_sem=recv, device_id=device, device_id_type=MESH
        )

    def got(region, recv):
        remote(region, region, recv, recv, partner).wait_recv()

    def sent(region, send):
        remote(region, region, send, send, partner).wait_send()

    owns = (qkv_own, out_own, up_own, down_own)
    quarter = zb * 2 + xb
    q_side, q_level, q_diag = zb * 2 + 1 - xb, (1 - zb) * 2 + xb, 3 - quarter

    def own(t, q=None):
        if q is None:
            return owns[t]
        if t == 0:
            return qkv_own.at[:, rows_of(q, part // 4), :]
        rows = owns[t].shape[0] // 4
        return owns[t].at[rows_of(q, rows), :]

    def region(t, m, q=None):
        if t < 2:
            rows = part if q is None else part // 4
            start = m * part + (0 if q is None else q * rows)
            where = ds(start, rows, part // 4)
            return wqkv.at[:, where, :] if t == 0 else w_out.at[where, :]
        full = (w_up, w_down)[t - 2]
        if q is None:
            return full.at[m]
        rows = full.shape[1] // 4
        return full.at[m, rows_of(q, rows), :]

    m_core, m_y, m_diag = me + 1 - 2 * c, me + 2 - 4 * y, 3 - me
    through_side = (True, False, True, False)

    for i, peer in enumerate((diagonal, above, partner)):
        remote(small_own, small.at[me], small_send.at[i], small_recv.at[i], peer).start()
    pltpu.make_async_copy(small_own, small.at[me], local.at[0]).start()
    pltpu.make_async_copy(tokens.at[ds(me * count, count), :], x, local.at[1]).start()
    for t in range(4):
        remote(own(t, quarter), region(t, me, quarter), ag_send.at[t, 1], ag_recv.at[t, 1], above).start()
        pltpu.make_async_copy(own(t), region(t, me), ag_local.at[t]).start()
        remote(own(t), region(t, me), ag_send.at[t, 0], ag_recv.at[t, 0], partner).start()
    pltpu.make_async_copy(cot_hbm, cot, local.at[2]).start()

    def pass_on(t, q, k, device):
        where = region(t, m_y, q)
        remote(where, where, ag_send.at[t, k], ag_recv.at[t, k], device).start()

    def ag_y(t):
        got(region(t, m_y, quarter), ag_recv.at[t, 1])
        pass_on(t, quarter, 2, side)
        pass_on(t, quarter, 3, level)
        pass_on(t, quarter, 4, partner)

    def ag_side(t):
        got(region(t, m_y, q_side), ag_recv.at[t, 2])
        if not through_side[t]:
            pass_on(t, q_side, 7, level)
        pass_on(t, q_side, 5, partner)

    def ag_level(t):
        got(region(t, m_y, q_level), ag_recv.at[t, 3])
        if through_side[t]:
            pass_on(t, q_level, 7, side)
        pass_on(t, q_level, 6, partner)

    def ag_diag(t):
        got(region(t, m_y, q_diag), ag_recv.at[t, 7])
        pass_on(t, q_diag, 8, partner)

    def ag_near(t):
        pltpu.make_async_copy(own(t), region(t, me), ag_local.at[t]).wait()
        got(region(t, m_core), ag_recv.at[t, 0])

    def ag_rest(t):
        for k, q in ((4, quarter), (5, q_side), (6, q_level), (8, q_diag)):
            got(region(t, m_diag, q), ag_recv.at[t, k])

    def ag_sends(t):
        sent(own(t), ag_send.at[t, 0])
        sent(own(t, quarter), ag_send.at[t, 1])
        for k in range(2, 9):
            sent(own(t, quarter), ag_send.at[t, k])

    vec[...] = jnp.zeros_like(vec)
    for s in range(sequences):
        mine = segment[pl.ds(me * sequences + s, 1), :].astype(F32)
        column = jnp.broadcast_to(mine, (128, LEN)).T[:, :1]
        row_ids = lax.broadcasted_iota(jnp.int32, (LEN, LEN), 0)
        col_ids = lax.broadcasted_iota(jnp.int32, (LEN, LEN), 1)
        allowed = ((column == mine) & (mine != 0.0)) | (row_ids == col_ids)
        bias[s] = jnp.where(allowed, 0.0, -1e30)
        stats[rows_of(s, LEN), :] = jnp.zeros((LEN, 128), F32)
    pltpu.make_async_copy(small_own, small.at[me], local.at[0]).wait()
    for i, m in enumerate((m_diag, m_y, m_core)):
        got(small.at[m], small_recv.at[i])
    vectors = sum(small[m].astype(F32) for m in range(4))
    pltpu.make_async_copy(tokens.at[ds(0, count), :], x, local.at[1]).wait()
    g1, b1, b_query, b_value, b_out, g2, b2, b_down = (vectors[i : i + 1] for i in range(8))

    def ln_one(i):
        r = rows_of(i, TILE)
        normal, _ = normal_of(x[r, :].astype(F32))
        normed[r, :] = (normal * g1 + b1).astype(BF16)

    each(count // TILE, ln_one)
    lane = lax.broadcasted_iota(jnp.int32, (LEN, 128), 1)
    first = lane < HD
    pairs = half // 128
    small_sum = sum(small[m].astype(F32) for m in range(4))
    vec_recv[0] = small_sum

    def project(side_of):
        columns = ds(side_of * half, half, 128)

        def step(i):
            r = rows_of(i, LEN)
            value = normed[r, :]
            biases = vec_recv.at[0]
            query = nt(value, wqkv[0, columns, :]) + biases[2:3, columns]
            qs[r, columns] = (query.astype(BF16).astype(F32) * (HD**-0.5)).astype(BF16)
            ks[r, columns] = nt(value, wqkv[1, columns, :]).astype(BF16)
            vs[r, columns] = (nt(value, wqkv[2, columns, :]) + biases[3:4, columns]).astype(BF16)

        each(count // LEN, step)

    def attend(side_of, table):
        def step(i):
            s, p = i // pairs, side_of * pairs + i % pairs
            r, cols = rows_of(s, LEN), rows_of(p, 128)
            q2, k2, v2 = qs[r, cols], ks[r, cols], vs[r, cols]
            results = []
            kept = stats[r, :]
            for part_of in range(2):
                mine = first if part_of == 0 else ~first
                scores = nt(jnp.where(mine, q2, jnp.zeros_like(q2)), k2) + bias[s]
                top = jnp.max(scores, axis=-1, keepdims=True)
                expo = jnp.exp(scores - top)
                total = jnp.sum(expo, axis=-1, keepdims=True)
                results.append(nn(expo.astype(BF16), v2) * (1.0 / total))
                kept = jnp.where(lane == 2 * p + part_of, top + jnp.log(total), kept)
            stats[r, :] = kept
            attended[r, cols] = jnp.where(first, results[0], results[1]).astype(BF16)
            at_steps(i, table)

        each(sequences * pairs, step)

    def run(function, *args):
        return functools.partial(function, *args)

    ag_near(0)
    project(y)
    attend(
        y,
        {
            0: [run(ag_y, 0), run(ag_y, 1)],
            3: [run(ag_level, 0), run(ag_side, 0)],
            4: [run(ag_side, 1), run(ag_level, 1)],
            5: [run(ag_y, 2)],
        },
    )
    ag_diag(0)
    ag_rest(0)
    project(1 - y)
    attend(
        1 - y,
        {
            0: [run(ag_diag, 1), run(ag_y, 3)],
            2: [run(ag_side, 2), run(ag_level, 2)],
            5: [run(ag_side, 3), run(ag_level, 3), run(ag_diag, 2)],
        },
    )
    ag_near(1)
    ag_rest(1)

    def out_step(i):
        r = rows_of(i, TILE)
        value = x[r, :].astype(F32) + nn(attended[r, :], w_out[...]) + vec_recv[0, 4:5, :]
        hid[r, :] = value
        pltpu.make_async_copy(hid.at[r, :], hidden_hbm.at[r, :], tile_a.at[i]).start()
        normal, _ = normal_of(value)
        n2[r, :] = (normal * vec_recv[0, 5:6, :] + vec_recv[0, 6:7, :]).astype(BF16)

    each(count // TILE, out_step)
    ag_near(2)
    ag_rest(2)
    ag_diag(3)
    ag_near(3)
    ag_rest(3)
    pltpu.make_async_copy(cot_hbm, cot, local.at[2]).wait()

    up_bias = vec_recv.at[0]
    feed_slots = 2

    def unit(u, kept, cr, yr, xr, zr, er):
        rows = kept.shape[0]
        return (u, rows, kept, cr, yr, xr, zr, er)

    def own_half(rows):
        return ds(xb * (rows // 2), rows // 2, rows // 4)

    def other_half(rows):
        return ds((1 - xb) * (rows // 2), rows // 2, rows // 4)

    def own_quarter(rows):
        return ds(xb * (rows // 2) + zb * (rows // 4), rows // 4)

    def other_quarter(rows):
        return ds(xb * (rows // 2) + (1 - zb) * (rows // 4), rows // 4)

    def send_unit(u, k, source, target, device):
        remote(source, target, unit_send.at[u, k], unit_recv.at[u, k], device).start()

    def take_sum(unit_of):
        u, rows, kept, cr, yr, xr, zr, er = unit_of
        got(cr, unit_recv.at[u, 2])
        got(yr, unit_recv.at[u, 1])
        add_into(kept, cr, yr)
        send_unit(u, 3, kept.at[other_half(rows), :], xr, side)

    def far_room(unit_of, i):
        u, rows, kept, cr, yr, xr, zr, er = unit_of
        return er if i == 0 else cr.at[(i - 1) * (rows // 4) : i * (rows // 4), :]

    def send_far(unit_of, i):
        u, rows, kept, cr, yr, xr, zr, er = unit_of
        if i > 0:
            pl.semaphore_wait(ready.at[u, 2 + i], 1)
        send_unit(u, 7 + i, kept.at[own_quarter(rows), :], far_room(unit_of, i), far[i])

    def take_side(unit_of):
        u, rows, kept, cr, yr, xr, zr, er = unit_of
        for i in range(1, len(far)):
            pl.semaphore_signal(ready.at[u, 2 + i], inc=1, device_id=far[i], device_id_type=MESH)
        got(xr, unit_recv.at[u, 3])
        sent(xr, unit_send.at[u, 3])
        pl.semaphore_signal(ready.at[u, 0], inc=1, device_id=side, device_id_type=MESH)
        add_into(kept.at[own_half(rows), :], xr)
        send_unit(u, 4, kept.at[other_quarter(rows), :], zr, level)

    def give_level(unit_of):
        u, rows, kept, cr, yr, xr, zr, er = unit_of
        mine = kept.at[own_quarter(rows), :]
        pl.semaphore_wait(ready.at[u, 1], 1)
        send_unit(u, 5, mine, mine, level)

    def take_level(unit_of):
        u, rows, kept, cr, yr, xr, zr, er = unit_of
        got(zr, unit_recv.at[u, 4])
        sent(zr, unit_send.at[u, 4])
        pl.semaphore_signal(ready.at[u, 1], inc=1, device_id=level, device_id_type=MESH)
        mine = kept.at[own_quarter(rows), :]
        add_into(mine, zr)
        if far:
            send_far(unit_of, 0)
        else:
            give_level(unit_of)

    def take_far(unit_of):
        u, rows, kept, cr, yr, xr, zr, er = unit_of
        mine = kept.at[own_quarter(rows), :]
        for i, _ in enumerate(far):
            landed = far_room(unit_of, i)
            got(landed, unit_recv.at[u, 7 + i])
            sent(mine, unit_send.at[u, 7 + i])
            add_into(mine, landed)
            if i + 1 < len(far):
                send_far(unit_of, i + 1)
        if far:
            give_level(unit_of)

    def give_side(unit_of):
        u, rows, kept, cr, yr, xr, zr, er = unit_of
        got(kept.at[other_quarter(rows), :], unit_recv.at[u, 5])
        mine = kept.at[own_half(rows), :]
        pl.semaphore_wait(ready.at[u, 0], 1)
        send_unit(u, 6, mine, mine, side)

    def finish(unit_of, target, sem):
        u, rows, kept, cr, yr, xr, zr, er = unit_of
        got(kept.at[other_half(rows), :], unit_recv.at[u, 6])
        pltpu.make_async_copy(kept, target, sem).start()

    def unit_sends(unit_of):
        u, rows, kept, cr, yr, xr, zr, er = unit_of
        sent(kept, unit_send.at[u, 1])
        sent(kept.at[own_half(rows), :], unit_send.at[u, 6])
        sent(kept.at[own_quarter(rows), :], unit_send.at[u, 5])

    feeds = [
        unit(s, fp.at[feed_slots + 3 + s], fcr.at[s], fyr.at[s], fxr.at[s], fzr.at[s], fer.at[s]) for s in range(3)
    ]
    proj = unit(3, op.at[3], ocr, oyr, oxr, ozr, oer)
    attn = unit(4, qp.at[2], qcr, qyr, qxr, qzr, qer)

    def feed_first(sub, slot):
        send_unit(sub, 0, fp.at[slot], fcr.at[sub], partner)

    def feed_second(sub, slot):
        got(fcr.at[sub], unit_recv.at[sub, 0])
        add_into(fp.at[slot], fcr.at[sub])
        pl.semaphore_signal(credit, inc=1, device_id=partner, device_id_type=MESH)
        send_unit(sub, 1, fp.at[slot], fyr.at[sub], above)

    def feed_third(sub, slot):
        pl.semaphore_wait(credit, 1)
        send_unit(sub, 2, fp.at[slot], fcr.at[sub], partner)

    steps = 12

    def feed_step(i):
        late, odd, sub = i // 6, i % 2, (i % 6) // 2
        m = 2 * jnp.where(late == 0, 1 - y, y) + jnp.where(odd == 0, 1 - c, c)
        slot = jnp.where(odd == 0, (i // 2) % feed_slots, feed_slots + 3 * late + sub)
        cols = rows_of(sub, PIECE)
        whole = rows_of(m * 3 + sub, PIECE)
        wu, wd = w_up[m, :, cols], w_down[m, cols, :]
        piece_bias = up_bias[pl.ds(8 + m, 1), cols]
        buffer = i % 2

        @pl.when(i >= 2)
        def _():
            pltpu.make_async_copy(act.at[buffer], act_hbm.at[:, whole], act_sem.at[buffer]).wait()

        @pl.when((i >= 4) & (odd == 0))
        def _():
            before = i - 4
            sent(fp.at[slot], unit_send.at[(before % 6) // 2, 2 * (before // 6)])

        def rows_step(j):
            r = rows_of(j, LEN)
            up = nn(n2[r, :], wu) + piece_bias
            half_cdf = 0.5 * (1.0 + lax.erf(up * (0.5**0.5)))
            slope = half_cdf + up * (jnp.exp(-0.5 * up * up) * 0.3989422804014327)
            act[buffer, r, :] = (up * half_cdf).astype(BF16)
            grad = (nt(cot[r, :], wd) * slope).astype(BF16)
            gup[r, whole] = grad
            vec[pl.ds(8 + m, 1), cols] += column_sum(grad.astype(F32))

        each(count // LEN, rows_step)
        pltpu.make_async_copy(act.at[buffer], act_hbm.at[:, whole], act_sem.at[buffer]).start()
        fp[slot, :PIECE, :] = tn(act[buffer], cot[...]).astype(BF16)
        fp[slot, PIECE:, :] = tn(gup[:, whole], n2[...]).astype(BF16)

        @pl.when((late == 0) & (odd == 0))
        def _():
            feed_first(sub, slot)

        @pl.when((late == 0) & (odd == 1))
        def _():
            feed_second(sub, slot)

        @pl.when((late == 1) & (odd == 0))
        def _():
            feed_third(sub, slot)

        at_steps(i, {7: [run(take_sum, feeds[0])], 10: [run(take_side, feeds[0])], 11: [run(take_sum, feeds[1])]})

    vec[8:16, :] = jnp.zeros_like(vec[8:16, :])
    each(steps, feed_step)
    for buffer in range(2):
        pltpu.make_async_copy(act.at[buffer], act_hbm.at[:, ds(0, PIECE)], act_sem.at[buffer]).wait()
    for i in range(count // TILE):
        r = rows_of(i, TILE)
        pltpu.make_async_copy(hid.at[r, :], hidden_hbm.at[r, :], tile_a.at[i]).wait()

    def hidden_step(i):
        r = rows_of(i, TILE)
        incoming = nt(gup[r, :width], w_up[0])
        for m in range(1, 4):
            incoming += nt(gup[r, m * width : (m + 1) * width], w_up[m])
        normal, inverse = normal_of(hid[r, :])
        wide = cot[r, :].astype(F32)
        grad = wide + norm_input_back(normal, inverse, incoming * vec_recv[0, 5:6, :])
        hid[r, :] = grad
        vec[4:5, :] += column_sum(grad)
        vec[5:6, :] += column_sum(incoming * normal)
        vec[6:7, :] += column_sum(incoming)
        vec[7:8, :] += column_sum(wide)
        narrow = grad.astype(BF16)
        gup[r, 3 * width :] = narrow
        n2[r, :] = nt(narrow, w_out[...]).astype(BF16)
        at_steps(i, {0: [run(take_level, feeds[0])], 3: [run(take_far, feeds[0]), run(take_side, feeds[1])]})

    each(count // TILE, hidden_step)
    product = tn(attended[...], gup[:, 3 * width :])
    for m in range(4):
        slot = 2 * jnp.where(y == m // 2, 1, 0) + jnp.where(c == m % 2, 1, 0)
        op[slot] = product[m * part : (m + 1) * part, :].astype(BF16)
    send_unit(3, 0, op.at[0], ocr, partner)

    def proj_second():
        got(ocr, unit_recv.at[3, 0])
        add_into(op.at[1], ocr)
        pl.semaphore_signal(credit, inc=1, device_id=partner, device_id_type=MESH)
        send_unit(3, 1, op.at[1], oyr, above)

    def proj_third():
        pl.semaphore_wait(credit, 1)
        send_unit(3, 2, op.at[2], ocr, partner)

    def attend_back(side_of, table):
        def step(i):
            s, p = i // pairs, side_of * pairs + i % pairs
            r, cols = rows_of(s, LEN), rows_of(p, 128)

            @pl.when(i % pairs == 0)
            def _():
                stat_rows[...] = stats[r, :].T

            q2, k2, v2, d2 = qs[r, cols], ks[r, cols], vs[r, cols], n2[r, cols]
            rq, rk, rv = 0.0, 0.0, 0.0
            for part_of in range(2):
                mine = first if part_of == 0 else ~first
                qm = jnp.where(mine, q2, jnp.zeros_like(q2))
                km = jnp.where(mine, k2, jnp.zeros_like(k2))
                dm = jnp.where(mine, d2, jnp.zeros_like(d2))
                probs = jnp.exp(nt(k2, qm) + bias[s] - stat_rows[pl.ds(2 * p + part_of, 1), :])
                grad_probs = nt(v2, dm)
                inner = jnp.sum(probs * grad_probs, axis=0, keepdims=True)
                grad_scores = (probs * (grad_probs - inner)).astype(BF16)
                rv += nn(probs.astype(BF16), dm)
                rk += nn(grad_scores, qm)
                rq += tn(grad_scores, km)
            gup[r, cols] = (rq * (HD**-0.5)).astype(BF16)
            gup[r, ds(width + p * 128, 128)] = rk.astype(BF16)
            gup[r, ds(2 * width + p * 128, 128)] = rv.astype(BF16)
            at_steps(i, table)

        each(sequences * pairs, step)

    def weight_of_half(side_of, kept_slot):
        for k in range(3):
            grads = gup[:, ds(k * width + side_of * half, half, 128)]
            product = tn(grads, normed[...]).astype(BF16)
            for core in range(2):
                slot = jnp.where(c == core, kept_slot, 0)
                qp[slot, k * part : (k + 1) * part, :] = product[core * part : (core + 1) * part, :]

    attend_back(
        1 - y,
        {
            0: [proj_second, run(give_side, feeds[0]), run(take_level, feeds[1])],
            1: [proj_third, run(take_sum, feeds[2])],
            3: [run(finish, feeds[0], feed_out.at[0], local.at[3]), run(take_far, feeds[1]), run(take_sum, proj)],
            4: [run(take_side, feeds[2])],
            5: [run(give_side, feeds[1]), run(take_side, proj)],
        },
    )
    weight_of_half(1 - y, 1)
    send_unit(4, 0, qp.at[0], qcr, partner)

    def attn_second():
        got(qcr, unit_recv.at[4, 0])
        add_into(qp.at[1], qcr)
        pl.semaphore_signal(credit, inc=1, device_id=partner, device_id_type=MESH)
        send_unit(4, 1, qp.at[1], qyr, above)

    attend_back(
        y,
        {
            0: [attn_second, run(take_level, feeds[2])],
            1: [run(take_level, proj)],
            2: [run(take_far, feeds[2])],
            3: [run(finish, feeds[1], feed_out.at[1], local.at[4]), run(take_far, proj), run(give_side, feeds[2])],
            5: [run(give_side, proj), run(finish, feeds[2], feed_out.at[2], local.at[5])],
        },
    )
    sent(qp.at[0], unit_send.at[4, 0])
    weight_of_half(y, 2)
    pl.semaphore_wait(credit, 1)
    send_unit(4, 2, qp.at[0], qcr, partner)

    def input_step(i):
        r = rows_of(i, TILE)
        q, k, v = gup[r, :width], gup[r, width : 2 * width], gup[r, 2 * width : 3 * width]
        incoming = nn(q, wqkv[0]) + nn(k, wqkv[1]) + nn(v, wqkv[2])
        normal, inverse = normal_of(x[r, :].astype(F32))
        hid[r, :] += norm_input_back(normal, inverse, incoming * vec_recv[0, 0:1, :])
        vec[0:1, :] += column_sum(incoming * normal)
        vec[1:2, :] += column_sum(incoming)
        vec[2:3, :] += column_sum(q.astype(F32))
        vec[3:4, :] += column_sum(v.astype(F32))
        pltpu.make_async_copy(hid.at[r, :], grad_x.at[r, :], tile_a.at[i]).start()
        pltpu.make_async_copy(act_hbm.at[r, :], gup.at[r, :], tile_b.at[i]).start()
        at_steps(i, {0: [run(take_sum, attn)], 3: [run(finish, proj, proj_out, local.at[6])]})

    each(count // TILE, input_step)

    def reload(i):
        r = rows_of(i, TILE)
        pltpu.make_async_copy(hid.at[r, :], grad_x.at[r, :], tile_a.at[i]).wait()
        pltpu.make_async_copy(hidden_hbm.at[r, :], hid.at[r, :], tile_a.at[i]).start()

    each(count // TILE, reload)
    b_down = vec_recv[0, 7:8, :]

    rounds = [partner, above, side, level] + far

    def vec_start(i):
        remote(vec, vec_recv.at[1 + i], vec_send.at[i], vec_got.at[i], rounds[i]).start()

    def vec_step(i):
        got(vec_recv.at[1 + i], vec_got.at[i])
        sent(vec, vec_send.at[i])
        vec[...] += vec_recv[1 + i]
        if i + 1 < len(rounds):
            vec_start(i + 1)

    vec_start(0)

    def output_step(i):
        r = rows_of(i, TILE)
        pltpu.make_async_copy(hidden_hbm.at[r, :], hid.at[r, :], tile_a.at[i]).wait()
        pltpu.make_async_copy(act_hbm.at[r, :], gup.at[r, :], tile_b.at[i]).wait()
        result = hid[r, :] + b_down
        for m in range(4):
            result += nn(gup[r, m * width : (m + 1) * width], w_down[m])
        x[r, :] = result.astype(BF16)
        pltpu.make_async_copy(x.at[r, :], output.at[r, :], tile_a.at[i]).start()
        at_steps(
            i,
            {
                0: [run(vec_step, 0)],
                1: [run(vec_step, 1)],
                2: [run(take_side, attn), run(vec_step, 2)],
                3: [run(vec_step, 3)],
            },
        )

    each(count // TILE, output_step)
    take_level(attn)
    for i in range(4, len(rounds)):
        vec_step(i)
    pltpu.make_async_copy(vec, vec_out, local.at[7]).start()
    take_far(attn)
    give_side(attn)
    finish(attn, qkv_out, local.at[8])

    for i in range(3):
        sent(small_own, small_send.at[i])
    for t in range(4):
        ag_sends(t)
    for k, slot in ((1, 0), (2, 1)):
        sent(fp.at[slot], unit_send.at[k, 2])
    for k in (0, 2):
        sent(op.at[0], unit_send.at[3, k])
    sent(qp.at[0], unit_send.at[4, 2])
    for unit_of in feeds + [proj, attn]:
        unit_sends(unit_of)
    for i in range(count // TILE):
        r = rows_of(i, TILE)
        pltpu.make_async_copy(x.at[r, :], output.at[r, :], tile_a.at[i]).wait()
    for s in range(3):
        pltpu.make_async_copy(feeds[s][2], feed_out.at[s], local.at[3 + s]).wait()
    pltpu.make_async_copy(op.at[3], proj_out, local.at[6]).wait()
    pltpu.make_async_copy(vec, vec_out, local.at[7]).wait()
    pltpu.make_async_copy(qp.at[2], qkv_out, local.at[8]).wait()


def per_device(
    dp, tokens, segment, ln1_gain, ln1_bias, w_qkv, b_qv, w_out, b_out, ln2_gain, ln2_bias, w_up, b_up, w_down, b_down,
    cotangent,
):
    mp = 4
    me = lax.axis_index("mp")
    count, width = cotangent.shape
    part = width // mp
    feed = w_up.shape[1]
    bits = dp.bit_length() - 1
    far = bits - 2
    pieces = jnp.stack([ln1_gain, ln1_bias, b_qv[0], b_qv[1], b_out, ln2_gain, ln2_bias, b_down])
    small_own = lax.dynamic_update_slice(jnp.zeros((16, width), BF16), pieces, (0, me * part))
    small_own = lax.dynamic_update_slice(small_own, b_up.reshape(1, feed), (8 + me, 0))
    qkv_own = w_qkv.swapaxes(1, 2)

    def shape(*dims, kind=BF16):
        return jax.ShapeDtypeStruct(dims, kind)

    def room(*dims, kind=BF16):
        return pltpu.VMEM(dims, kind)

    unit_rows = 2 * PIECE
    dma = pltpu.SemaphoreType.DMA
    outs = [
        shape(count, width), shape(count, width, kind=F32), shape(3, unit_rows, width), shape(part, width),
        shape(3 * part, width), shape(16, width, kind=F32), shape(count, mp * feed), shape(count, width, kind=F32),
    ]

    def unit_rooms(rows, slots, lead):
        return [
            room(slots, rows, width), room(*lead, rows, width), room(*lead, rows, width),
            room(*lead, rows // 2, width), room(*lead, rows // 4, width), room(*lead, rows // 4, width),
        ]

    scratch = [
        room(mp, 16, width), room(3, width, width), room(width, width), room(mp, width, feed), room(mp, feed, width),
        *[room(count, width) for _ in range(8)],
        room(count, 128, kind=F32), room(count, width, kind=F32), room(count, mp * feed), room(2, count, PIECE),
        room(count // LEN, LEN, LEN, kind=F32), room(128, LEN, kind=F32), room(16, width, kind=F32),
        room(1 + 2 + bits, 16, width, kind=F32),
        *unit_rooms(unit_rows, 8, (3,)), *unit_rooms(part, 4, ()), *unit_rooms(3 * part, 3, ()),
        dma((4,)), dma((4, 9)), dma((4, 9)), dma((3,)), dma((3,)), dma((9,)), dma((2,)), dma((4,)), dma((4,)),
        dma((5, 7 + max(far, 1))), dma((5, 7 + max(far, 1))), dma((2 + bits,)), dma((2 + bits,)),
        pltpu.SemaphoreType.REGULAR, pltpu.SemaphoreType.REGULAR((5, 2 + max(far, 1))),
    ]
    args = (
        small_own, qkv_own, w_out, w_up, w_down, tokens, cotangent, segment.reshape(-1, LEN),
    )
    results = pl.pallas_call(
        functools.partial(layer_kernel, dp),
        out_shape=outs,
        in_specs=[HBM] * 7 + [VMEM],
        out_specs=[HBM] * len(outs),
        scratch_shapes=scratch,
        compiler_params=pltpu.CompilerParams(
            vmem_limit_bytes=VMEM_LIMIT, collective_id=0, has_side_effects=True
        ),
    )(*args)
    output, grad_x, feeds, proj, attn, vec = results[:6]
    eight = lax.dynamic_slice_in_dim(vec[:8], me * part, part, 1)
    grad_b_up = lax.dynamic_slice_in_dim(vec, 8 + me, 1, 0).reshape(-1)
    g_down = feeds[:, :PIECE].reshape(feed, width).astype(F32)
    g_up = feeds[:, PIECE:].reshape(feed, width).T.astype(F32)
    g_qkv = attn.reshape(3, part, width).swapaxes(1, 2).astype(F32)
    return (
        output, grad_x, eight[0], eight[1], g_qkv, eight[2:4], proj.astype(F32), eight[4], eight[5], eight[6],
        g_up, grad_b_up, g_down, eight[7],
    )


def solution(mesh):
    rows = P(("dp", "mp"), None)
    return jax.shard_map(
        functools.partial(per_device, mesh.shape["dp"]),
        mesh=mesh,
        in_specs=(
            P("dp", None), P("dp"), P("mp"), P("mp"), P(None, None, "mp"), P(None, "mp"), P("mp", None), P("mp"),
            P("mp"), P("mp"), P(None, "mp"), P("mp"), P("mp", None), P("mp"), rows,
        ),
        out_specs=(
            rows, rows, P("mp"), P("mp"), P(None, None, "mp"), P(None, "mp"), P("mp", None), P("mp"), P("mp"), P("mp"),
            P(None, "mp"), P("mp"), P("mp", None), P("mp"),
        ),
        check_vma=False,
    )
```

```python
import functools

import jax
import jax.numpy as jnp
from jax import lax
from jax.experimental import pallas as pl
from jax.experimental.pallas import tpu as pltpu
from jax.sharding import PartitionSpec as P

HD = 64
LEN = 512
PIECE = 256
TILE = 256
F32 = jnp.float32
BF16 = jnp.bfloat16
MESH = pl.DeviceIdType.MESH
VMEM_LIMIT = 67043328
HBM = pl.BlockSpec(memory_space=pl.ANY)
VMEM = pl.BlockSpec(memory_space=pltpu.VMEM)


def nn(left, right):
    return jnp.dot(left, right, preferred_element_type=F32)


def nt(left, right):
    return lax.dot_general(left, right, (((1,), (1,)), ((), ())), preferred_element_type=F32)


def tn(left, right):
    return lax.dot_general(left, right, (((0,), (0,)), ((), ())), preferred_element_type=F32)


def ds(start, size, step=None):
    if isinstance(start, int):
        return pl.ds(start, size)
    return pl.ds(pl.multiple_of(start, step or size), size)


def rows_of(index, count):
    return ds(index * count, count)


def normal_of(values):
    centered = values - jnp.mean(values, axis=-1, keepdims=True)
    spread = jnp.mean(centered * centered, axis=-1, keepdims=True)
    inverse = lax.rsqrt(spread + 1e-06)
    return centered * inverse, inverse


def norm_input_back(normal, inverse, scaled):
    inner = jnp.mean(scaled * normal, axis=-1, keepdims=True)
    return inverse * (scaled - jnp.mean(scaled, axis=-1, keepdims=True) - normal * inner)


def column_sum(values):
    return jnp.sum(values, axis=0, keepdims=True)


def each(count, body):
    lax.fori_loop(0, count, lambda i, carry: (body(i), carry)[1], 0)


def at_steps(index, table):
    for step, actions in table.items():

        @pl.when(index == step)
        def _(actions=actions):
            for action in actions:
                action()


def add_into(target, *sources):
    rows = target.shape[0]
    tile = 64 if rows % 64 == 0 else 48

    def step(i):
        r = rows_of(i, tile)
        value = target[r, :].astype(F32)
        for source in sources:
            value += source[r, :].astype(F32)
        target[r, :] = value.astype(BF16)

    each(rows // tile, step)


def layer_kernel(
    dp, small_own, qkv_own, out_own, up_own, down_own, tokens, cot_hbm, segment,
    output, grad_x, feed_out, proj_out, qkv_out, vec_out, act_hbm, hidden_hbm,
    small, wqkv, w_out, w_up, w_down, x, cot, normed, qs, ks, vs, attended, n2, hid, gup, act, bias,
    stat_rows, vec, vec_recv, fp, fcr, fyr, fxr, op, ocr, oyr, oxr,
    ag_local, ag_send, ag_recv, small_send, small_recv, local, act_sem, tile_a, tile_b, unit_send, unit_recv,
    vec_send, vec_got, credit, ready,
):
    me, d = lax.axis_index("mp"), lax.axis_index("dp")
    y, c = me // 2, me % 2
    count, width = x.shape
    part = width // 4
    half = width // 2
    sequences = count // LEN
    xb, zb = d % 2, (d // 2) % 2

    def across(bit):
        return d + bit - 2 * bit * ((d // bit) % 2)

    partner, above = (d, me + 1 - 2 * c), (d, me + 2 - 4 * y)
    diagonal = (d, 3 - me)
    side, level = (across(1), me), (across(2), me)
    far = [(across(bit), me) for bit in [1 << i for i in range(2, 12)] if bit < dp]
    peers = [partner, above, diagonal, side, level] + far
    barrier = pltpu.get_barrier_semaphore()
    for peer in peers:
        pl.semaphore_signal(barrier, inc=1, device_id=peer, device_id_type=MESH)
    pl.semaphore_wait(barrier, len(peers))

    def remote(source, target, send, recv, device):
        return pltpu.make_async_remote_copy(
            src_ref=source, dst_ref=target, send_sem=send, recv_sem=recv, device_id=device, device_id_type=MESH
        )

    def got(region, recv):
        remote(region, region, recv, recv, partner).wait_recv()

    def sent(region, send):
        remote(region, region, send, send, partner).wait_send()

    quarter = zb * 2 + xb
    q_side, q_level, q_diag = zb * 2 + 1 - xb, (1 - zb) * 2 + xb, 3 - quarter
    tensors = 4 + 2 * (w_up.shape[2] // PIECE)
    q_in, k_in, v_in, o_in = range(4)
    ups, downs = range(4, tensors, 2), range(5, tensors, 2)

    def window(ref, t, q, start):
        piece = (t - 4) // 2 * PIECE
        if t in ups:
            rows = width if q is None else width // 4
            return ref.at[*start, ds(0 if q is None else q * rows, rows), ds(piece, PIECE)]
        rows = PIECE if q is None else PIECE // 4
        return ref.at[*start, ds(piece + (0 if q is None else q * rows), rows, PIECE // 4), :]

    def own(t, q=None):
        if t > o_in:
            return window(up_own if t in ups else down_own, t, q, ())
        rows = ds(0, part) if q is None else rows_of(q, part // 4)
        return out_own.at[rows, :] if t == o_in else qkv_own.at[t, rows, :]

    def region(t, m, q=None):
        if t > o_in:
            return window(w_up if t in ups else w_down, t, q, (m,))
        rows = part if q is None else part // 4
        where = ds(m * part + (0 if q is None else q * rows), rows, part // 4)
        return w_out.at[where, :] if t == o_in else wqkv.at[t, where, :]

    m_core, m_y, m_diag = me + 1 - 2 * c, me + 2 - 4 * y, 3 - me
    through_side = [t in (q_in, v_in) or t in ups for t in range(tensors)]

    for i, peer in enumerate((diagonal, above, partner)):
        remote(small_own, small.at[me], small_send.at[i], small_recv.at[i], peer).start()
    pltpu.make_async_copy(small_own, small.at[me], local.at[0]).start()
    pltpu.make_async_copy(tokens.at[ds(me * count, count), :], x, local.at[1]).start()
    for t in range(tensors):
        remote(own(t, quarter), region(t, me, quarter), ag_send.at[t, 1], ag_recv.at[t, 1], above).start()
        pltpu.make_async_copy(own(t), region(t, me), ag_local.at[t]).start()
        remote(own(t), region(t, me), ag_send.at[t, 0], ag_recv.at[t, 0], partner).start()
    pltpu.make_async_copy(cot_hbm, cot, local.at[2]).start()

    def pass_on(t, q, k, device):
        where = region(t, m_y, q)
        remote(where, where, ag_send.at[t, k], ag_recv.at[t, k], device).start()

    def ag_y(t):
        got(region(t, m_y, quarter), ag_recv.at[t, 1])
        pass_on(t, quarter, 2, side)
        pass_on(t, quarter, 3, level)
        pass_on(t, quarter, 4, partner)

    def ag_side(t):
        got(region(t, m_y, q_side), ag_recv.at[t, 2])
        if not through_side[t]:
            pass_on(t, q_side, 7, level)
        pass_on(t, q_side, 5, partner)

    def ag_level(t):
        got(region(t, m_y, q_level), ag_recv.at[t, 3])
        if through_side[t]:
            pass_on(t, q_level, 7, side)
        pass_on(t, q_level, 6, partner)

    def ag_diag(t):
        got(region(t, m_y, q_diag), ag_recv.at[t, 7])
        pass_on(t, q_diag, 8, partner)

    def ag_near(t):
        pltpu.make_async_copy(own(t), region(t, me), ag_local.at[t]).wait()
        got(region(t, m_core), ag_recv.at[t, 0])

    def ag_rest(t):
        for k, q in ((4, quarter), (5, q_side), (6, q_level), (8, q_diag)):
            got(region(t, m_diag, q), ag_recv.at[t, k])

    def ag_sends(t):
        sent(own(t), ag_send.at[t, 0])
        sent(own(t, quarter), ag_send.at[t, 1])
        for k in range(2, 9):
            sent(own(t, quarter), ag_send.at[t, k])

    vec[...] = jnp.zeros_like(vec)
    for s in range(sequences):
        mine = segment[pl.ds(me * sequences + s, 1), :].astype(F32)
        column = jnp.broadcast_to(mine, (128, LEN)).T[:, :1]
        row_ids = lax.broadcasted_iota(jnp.int32, (LEN, LEN), 0)
        col_ids = lax.broadcasted_iota(jnp.int32, (LEN, LEN), 1)
        allowed = ((column == mine) & (mine != 0.0)) | (row_ids == col_ids)
        bias[s] = jnp.where(allowed, 0.0, -1e30)
        hid[rows_of(s, LEN), :128] = jnp.zeros((LEN, 128), F32)
    pltpu.make_async_copy(small_own, small.at[me], local.at[0]).wait()
    for i, m in enumerate((m_diag, m_y, m_core)):
        got(small.at[m], small_recv.at[i])
    vectors = sum(small[m].astype(F32) for m in range(4))
    pltpu.make_async_copy(tokens.at[ds(0, count), :], x, local.at[1]).wait()
    g1, b1, b_query, b_value, b_out, g2, b2, b_down = (vectors[i : i + 1] for i in range(8))

    def ln_one(i):
        r = rows_of(i, TILE)
        normal, _ = normal_of(x[r, :].astype(F32))
        normed[r, :] = (normal * g1 + b1).astype(BF16)

    each(count // TILE, ln_one)
    lane = lax.broadcasted_iota(jnp.int32, (LEN, 128), 1)
    first = lane < HD
    pairs = half // 128
    small_sum = sum(small[m].astype(F32) for m in range(4))
    vec_recv[0] = small_sum

    def project(side_of, table):
        columns = ds(side_of * half, half, 128)

        def step(i):
            r = rows_of(i, LEN)
            value = normed[r, :]
            biases = vec_recv.at[0]
            query = nt(value, wqkv[0, columns, :]) + biases[2:3, columns]
            qs[r, columns] = (query.astype(BF16).astype(F32) * (HD**-0.5)).astype(BF16)
            ks[r, columns] = nt(value, wqkv[1, columns, :]).astype(BF16)
            vs[r, columns] = (nt(value, wqkv[2, columns, :]) + biases[3:4, columns]).astype(BF16)
            at_steps(i, table)

        each(count // LEN, step)

    def attend(side_of, table):
        def step(i):
            s, p = i // pairs, side_of * pairs + i % pairs
            r, cols = rows_of(s, LEN), rows_of(p, 128)
            q2, k2, v2 = qs[r, cols], ks[r, cols], vs[r, cols]
            results = []
            kept = hid[r, :128]
            for part_of in range(2):
                mine = first if part_of == 0 else ~first
                scores = nt(jnp.where(mine, q2, jnp.zeros_like(q2)), k2) + bias[s]
                top = jnp.max(scores, axis=-1, keepdims=True)
                expo = jnp.exp(scores - top)
                total = jnp.sum(expo, axis=-1, keepdims=True)
                results.append(nn(expo.astype(BF16), v2) * (1.0 / total))
                kept = jnp.where(lane == 2 * p + part_of, top + jnp.log(total), kept)
            hid[r, :128] = kept
            attended[r, cols] = jnp.where(first, results[0], results[1]).astype(BF16)
            at_steps(i, table)

        each(sequences * pairs, step)

    def run(function, *args):
        return functools.partial(function, *args)

    def near(t):
        return [run(ag_side, t), run(ag_level, t)]

    for t in (q_in, k_in, v_in):
        ag_near(t)
    project(y, {0: [run(ag_y, q_in)]})
    attend(
        y,
        {
            0: [run(ag_y, k_in)],
            1: [*near(q_in), run(ag_y, v_in)],
            4: near(k_in),
            5: [run(ag_diag, q_in), *near(v_in), run(ag_y, ups[0]), run(ag_y, downs[0]), run(ag_y, o_in)],
        },
    )
    ag_diag(k_in)
    ag_diag(v_in)
    for t in (q_in, k_in, v_in):
        ag_rest(t)
    project(1 - y, {1: near(ups[0])})
    attend(
        1 - y,
        {
            1: [*near(downs[0]), run(ag_y, ups[1])],
            2: [*near(o_in), run(ag_y, downs[1])],
            3: [run(ag_diag, ups[0])],
            5: [run(ag_diag, downs[0]), *near(ups[1]), run(ag_y, ups[2]), run(ag_y, downs[2])],
        },
    )
    for s in range(sequences):
        stat_rows[s] = hid[rows_of(s, LEN), :128].T
    ag_near(o_in)
    ag_diag(o_in)
    ag_rest(o_in)

    def out_step(i):
        r = rows_of(i, TILE)
        value = x[r, :].astype(F32) + nn(attended[r, :], w_out[...]) + vec_recv[0, 4:5, :]
        hid[r, :] = value
        pltpu.make_async_copy(hid.at[r, :], hidden_hbm.at[r, :], tile_a.at[i]).start()
        normal, _ = normal_of(value)
        n2[r, :] = (normal * vec_recv[0, 5:6, :] + vec_recv[0, 6:7, :]).astype(BF16)
        at_steps(i, {1: near(downs[1]), 3: [run(ag_diag, ups[1])]})

    each(count // TILE, out_step)
    for t in range(o_in + 1, tensors):
        ag_near(t)
    ag_rest(ups[0])
    ag_rest(downs[0])
    pltpu.make_async_copy(cot_hbm, cot, local.at[2]).wait()

    up_bias = vec_recv.at[0]
    feed_slots = 2

    def unit(u, kept, cr, yr, xr):
        rows = kept.shape[0]
        return (u, rows, kept, cr, yr, xr)

    def own_half(rows):
        return ds(xb * (rows // 2), rows // 2, rows // 4)

    def other_half(rows):
        return ds((1 - xb) * (rows // 2), rows // 2, rows // 4)

    def own_quarter(rows):
        return ds(xb * (rows // 2) + zb * (rows // 4), rows // 4)

    def other_quarter(rows):
        return ds(xb * (rows // 2) + (1 - zb) * (rows // 4), rows // 4)

    def send_unit(u, k, source, target, device):
        remote(source, target, unit_send.at[u, k], unit_recv.at[u, k], device).start()

    def take_sum(unit_of):
        u, rows, kept, cr, yr, xr = unit_of
        got(cr, unit_recv.at[u, 2])
        got(yr, unit_recv.at[u, 1])
        add_into(kept, cr, yr)
        pl.semaphore_signal(ready.at[u, 2], inc=1, device_id=level, device_id_type=MESH)
        send_unit(u, 3, kept.at[other_half(rows), :], xr, side)

    def far_room(unit_of, i):
        u, rows, kept, cr, yr, xr = unit_of
        return cr.at[i * (rows // 4) : (i + 1) * (rows // 4), :]

    def send_far(unit_of, i):
        u, rows, kept, cr, yr, xr = unit_of
        pl.semaphore_wait(ready.at[u, 3 + i], 1)
        send_unit(u, 7 + i, kept.at[own_quarter(rows), :], far_room(unit_of, i), far[i])

    def take_side(unit_of):
        u, rows, kept, cr, yr, xr = unit_of
        for i in range(len(far)):
            pl.semaphore_signal(ready.at[u, 3 + i], inc=1, device_id=far[i], device_id_type=MESH)
        got(xr, unit_recv.at[u, 3])
        sent(xr, unit_send.at[u, 3])
        pl.semaphore_signal(ready.at[u, 0], inc=1, device_id=side, device_id_type=MESH)
        add_into(kept.at[own_half(rows), :], xr)
        pl.semaphore_wait(ready.at[u, 2], 1)
        send_unit(u, 4, kept.at[other_quarter(rows), :], yr.at[: rows // 4, :], level)

    def give_level(unit_of):
        u, rows, kept, cr, yr, xr = unit_of
        mine = kept.at[own_quarter(rows), :]
        pl.semaphore_wait(ready.at[u, 1], 1)
        send_unit(u, 5, mine, mine, level)

    def take_level(unit_of):
        u, rows, kept, cr, yr, xr = unit_of
        landed = yr.at[: rows // 4, :]
        got(landed, unit_recv.at[u, 4])
        sent(landed, unit_send.at[u, 4])
        pl.semaphore_signal(ready.at[u, 1], inc=1, device_id=level, device_id_type=MESH)
        mine = kept.at[own_quarter(rows), :]
        add_into(mine, landed)
        if far:
            send_far(unit_of, 0)
        else:
            give_level(unit_of)

    def take_far(unit_of):
        u, rows, kept, cr, yr, xr = unit_of
        mine = kept.at[own_quarter(rows), :]
        for i, _ in enumerate(far):
            landed = far_room(unit_of, i)
            got(landed, unit_recv.at[u, 7 + i])
            sent(mine, unit_send.at[u, 7 + i])
            add_into(mine, landed)
            if i + 1 < len(far):
                send_far(unit_of, i + 1)
        if far:
            give_level(unit_of)

    def give_side(unit_of):
        u, rows, kept, cr, yr, xr = unit_of
        got(kept.at[other_quarter(rows), :], unit_recv.at[u, 5])
        mine = kept.at[own_half(rows), :]
        pl.semaphore_wait(ready.at[u, 0], 1)
        send_unit(u, 6, mine, mine, side)

    def finish(unit_of, target, sem):
        u, rows, kept, cr, yr, xr = unit_of
        got(kept.at[other_half(rows), :], unit_recv.at[u, 6])
        pltpu.make_async_copy(kept, target, sem).start()

    def unit_sends(unit_of):
        u, rows, kept, cr, yr, xr = unit_of
        sent(kept, unit_send.at[u, 1])
        sent(kept.at[own_half(rows), :], unit_send.at[u, 6])
        sent(kept.at[own_quarter(rows), :], unit_send.at[u, 5])

    feeds = [
        unit(s, fp.at[feed_slots + 3 + s], fcr.at[s], fyr.at[s], fxr.at[s]) for s in range(3)
    ]
    smalls = [
        unit(3 + n, op.at[4 * n + 3], ocr.at[n], oyr.at[n], oxr.at[n]) for n in range(4)
    ]
    proj, heads_a, heads_b, shared = smalls

    def feed_first(sub, slot):
        send_unit(sub, 0, fp.at[slot], fcr.at[sub], partner)

    def feed_second(sub, slot):
        got(fcr.at[sub], unit_recv.at[sub, 0])
        add_into(fp.at[slot], fcr.at[sub])
        pl.semaphore_signal(credit, inc=1, device_id=partner, device_id_type=MESH)
        send_unit(sub, 1, fp.at[slot], fyr.at[sub], above)

    def feed_third(sub, slot):
        pl.semaphore_wait(credit, 1)
        send_unit(sub, 2, fp.at[slot], fcr.at[sub], partner)

    steps = 12

    def feed_step(i):
        late, odd, sub = i // 6, i % 2, (i % 6) // 2
        m = 2 * jnp.where(late == 0, 1 - y, y) + jnp.where(odd == 0, 1 - c, c)
        slot = jnp.where(odd == 0, (i // 2) % feed_slots, feed_slots + 3 * late + sub)
        cols = rows_of(sub, PIECE)
        whole = rows_of(m * 3 + sub, PIECE)
        wu, wd = w_up[m, :, cols], w_down[m, cols, :]
        piece_bias = up_bias[pl.ds(8 + m, 1), cols]
        buffer = i % 2

        @pl.when(i >= 2)
        def _():
            pltpu.make_async_copy(act.at[buffer], act_hbm.at[:, whole], act_sem.at[buffer]).wait()

        @pl.when((i >= 4) & (odd == 0))
        def _():
            before = i - 4
            sent(fp.at[slot], unit_send.at[(before % 6) // 2, 2 * (before // 6)])

        def rows_step(j):
            r = rows_of(j, LEN)
            up = nn(n2[r, :], wu) + piece_bias
            half_cdf = 0.5 * (1.0 + lax.erf(up * (0.5**0.5)))
            slope = half_cdf + up * (jnp.exp(-0.5 * up * up) * 0.3989422804014327)
            act[buffer, r, :] = (up * half_cdf).astype(BF16)
            grad = (nt(cot[r, :], wd) * slope).astype(BF16)
            gup[r, whole] = grad
            vec[pl.ds(8 + m, 1), cols] += column_sum(grad.astype(F32))

        each(count // LEN, rows_step)
        pltpu.make_async_copy(act.at[buffer], act_hbm.at[:, whole], act_sem.at[buffer]).start()
        fp[slot, :PIECE, :] = tn(act[buffer], cot[...]).astype(BF16)
        fp[slot, PIECE:, :] = tn(gup[:, whole], n2[...]).astype(BF16)

        @pl.when((late == 0) & (odd == 0))
        def _():
            feed_first(sub, slot)

        @pl.when((late == 0) & (odd == 1))
        def _():
            feed_second(sub, slot)

        @pl.when((late == 1) & (odd == 0))
        def _():
            feed_third(sub, slot)

        at_steps(
            i,
            {
                0: [*near(ups[2]), run(ag_diag, downs[1])],
                1: [*near(downs[2]), run(ag_rest, ups[1]), run(ag_rest, downs[1])],
                3: [run(ag_diag, ups[2]), run(ag_diag, downs[2]), run(ag_rest, ups[2]), run(ag_rest, downs[2])],
                8: [run(take_sum, feeds[0])],
            },
        )

    vec[8:16, :] = jnp.zeros_like(vec[8:16, :])
    each(steps, feed_step)
    for buffer in range(2):
        pltpu.make_async_copy(act.at[buffer], act_hbm.at[:, ds(0, PIECE)], act_sem.at[buffer]).wait()
    for i in range(count // TILE):
        r = rows_of(i, TILE)
        pltpu.make_async_copy(hid.at[r, :], hidden_hbm.at[r, :], tile_a.at[i]).wait()

    def hidden_step(i):
        r = rows_of(i, TILE)
        incoming = nt(gup[r, :width], w_up[0])
        for m in range(1, 4):
            incoming += nt(gup[r, m * width : (m + 1) * width], w_up[m])
        normal, inverse = normal_of(hid[r, :])
        wide = cot[r, :].astype(F32)
        grad = wide + norm_input_back(normal, inverse, incoming * vec_recv[0, 5:6, :])
        hid[r, :] = grad
        vec[4:5, :] += column_sum(grad)
        vec[5:6, :] += column_sum(incoming * normal)
        vec[6:7, :] += column_sum(incoming)
        vec[7:8, :] += column_sum(wide)
        narrow = grad.astype(BF16)
        gup[r, 3 * width :] = narrow
        n2[r, :] = nt(narrow, w_out[...]).astype(BF16)
        at_steps(i, {0: [run(take_side, feeds[0])], 1: [run(take_sum, feeds[1])], 3: [run(take_level, feeds[0])]})

    each(count // TILE, hidden_step)
    product = tn(attended[...], gup[:, 3 * width :])
    for m in range(4):
        slot = 2 * jnp.where(y == m // 2, 1, 0) + jnp.where(c == m % 2, 1, 0)
        op[slot] = product[m * part : (m + 1) * part, :].astype(BF16)

    def small_first(n):
        send_unit(3 + n, 0, op.at[4 * n], ocr.at[n], partner)

    def small_second(n):
        got(ocr.at[n], unit_recv.at[3 + n, 0])
        add_into(op.at[4 * n + 1], ocr.at[n])
        pl.semaphore_signal(credit, inc=1, device_id=partner, device_id_type=MESH)
        send_unit(3 + n, 1, op.at[4 * n + 1], oyr.at[n], above)

    def small_third(n):
        pl.semaphore_wait(credit, 1)
        send_unit(3 + n, 2, op.at[4 * n + 2], ocr.at[n], partner)

    small_first(0)
    def attend_back(side_of, table):
        def step(i):
            s, p = i % sequences, side_of * pairs + 2 * (i // sequences) % pairs
            r, cols = rows_of(s, LEN), rows_of(p, 128)
            q2, k2, v2, d2 = qs[r, cols], ks[r, cols], vs[r, cols], n2[r, cols]
            rq, rk, rv = 0.0, 0.0, 0.0
            for part_of in range(2):
                mine = first if part_of == 0 else ~first
                qm = jnp.where(mine, q2, jnp.zeros_like(q2))
                km = jnp.where(mine, k2, jnp.zeros_like(k2))
                dm = jnp.where(mine, d2, jnp.zeros_like(d2))
                probs = jnp.exp(nt(k2, qm) + bias[s] - stat_rows[s, pl.ds(2 * p + part_of, 1), :])
                grad_probs = nt(v2, dm)
                inner = jnp.sum(probs * grad_probs, axis=0, keepdims=True)
                grad_scores = (probs * (grad_probs - inner)).astype(BF16)
                rv += nn(probs.astype(BF16), dm)
                rk += nn(grad_scores, qm)
                rq += tn(grad_scores, km)
            gup[r, cols] = (rq * (HD**-0.5)).astype(BF16)
            gup[r, ds(width + p * 128, 128)] = rk.astype(BF16)
            gup[r, ds(2 * width + p * 128, 128)] = rv.astype(BF16)
            at_steps(i, table)

        each(sequences * pairs, step)

    def weight_of_pair(side_of, p):
        first_column = side_of * half + p * 128
        grads = jnp.concatenate([gup[:, ds(k * width + first_column, 128)] for k in range(3)], axis=1)
        return tn(grads, normed[...]).astype(BF16)

    def slot_of(core, late):
        return jnp.where(c == core, 1, 0) + 2 * late

    def weight_of_outer(side_of, late):
        for core, p in ((0, 0), (1, 2)):
            product = weight_of_pair(side_of, p)
            slot = slot_of(core, late)
            op[4 + slot] = product[:part]
            op[8 + slot] = product[part:]

    def weight_of_shared(side_of, late):
        product = weight_of_pair(side_of, 1)
        for core in range(2):
            slot = slot_of(core, late)
            for k in range(3):
                start = k * 128 + core * HD
                op[12 + slot, k * HD : (k + 1) * HD, :] = product[start : start + HD]

    attend_back(
        1 - y,
        {
            0: [run(small_second, 0), run(small_third, 0)],
            1: [run(take_side, feeds[1])],
            3: [
                run(weight_of_outer, 1 - y, 0), run(small_first, 1), run(small_first, 2), run(take_sum, feeds[2]),
                run(take_far, feeds[0]), run(take_level, feeds[1]),
            ],
            4: [run(small_second, 1), run(small_second, 2)],
            5: [run(take_sum, proj)],
        },
    )
    weight_of_shared(1 - y, 0)
    small_first(3)
    give_side(feeds[0])
    attend_back(
        y,
        {
            0: [run(small_second, 3)],
            2: [run(take_side, feeds[2]), run(take_far, feeds[1])],
            3: [run(weight_of_outer, y, 1), run(small_third, 1), run(small_third, 2), run(take_side, proj)],
            5: [run(take_sum, heads_a), run(take_sum, heads_b), run(give_side, feeds[1])],
        },
    )
    weight_of_shared(y, 1)
    small_third(3)
    finish(feeds[0], feed_out.at[0], local.at[3])

    def input_step(i):
        r = rows_of(i, TILE)
        q, k, v = gup[r, :width], gup[r, width : 2 * width], gup[r, 2 * width : 3 * width]
        incoming = nn(q, wqkv[0]) + nn(k, wqkv[1]) + nn(v, wqkv[2])
        normal, inverse = normal_of(x[r, :].astype(F32))
        hid[r, :] += norm_input_back(normal, inverse, incoming * vec_recv[0, 0:1, :])
        vec[0:1, :] += column_sum(incoming * normal)
        vec[1:2, :] += column_sum(incoming)
        vec[2:3, :] += column_sum(q.astype(F32))
        vec[3:4, :] += column_sum(v.astype(F32))
        pltpu.make_async_copy(hid.at[r, :], grad_x.at[r, :], tile_a.at[i]).start()
        pltpu.make_async_copy(act_hbm.at[r, :], gup.at[r, :], tile_b.at[i]).start()
        at_steps(
            i,
            {
                0: [run(take_level, feeds[2])],
                1: [run(take_sum, shared), run(take_level, proj)],
                2: [run(take_side, heads_a)],
            },
        )

    each(count // TILE, input_step)

    def reload(i):
        r = rows_of(i, TILE)
        pltpu.make_async_copy(hid.at[r, :], grad_x.at[r, :], tile_a.at[i]).wait()
        pltpu.make_async_copy(hidden_hbm.at[r, :], hid.at[r, :], tile_a.at[i]).start()

    each(count // TILE, reload)
    b_down = vec_recv[0, 7:8, :]

    rounds = [partner, above, side, level] + far

    def vec_start(i):
        remote(vec, vec_recv.at[1 + i], vec_send.at[i], vec_got.at[i], rounds[i]).start()

    def vec_step(i):
        got(vec_recv.at[1 + i], vec_got.at[i])
        sent(vec, vec_send.at[i])
        vec[...] += vec_recv[1 + i]
        if i + 1 < len(rounds):
            vec_start(i + 1)

    vec_start(0)

    def output_step(i):
        r = rows_of(i, TILE)
        pltpu.make_async_copy(hidden_hbm.at[r, :], hid.at[r, :], tile_a.at[i]).wait()
        pltpu.make_async_copy(act_hbm.at[r, :], gup.at[r, :], tile_b.at[i]).wait()
        result = hid[r, :] + b_down
        for m in range(4):
            result += nn(gup[r, m * width : (m + 1) * width], w_down[m])
        x[r, :] = result.astype(BF16)
        pltpu.make_async_copy(x.at[r, :], output.at[r, :], tile_a.at[i]).start()
        at_steps(
            i,
            {
                0: [run(take_side, heads_b), run(vec_step, 0)],
                1: [run(vec_step, 1)],
                2: [run(take_level, heads_a), run(vec_step, 2)],
                3: [run(take_level, heads_b), run(take_far, feeds[2]), run(vec_step, 3)],
            },
        )

    each(count // TILE, output_step)
    for i in range(4, len(rounds)):
        vec_step(i)
    pltpu.make_async_copy(vec, vec_out, local.at[7]).start()

    def place(n):
        kept = smalls[n][2]
        pair_at, shared_at = HD * c, 2 * HD * (1 - c)
        if n == 1:
            moves = ((0, 128, pair_at), (128, 64, part + pair_at))
        elif n == 2:
            moves = ((0, 64, part + pair_at + 64), (64, 128, 2 * part + pair_at))
        else:
            moves = tuple((k * HD, HD, k * part + shared_at) for k in range(3))
        return [
            pltpu.make_async_copy(
                kept.at[start : start + rows, :], qkv_out.at[ds(where, rows, HD), :], local.at[6 + 2 * n + k]
            )
            for k, (start, rows, where) in enumerate(moves)
        ]

    def finish_heads(n):
        rows = smalls[n][1]
        got(smalls[n][2].at[other_half(rows), :], unit_recv.at[3 + n, 6])
        for copy in place(n):
            copy.start()

    finish(feeds[1], feed_out.at[1], local.at[4])
    take_far(proj)
    take_side(shared)
    take_far(heads_a)
    take_far(heads_b)
    give_side(feeds[2])
    give_side(proj)
    take_level(shared)
    give_side(heads_a)
    give_side(heads_b)
    take_far(shared)
    finish(feeds[2], feed_out.at[2], local.at[5])
    give_side(shared)
    finish(proj, proj_out, local.at[6])
    finish_heads(1)
    finish_heads(2)
    finish_heads(3)

    for i in range(3):
        sent(small_own, small_send.at[i])
    for t in range(tensors):
        ag_sends(t)
    for k, slot in ((1, 0), (2, 1)):
        sent(fp.at[slot], unit_send.at[k, 2])
    for n in range(4):
        for k in (0, 2):
            sent(op.at[4 * n + k], unit_send.at[3 + n, k])
    for unit_of in feeds + smalls:
        unit_sends(unit_of)
    for i in range(count // TILE):
        r = rows_of(i, TILE)
        pltpu.make_async_copy(x.at[r, :], output.at[r, :], tile_a.at[i]).wait()
    for s in range(3):
        pltpu.make_async_copy(feeds[s][2], feed_out.at[s], local.at[3 + s]).wait()
    pltpu.make_async_copy(op.at[3], proj_out, local.at[6]).wait()
    for n in range(1, 4):
        for copy in place(n):
            copy.wait()
    pltpu.make_async_copy(vec, vec_out, local.at[7]).wait()


def per_device(
    dp, tokens, segment, ln1_gain, ln1_bias, w_qkv, b_qv, w_out, b_out, ln2_gain, ln2_bias, w_up, b_up, w_down, b_down,
    cotangent,
):
    mp = 4
    me = lax.axis_index("mp")
    count, width = cotangent.shape
    part = width // mp
    feed = w_up.shape[1]
    bits = dp.bit_length() - 1
    far = bits - 2
    pieces = jnp.stack([ln1_gain, ln1_bias, b_qv[0], b_qv[1], b_out, ln2_gain, ln2_bias, b_down])
    small_own = lax.dynamic_update_slice(jnp.zeros((16, width), BF16), pieces, (0, me * part))
    small_own = lax.dynamic_update_slice(small_own, b_up.reshape(1, feed), (8 + me, 0))
    qkv_own = w_qkv.swapaxes(1, 2)

    def shape(*dims, kind=BF16):
        return jax.ShapeDtypeStruct(dims, kind)

    def room(*dims, kind=BF16):
        return pltpu.VMEM(dims, kind)

    unit_rows = 2 * PIECE
    tensors = 4 + 2 * (feed // PIECE)
    dma = pltpu.SemaphoreType.DMA
    outs = [
        shape(count, width), shape(count, width, kind=F32), shape(3, unit_rows, width), shape(part, width),
        shape(3 * part, width), shape(16, width, kind=F32), shape(count, mp * feed), shape(count, width, kind=F32),
    ]

    def unit_rooms(rows, slots, lead):
        return [
            room(slots, rows, width), room(*lead, rows, width), room(*lead, rows, width),
            room(*lead, rows // 2, width),
        ]

    scratch = [
        room(mp, 16, width), room(3, width, width), room(width, width), room(mp, width, feed), room(mp, feed, width),
        *[room(count, width) for _ in range(8)],
        room(count, width, kind=F32), room(count, mp * feed), room(2, count, PIECE),
        room(count // LEN, LEN, LEN, kind=F32), room(count // LEN, 128, LEN, kind=F32), room(16, width, kind=F32),
        room(1 + 2 + bits, 16, width, kind=F32),
        *unit_rooms(unit_rows, 8, (3,)), *unit_rooms(part, 16, (4,)),
        dma((tensors,)), dma((tensors, 9)), dma((tensors, 9)), dma((3,)), dma((3,)), dma((15,)), dma((2,)), dma((4,)), dma((4,)),
        dma((7, 7 + max(far, 1))), dma((7, 7 + max(far, 1))), dma((2 + bits,)), dma((2 + bits,)),
        pltpu.SemaphoreType.REGULAR, pltpu.SemaphoreType.REGULAR((7, 3 + max(far, 1))),
    ]
    args = (
        small_own, qkv_own, w_out, w_up, w_down, tokens, cotangent, segment.reshape(-1, LEN),
    )
    results = pl.pallas_call(
        functools.partial(layer_kernel, dp),
        out_shape=outs,
        in_specs=[HBM] * 7 + [VMEM],
        out_specs=[HBM] * len(outs),
        scratch_shapes=scratch,
        compiler_params=pltpu.CompilerParams(
            vmem_limit_bytes=VMEM_LIMIT, collective_id=0, has_side_effects=True
        ),
    )(*args)
    output, grad_x, feeds, proj, attn, vec = results[:6]
    eight = lax.dynamic_slice_in_dim(vec[:8], me * part, part, 1)
    grad_b_up = lax.dynamic_slice_in_dim(vec, 8 + me, 1, 0).reshape(-1)
    g_down = feeds[:, :PIECE].reshape(feed, width).astype(F32)
    g_up = feeds[:, PIECE:].reshape(feed, width).T.astype(F32)
    g_qkv = attn.reshape(3, part, width).swapaxes(1, 2).astype(F32)
    return (
        output, grad_x, eight[0], eight[1], g_qkv, eight[2:4], proj.astype(F32), eight[4], eight[5], eight[6],
        g_up, grad_b_up, g_down, eight[7],
    )


def solution(mesh):
    rows = P(("dp", "mp"), None)
    return jax.shard_map(
        functools.partial(per_device, mesh.shape["dp"]),
        mesh=mesh,
        in_specs=(
            P("dp", None), P("dp"), P("mp"), P("mp"), P(None, None, "mp"), P(None, "mp"), P("mp", None), P("mp"),
            P("mp"), P("mp"), P(None, "mp"), P("mp"), P("mp", None), P("mp"), rows,
        ),
        out_specs=(
            rows, rows, P("mp"), P("mp"), P(None, None, "mp"), P(None, "mp"), P("mp", None), P("mp"), P("mp"), P("mp"),
            P(None, "mp"), P("mp"), P("mp", None), P("mp"),
        ),
        check_vma=False,
    )
```

```python
import functools

import jax
import jax.numpy as jnp
from jax import lax
from jax.experimental import pallas as pl
from jax.experimental.pallas import tpu as pltpu
from jax.sharding import PartitionSpec as P

HD = 64
LEN = 512
PIECE = 256
TILE = 256
F32 = jnp.float32
BF16 = jnp.bfloat16
MESH = pl.DeviceIdType.MESH
VMEM_LIMIT = 67043328
HBM = pl.BlockSpec(memory_space=pl.ANY)
VMEM = pl.BlockSpec(memory_space=pltpu.VMEM)


def nn(left, right):
    return jnp.dot(left, right, preferred_element_type=F32)


def nt(left, right):
    return lax.dot_general(left, right, (((1,), (1,)), ((), ())), preferred_element_type=F32)


def tn(left, right):
    return lax.dot_general(left, right, (((0,), (0,)), ((), ())), preferred_element_type=F32)


def ds(start, size, step=None):
    if isinstance(start, int):
        return pl.ds(start, size)
    return pl.ds(pl.multiple_of(start, step or size), size)


def rows_of(index, count):
    return ds(index * count, count)


def normal_of(values):
    centered = values - jnp.mean(values, axis=-1, keepdims=True)
    spread = jnp.mean(centered * centered, axis=-1, keepdims=True)
    inverse = lax.rsqrt(spread + 1e-06)
    return centered * inverse, inverse


def norm_input_back(normal, inverse, scaled):
    inner = jnp.mean(scaled * normal, axis=-1, keepdims=True)
    return inverse * (scaled - jnp.mean(scaled, axis=-1, keepdims=True) - normal * inner)


def column_sum(values):
    return jnp.sum(values, axis=0, keepdims=True)


def each(count, body):
    lax.fori_loop(0, count, lambda i, carry: (body(i), carry)[1], 0)


def at_steps(index, table):
    for step, actions in table.items():

        @pl.when(index == step)
        def _(actions=actions):
            for action in actions:
                action()


def add_into(target, *sources):
    rows = target.shape[0]
    tile = 64 if rows % 64 == 0 else 48

    def step(i):
        r = rows_of(i, tile)
        value = target[r, :].astype(F32)
        for source in sources:
            value += source[r, :].astype(F32)
        target[r, :] = value.astype(BF16)

    each(rows // tile, step)


def layer_kernel(
    dp, small_own, qkv_own, out_own, up_own, down_own, tokens, cot_hbm, segment,
    output, grad_x, down_out, up_out, proj_out, qkv_out, vec_out, act_hbm, hidden_hbm,
    small, wqkv, w_out, w_up, w_down, x, cot, normed, qs, ks, vs, attended, n2, hid, gup, act, bias,
    stat_rows, vec, vec_recv, fp, fcr, fyr, fxr, op, ocr, oyr, oxr,
    ag_local, ag_send, ag_recv, small_send, small_recv, local, feed_done, act_sem, tile_a, tile_b, tile_c, unit_send, unit_recv,
    vec_send, vec_got, credit, ready,
):
    me, d = lax.axis_index("mp"), lax.axis_index("dp")
    y, c = me // 2, me % 2
    count, width = x.shape
    part = width // 4
    half = width // 2
    sequences = count // LEN
    xb, zb = d % 2, (d // 2) % 2

    def across(bit):
        return d + bit - 2 * bit * ((d // bit) % 2)

    partner, above = (d, me + 1 - 2 * c), (d, me + 2 - 4 * y)
    diagonal = (d, 3 - me)
    side, level = (across(1), me), (across(2), me)
    far = [(across(bit), me) for bit in [1 << i for i in range(2, 12)] if bit < dp]
    peers = [partner, above, diagonal, side, level] + far
    barrier = pltpu.get_barrier_semaphore()
    for peer in peers:
        pl.semaphore_signal(barrier, inc=1, device_id=peer, device_id_type=MESH)
    pl.semaphore_wait(barrier, len(peers))

    def remote(source, target, send, recv, device):
        return pltpu.make_async_remote_copy(
            src_ref=source, dst_ref=target, send_sem=send, recv_sem=recv, device_id=device, device_id_type=MESH
        )

    def got(region, recv):
        remote(region, region, recv, recv, partner).wait_recv()

    def sent(region, send):
        remote(region, region, send, send, partner).wait_send()

    quarter = zb * 2 + xb
    q_side, q_level, q_diag = zb * 2 + 1 - xb, (1 - zb) * 2 + xb, 3 - quarter
    tensors = 4 + 2 * (w_up.shape[2] // PIECE)
    q_in, k_in, v_in, o_in = range(4)
    ups, downs = range(4, tensors, 2), range(5, tensors, 2)

    def window(ref, t, q, start):
        piece = (t - 4) // 2 * PIECE
        if t in ups:
            rows = width if q is None else width // 4
            return ref.at[*start, ds(0 if q is None else q * rows, rows), ds(piece, PIECE)]
        rows = PIECE if q is None else PIECE // 4
        return ref.at[*start, ds(piece + (0 if q is None else q * rows), rows, PIECE // 4), :]

    def own(t, q=None):
        if t > o_in:
            return window(up_own if t in ups else down_own, t, q, ())
        rows = ds(0, part) if q is None else rows_of(q, part // 4)
        return out_own.at[rows, :] if t == o_in else qkv_own.at[t, rows, :]

    def region(t, m, q=None):
        if t > o_in:
            return window(w_up if t in ups else w_down, t, q, (m,))
        rows = part if q is None else part // 4
        where = ds(m * part + (0 if q is None else q * rows), rows, part // 4)
        return w_out.at[where, :] if t == o_in else wqkv.at[t, where, :]

    m_core, m_y, m_diag = me + 1 - 2 * c, me + 2 - 4 * y, 3 - me
    through_side = [t in (q_in, v_in) or t in ups for t in range(tensors)]

    for i, peer in enumerate((diagonal, above, partner)):
        remote(small_own, small.at[me], small_send.at[i], small_recv.at[i], peer).start()
    pltpu.make_async_copy(small_own, small.at[me], local.at[0]).start()
    pltpu.make_async_copy(tokens.at[ds(me * count, count), :], x, local.at[1]).start()
    for t in range(tensors):
        remote(own(t, quarter), region(t, me, quarter), ag_send.at[t, 1], ag_recv.at[t, 1], above).start()
        pltpu.make_async_copy(own(t), region(t, me), ag_local.at[t]).start()
        remote(own(t), region(t, me), ag_send.at[t, 0], ag_recv.at[t, 0], partner).start()
    pltpu.make_async_copy(cot_hbm, cot, local.at[2]).start()

    def pass_on(t, q, k, device):
        where = region(t, m_y, q)
        remote(where, where, ag_send.at[t, k], ag_recv.at[t, k], device).start()

    def ag_y(t):
        got(region(t, m_y, quarter), ag_recv.at[t, 1])
        pass_on(t, quarter, 2, side)
        pass_on(t, quarter, 3, level)
        pass_on(t, quarter, 4, partner)

    def ag_side(t):
        got(region(t, m_y, q_side), ag_recv.at[t, 2])
        if not through_side[t]:
            pass_on(t, q_side, 7, level)
        pass_on(t, q_side, 5, partner)

    def ag_level(t):
        got(region(t, m_y, q_level), ag_recv.at[t, 3])
        if through_side[t]:
            pass_on(t, q_level, 7, side)
        pass_on(t, q_level, 6, partner)

    def ag_diag(t):
        got(region(t, m_y, q_diag), ag_recv.at[t, 7])
        pass_on(t, q_diag, 8, partner)

    def ag_near(t):
        pltpu.make_async_copy(own(t), region(t, me), ag_local.at[t]).wait()
        got(region(t, m_core), ag_recv.at[t, 0])

    def ag_rest(t):
        for k, q in ((4, quarter), (5, q_side), (6, q_level), (8, q_diag)):
            got(region(t, m_diag, q), ag_recv.at[t, k])

    def ag_sends(t):
        sent(own(t), ag_send.at[t, 0])
        sent(own(t, quarter), ag_send.at[t, 1])
        for k in range(2, 9):
            sent(own(t, quarter), ag_send.at[t, k])

    vec[...] = jnp.zeros_like(vec)
    for s in range(sequences):
        mine = segment[pl.ds(me * sequences + s, 1), :].astype(F32)
        column = jnp.broadcast_to(mine, (128, LEN)).T[:, :1]
        row_ids = lax.broadcasted_iota(jnp.int32, (LEN, LEN), 0)
        col_ids = lax.broadcasted_iota(jnp.int32, (LEN, LEN), 1)
        allowed = ((column == mine) & (mine != 0.0)) | (row_ids == col_ids)
        bias[s] = jnp.where(allowed, 0.0, -1e30)
        hid[rows_of(s, LEN), :128] = jnp.zeros((LEN, 128), F32)
    pltpu.make_async_copy(small_own, small.at[me], local.at[0]).wait()
    for i, m in enumerate((m_diag, m_y, m_core)):
        got(small.at[m], small_recv.at[i])
    place_row = lax.broadcasted_iota(jnp.int32, (part, width), 0)
    place_column = lax.broadcasted_iota(jnp.int32, (part, width), 1)
    vec_recv[0] = jnp.zeros(vec_recv.shape[1:], F32)
    for m in range(4):
        into = jnp.where(place_column == place_row + m * part, 1.0, 0.0).astype(BF16)
        vec_recv[0, :8, :] += nn(small[m, :8, :], into)
        for owner in range(4):
            vec_recv[0, 8 + owner : 9 + owner, :] += nn(small[owner, 8 + m : 9 + m, :], into)
    vectors = vec_recv[0]
    pltpu.make_async_copy(tokens.at[ds(0, count), :], x, local.at[1]).wait()
    g1, b1, b_query, b_value, b_out, g2, b2, b_down = (vectors[i : i + 1] for i in range(8))

    def ln_one(i):
        r = rows_of(i, TILE)
        normal, _ = normal_of(x[r, :].astype(F32))
        normed[r, :] = (normal * g1 + b1).astype(BF16)

    each(count // TILE, ln_one)
    lane = lax.broadcasted_iota(jnp.int32, (LEN, 128), 1)
    first = lane < HD
    pairs = half // 128

    def project(side_of, table):
        columns = ds(side_of * half, half, 128)

        def step(i):
            r = rows_of(i, LEN)
            value = normed[r, :]
            biases = vec_recv.at[0]
            query = nt(value, wqkv[0, columns, :]) + biases[2:3, columns]
            qs[r, columns] = (query.astype(BF16).astype(F32) * (HD**-0.5)).astype(BF16)
            ks[r, columns] = nt(value, wqkv[1, columns, :]).astype(BF16)
            vs[r, columns] = (nt(value, wqkv[2, columns, :]) + biases[3:4, columns]).astype(BF16)
            at_steps(i, table)

        each(count // LEN, step)

    def attend(side_of, table):
        def step(i):
            s, p = i // pairs, side_of * pairs + i % pairs
            r, cols = rows_of(s, LEN), rows_of(p, 128)
            q2, k2, v2 = qs[r, cols], ks[r, cols], vs[r, cols]
            results = []
            kept = hid[r, :128]
            for part_of in range(2):
                mine = first if part_of == 0 else ~first
                scores = nt(jnp.where(mine, q2, jnp.zeros_like(q2)), k2) + bias[s]
                top = jnp.max(scores, axis=-1, keepdims=True)
                expo = jnp.exp(scores - top)
                total = jnp.sum(expo, axis=-1, keepdims=True)
                results.append(nn(expo.astype(BF16), v2) * (1.0 / total))
                kept = jnp.where(lane == 2 * p + part_of, top + jnp.log(total), kept)
            hid[r, :128] = kept
            attended[r, cols] = jnp.where(first, results[0], results[1]).astype(BF16)
            at_steps(i, table)

        each(sequences * pairs, step)

    def run(function, *args):
        return functools.partial(function, *args)

    def near(t):
        return [run(ag_side, t), run(ag_level, t)]

    for t in (q_in, k_in, v_in):
        ag_near(t)
    project(y, {0: [run(ag_y, q_in)]})
    attend(
        y,
        {
            0: [run(ag_y, k_in)],
            1: [*near(q_in), run(ag_y, v_in)],
            4: near(k_in),
            5: [run(ag_diag, q_in), *near(v_in), run(ag_y, ups[0]), run(ag_y, downs[0]), run(ag_y, o_in)],
        },
    )
    ag_diag(k_in)
    ag_diag(v_in)
    for t in (q_in, k_in, v_in):
        ag_rest(t)
    project(1 - y, {1: near(ups[0])})
    attend(
        1 - y,
        {
            1: [*near(downs[0]), run(ag_y, ups[1])],
            2: [*near(o_in), run(ag_y, downs[1])],
            3: [run(ag_diag, ups[0])],
            5: [run(ag_diag, downs[0]), *near(ups[1]), run(ag_y, ups[2]), run(ag_y, downs[2])],
        },
    )
    for s in range(sequences):
        stat_rows[s] = hid[rows_of(s, LEN), :128].T
    ag_near(o_in)
    ag_diag(o_in)
    ag_rest(o_in)

    def out_step(i):
        r = rows_of(i, TILE)
        value = x[r, :].astype(F32) + nn(attended[r, :], w_out[...]) + vec_recv[0, 4:5, :]
        hid[r, :] = value
        pltpu.make_async_copy(hid.at[r, :], hidden_hbm.at[r, :], tile_a.at[i]).start()
        normal, _ = normal_of(value)
        n2[r, :] = (normal * vec_recv[0, 5:6, :] + vec_recv[0, 6:7, :]).astype(BF16)
        at_steps(i, {1: near(downs[1]), 3: [run(ag_diag, ups[1])]})

    each(count // TILE, out_step)
    for t in range(o_in + 1, tensors):
        ag_near(t)
    ag_rest(ups[0])
    ag_rest(downs[0])
    pltpu.make_async_copy(cot_hbm, cot, local.at[2]).wait()

    up_bias = vec_recv.at[0]
    feed_slots = 2
    rounds_far = max(len(far), 1)

    def unit(u, kept, cr, yr, xr):
        rows = kept.shape[0]
        return (u, rows, kept, cr, yr, xr)

    def own_half(rows):
        return ds(xb * (rows // 2), rows // 2, rows // 4)

    def other_half(rows):
        return ds((1 - xb) * (rows // 2), rows // 2, rows // 4)

    def own_quarter(rows):
        return ds(xb * (rows // 2) + zb * (rows // 4), rows // 4)

    def other_quarter(rows):
        return ds(xb * (rows // 2) + (1 - zb) * (rows // 4), rows // 4)

    def send_unit(u, k, source, target, device):
        remote(source, target, unit_send.at[u, k], unit_recv.at[u, k], device).start()

    def take_sum(unit_of):
        u, rows, kept, cr, yr, xr = unit_of
        got(cr, unit_recv.at[u, 2])
        got(yr, unit_recv.at[u, 1])
        add_into(kept, cr, yr)
        pl.semaphore_signal(ready.at[u, 2], inc=1, device_id=level, device_id_type=MESH)
        send_unit(u, 3, kept.at[other_half(rows), :], xr, side)

    def far_room(unit_of, i):
        u, rows, kept, cr, yr, xr = unit_of
        return cr.at[i * (rows // 4) : (i + 1) * (rows // 4), :]

    def send_far(unit_of, i):
        u, rows, kept, cr, yr, xr = unit_of
        pl.semaphore_wait(ready.at[u, 3 + i], 1)
        send_unit(u, 7 + i, kept.at[own_quarter(rows), :], far_room(unit_of, i), far[i])

    def take_side(unit_of):
        u, rows, kept, cr, yr, xr = unit_of
        for i in range(len(far)):
            pl.semaphore_signal(ready.at[u, 3 + i], inc=1, device_id=far[i], device_id_type=MESH)
        got(xr, unit_recv.at[u, 3])
        sent(xr, unit_send.at[u, 3])
        pl.semaphore_signal(ready.at[u, 0], inc=1, device_id=side, device_id_type=MESH)
        add_into(kept.at[own_half(rows), :], xr)
        pl.semaphore_wait(ready.at[u, 2], 1)
        send_unit(u, 4, kept.at[other_quarter(rows), :], yr.at[: rows // 4, :], level)

    def give_level(unit_of):
        u, rows, kept, cr, yr, xr = unit_of
        mine = kept.at[own_quarter(rows), :]
        pl.semaphore_wait(ready.at[u, 1], 1)
        send_unit(u, 5, mine, mine, level)
        pl.semaphore_wait(ready.at[u, 0], 1)
        send_unit(u, 6, mine, mine, side)

    def take_level(unit_of):
        u, rows, kept, cr, yr, xr = unit_of
        landed = yr.at[: rows // 4, :]
        got(landed, unit_recv.at[u, 4])
        sent(landed, unit_send.at[u, 4])
        pl.semaphore_signal(ready.at[u, 1], inc=1, device_id=level, device_id_type=MESH)
        mine = kept.at[own_quarter(rows), :]
        add_into(mine, landed)
        if far:
            send_far(unit_of, 0)
        else:
            give_level(unit_of)

    def take_far(unit_of):
        u, rows, kept, cr, yr, xr = unit_of
        mine = kept.at[own_quarter(rows), :]
        for i, _ in enumerate(far):
            landed = far_room(unit_of, i)
            got(landed, unit_recv.at[u, 7 + i])
            sent(mine, unit_send.at[u, 7 + i])
            add_into(mine, landed)
            if i + 1 < len(far):
                send_far(unit_of, i + 1)
        if far:
            give_level(unit_of)

    def give_side(unit_of):
        u, rows, kept, cr, yr, xr = unit_of
        other = kept.at[other_quarter(rows), :]
        got(other, unit_recv.at[u, 5])
        send_unit(u, 7 + rounds_far, other, other, side)

    def finish(unit_of, copies):
        u, rows, kept, cr, yr, xr = unit_of
        got(kept.at[own_quarter(rows), :], unit_recv.at[u, 6])
        got(kept.at[own_quarter(rows), :], unit_recv.at[u, 7 + rounds_far])
        for copy in copies():
            copy.start()

    def place_feed(sub):
        kept, piece = feeds[sub][2], slice(sub * PIECE, (sub + 1) * PIECE)
        blocks = [slice(k * PIECE, (k + 1) * PIECE) for k in range(width // PIECE)]
        moves = [(kept.at[:PIECE, :], down_out.at[piece, :])]
        moves += [(kept.at[PIECE:, block], up_out.at[block, piece]) for block in blocks]
        return [pltpu.make_async_copy(*move, feed_done.at[sub, k]) for k, move in enumerate(moves)]

    def place_proj():
        return [pltpu.make_async_copy(op.at[3], proj_out, local.at[6])]

    def unit_sends(unit_of):
        u, rows, kept, cr, yr, xr = unit_of
        sent(kept.at[own_half(rows), :] if u == 2 else kept, unit_send.at[u, 1])
        for k in (5, 6, 7 + rounds_far):
            sent(kept.at[own_quarter(rows), :], unit_send.at[u, k])

    feeds = [
        unit(s, fp.at[feed_slots + 3 + s], fcr.at[s], fyr.at[s], fxr.at[s]) for s in range(3)
    ]
    smalls = [
        unit(3 + n, op.at[4 * n + 3], ocr.at[n], oyr.at[n], oxr.at[n]) for n in range(4)
    ]
    proj, heads_a, heads_b, shared = smalls

    def feed_first(sub, slot):
        send_unit(sub, 0, fp.at[slot], fcr.at[sub], partner)

    def feed_second(sub, slot):
        got(fcr.at[sub], unit_recv.at[sub, 0])
        add_into(fp.at[slot], fcr.at[sub])
        pl.semaphore_signal(credit, inc=1, device_id=partner, device_id_type=MESH)

        @pl.when(sub < 2)
        def _():
            send_unit(sub, 1, fp.at[slot], fyr.at[sub], above)

        @pl.when(sub == 2)
        def _():
            rows = fp.shape[1]
            send_unit(2, 8 + rounds_far, fp.at[slot, other_half(rows), :], fyr.at[2, own_half(rows), :], side)

    def last_other():
        _, rows, _, _, yr, _ = feeds[2]
        passed = fp.at[feed_slots + 2]
        landed = yr.at[other_half(rows), :]
        got(landed, unit_recv.at[2, 8 + rounds_far])
        add_into(passed.at[own_half(rows), :], landed)
        send_unit(2, 1, passed.at[own_half(rows), :], yr.at[own_half(rows), :], above)

    def last_sum():
        u, rows, kept, cr, _, xr = feeds[2]
        got(cr, unit_recv.at[u, 2])
        add_into(kept, cr)
        for i in range(len(far)):
            pl.semaphore_signal(ready.at[u, 3 + i], inc=1, device_id=far[i], device_id_type=MESH)
        send_unit(u, 3, kept.at[other_half(rows), :], xr, side)

    def last_both():
        u, rows, kept, _, yr, xr = feeds[2]
        mine, landed = kept.at[own_half(rows), :], yr.at[own_half(rows), :]
        got(xr, unit_recv.at[u, 3])
        sent(xr, unit_send.at[u, 3])
        pl.semaphore_signal(ready.at[u, 0], inc=1, device_id=side, device_id_type=MESH)
        got(landed, unit_recv.at[u, 1])
        add_into(mine, xr, landed)
        pl.semaphore_signal(ready.at[u, 2], inc=1, device_id=level, device_id_type=MESH)
        pl.semaphore_wait(ready.at[u, 2], 1)
        send_unit(u, 4, kept.at[other_quarter(rows), :], yr.at[: rows // 4, :], level)

    def feed_third(sub, slot):
        pl.semaphore_wait(credit, 1)
        send_unit(sub, 2, fp.at[slot], fcr.at[sub], partner)

    steps = 12

    def feed_step(i):
        late, odd, sub = i // 6, i % 2, (i % 6) // 2
        m = 2 * jnp.where(late == 0, 1 - y, y) + jnp.where(odd == 0, 1 - c, c)
        slot = jnp.where(odd == 0, (i // 2) % feed_slots, feed_slots + 3 * late + sub)
        cols = rows_of(sub, PIECE)
        whole = rows_of(m * 3 + sub, PIECE)
        wu, wd = w_up[m, :, cols], w_down[m, cols, :]
        piece_bias = up_bias[pl.ds(8 + m, 1), cols]
        buffer = i % 2

        @pl.when(i >= 2)
        def _():
            pltpu.make_async_copy(act.at[buffer], act_hbm.at[:, whole], act_sem.at[buffer]).wait()

        @pl.when((i >= 4) & (odd == 0))
        def _():
            before = i - 4
            sent(fp.at[slot], unit_send.at[(before % 6) // 2, 2 * (before // 6)])

        def rows_step(j):
            r = rows_of(j, LEN)
            up = nn(n2[r, :], wu) + piece_bias
            half_cdf = 0.5 * (1.0 + lax.erf(up * (0.5**0.5)))
            slope = half_cdf + up * (jnp.exp(-0.5 * up * up) * 0.3989422804014327)
            act[buffer, r, :] = (up * half_cdf).astype(BF16)
            grad = (nt(cot[r, :], wd) * slope).astype(BF16)
            gup[r, whole] = grad
            vec[pl.ds(8 + m, 1), cols] += column_sum(grad.astype(F32))

        each(count // LEN, rows_step)
        pltpu.make_async_copy(act.at[buffer], act_hbm.at[:, whole], act_sem.at[buffer]).start()
        fp[slot, :PIECE, :] = tn(act[buffer], cot[...]).astype(BF16)
        product = tn(n2[...], gup[:, whole]).astype(BF16)
        for k in range(width // PIECE):
            fp[slot, PIECE:, k * PIECE : (k + 1) * PIECE] = product[k * PIECE : (k + 1) * PIECE, :]

        @pl.when((late == 0) & (odd == 0))
        def _():
            feed_first(sub, slot)

        @pl.when((late == 0) & (odd == 1))
        def _():
            feed_second(sub, slot)

        @pl.when((late == 1) & (odd == 0))
        def _():
            feed_third(sub, slot)

        at_steps(
            i,
            {
                0: [*near(ups[2]), run(ag_diag, downs[1])],
                1: [*near(downs[2]), run(ag_rest, ups[1]), run(ag_rest, downs[1])],
                3: [run(ag_diag, ups[2]), run(ag_diag, downs[2]), run(ag_rest, ups[2]), run(ag_rest, downs[2])],
                8: [run(take_sum, feeds[0])],
                9: [last_other],
            },
        )

    vec[8:16, :] = jnp.zeros_like(vec[8:16, :])
    each(steps, feed_step)
    for buffer in range(2):
        pltpu.make_async_copy(act.at[buffer], act_hbm.at[:, ds(0, PIECE)], act_sem.at[buffer]).wait()
    for i in range(count // TILE):
        r = rows_of(i, TILE)
        pltpu.make_async_copy(hid.at[r, :], hidden_hbm.at[r, :], tile_a.at[i]).wait()

    def hidden_step(i):
        r = rows_of(i, TILE)
        incoming = nt(gup[r, :width], w_up[0])
        for m in range(1, 4):
            incoming += nt(gup[r, m * width : (m + 1) * width], w_up[m])
        normal, inverse = normal_of(hid[r, :])
        wide = cot[r, :].astype(F32)
        grad = wide + norm_input_back(normal, inverse, incoming * vec_recv[0, 5:6, :])
        hid[r, :] = grad
        vec[4:5, :] += column_sum(grad)
        vec[5:6, :] += column_sum(incoming * normal)
        vec[6:7, :] += column_sum(incoming)
        vec[7:8, :] += column_sum(wide)
        narrow = grad.astype(BF16)
        gup[r, 3 * width :] = narrow
        n2[r, :] = nt(narrow, w_out[...]).astype(BF16)
        at_steps(i, {0: [last_sum, run(take_side, feeds[0])], 1: [run(take_sum, feeds[1])], 3: [run(take_level, feeds[0])]})

    each(count // TILE, hidden_step)
    product = tn(attended[...], gup[:, 3 * width :])
    for m in range(4):
        slot = 2 * jnp.where(y == m // 2, 1, 0) + jnp.where(c == m % 2, 1, 0)
        op[slot] = product[m * part : (m + 1) * part, :].astype(BF16)

    def small_first(n):
        send_unit(3 + n, 0, op.at[4 * n], ocr.at[n], partner)

    def small_second(n):
        got(ocr.at[n], unit_recv.at[3 + n, 0])
        add_into(op.at[4 * n + 1], ocr.at[n])
        pl.semaphore_signal(credit, inc=1, device_id=partner, device_id_type=MESH)
        send_unit(3 + n, 1, op.at[4 * n + 1], oyr.at[n], above)

    def small_third(n):
        pl.semaphore_wait(credit, 1)
        send_unit(3 + n, 2, op.at[4 * n + 2], ocr.at[n], partner)

    small_first(0)
    def attend_back(side_of, table):
        def step(i):
            s, p = i % sequences, side_of * pairs + 2 * (i // sequences) % pairs
            r, cols = rows_of(s, LEN), rows_of(p, 128)
            q2, k2, v2, d2 = qs[r, cols], ks[r, cols], vs[r, cols], n2[r, cols]
            rq, rk, rv = 0.0, 0.0, 0.0
            for part_of in range(2):
                mine = first if part_of == 0 else ~first
                qm = jnp.where(mine, q2, jnp.zeros_like(q2))
                km = jnp.where(mine, k2, jnp.zeros_like(k2))
                dm = jnp.where(mine, d2, jnp.zeros_like(d2))
                probs = jnp.exp(nt(k2, qm) + bias[s] - stat_rows[s, pl.ds(2 * p + part_of, 1), :])
                grad_probs = nt(v2, dm)
                inner = jnp.sum(probs * grad_probs, axis=0, keepdims=True)
                grad_scores = (probs * (grad_probs - inner)).astype(BF16)
                rv += nn(probs.astype(BF16), dm)
                rk += nn(grad_scores, qm)
                rq += tn(grad_scores, km)
            gup[r, cols] = (rq * (HD**-0.5)).astype(BF16)
            gup[r, ds(width + p * 128, 128)] = rk.astype(BF16)
            gup[r, ds(2 * width + p * 128, 128)] = rv.astype(BF16)
            at_steps(i, table)

        each(sequences * pairs, step)

    def weight_of_pair(side_of, p):
        first_column = side_of * half + p * 128
        grads = jnp.concatenate([gup[:, ds(k * width + first_column, 128)] for k in range(3)], axis=1)
        return tn(grads, normed[...]).astype(BF16)

    def slot_of(core, late):
        return jnp.where(c == core, 1, 0) + 2 * late

    def weight_of_outer(side_of, late):
        for core, p in ((0, 0), (1, 2)):
            product = weight_of_pair(side_of, p)
            slot = slot_of(core, late)
            op[4 + slot] = product[:part]
            op[8 + slot] = product[part:]

    def weight_of_shared(side_of, late):
        product = weight_of_pair(side_of, 1)
        for core in range(2):
            slot = slot_of(core, late)
            for k in range(3):
                start = k * 128 + core * HD
                op[12 + slot, k * HD : (k + 1) * HD, :] = product[start : start + HD]

    attend_back(
        1 - y,
        {
            0: [run(small_second, 0), run(small_third, 0), last_both],
            3: [
                run(weight_of_outer, 1 - y, 0), run(small_first, 1), run(small_first, 2), run(take_level, feeds[2]),
                run(take_far, feeds[0]), run(take_side, feeds[1]), run(take_sum, proj),
            ],
            4: [run(small_second, 1), run(small_second, 2)],
        },
    )
    weight_of_shared(1 - y, 0)
    small_first(3)
    take_side(proj)
    attend_back(
        y,
        {
            0: [run(small_second, 3), run(give_side, feeds[0])],
            2: [run(take_level, feeds[1])],
            3: [run(weight_of_outer, y, 1), run(small_third, 1), run(small_third, 2), run(take_far, feeds[2])],
            4: [run(take_sum, heads_a), run(take_level, proj)],
            5: [run(take_sum, heads_b)],
        },
    )
    weight_of_shared(y, 1)
    small_third(3)
    finish(feeds[0], run(place_feed, 0))

    def input_step(i):
        r = rows_of(i, TILE)
        q, k, v = gup[r, :width], gup[r, width : 2 * width], gup[r, 2 * width : 3 * width]
        incoming = nn(q, wqkv[0]) + nn(k, wqkv[1]) + nn(v, wqkv[2])
        normal, inverse = normal_of(x[r, :].astype(F32))
        hid[r, :] += norm_input_back(normal, inverse, incoming * vec_recv[0, 0:1, :])
        vec[0:1, :] += column_sum(incoming * normal)
        vec[1:2, :] += column_sum(incoming)
        vec[2:3, :] += column_sum(q.astype(F32))
        vec[3:4, :] += column_sum(v.astype(F32))
        pltpu.make_async_copy(hid.at[r, :], grad_x.at[r, :], tile_c.at[i]).start()
        pltpu.make_async_copy(act_hbm.at[r, :], gup.at[r, :], tile_b.at[i]).start()
        at_steps(
            i,
            {
                0: [run(take_side, heads_a)],
                1: [run(take_sum, shared), run(take_far, feeds[1]), run(give_side, feeds[2])],
                3: [run(take_side, heads_b), run(take_far, proj)],
            },
        )

    each(count // TILE, input_step)

    def reload(i):
        r = rows_of(i, TILE)
        pltpu.make_async_copy(hid.at[r, :], grad_x.at[r, :], tile_c.at[i]).wait()
        pltpu.make_async_copy(hidden_hbm.at[r, :], hid.at[r, :], tile_a.at[i]).start()

    each(count // TILE, reload)
    b_down = vec_recv[0, 7:8, :]

    rounds = [partner, above, side, level] + far

    def vec_start(i):
        remote(vec, vec_recv.at[1 + i], vec_send.at[i], vec_got.at[i], rounds[i]).start()

    def vec_step(i):
        got(vec_recv.at[1 + i], vec_got.at[i])
        sent(vec, vec_send.at[i])
        vec[...] += vec_recv[1 + i]
        if i + 1 < len(rounds):
            vec_start(i + 1)

    vec_start(0)

    def output_step(i):
        r = rows_of(i, TILE)
        pltpu.make_async_copy(hidden_hbm.at[r, :], hid.at[r, :], tile_a.at[i]).wait()
        pltpu.make_async_copy(act_hbm.at[r, :], gup.at[r, :], tile_b.at[i]).wait()
        result = hid[r, :] + b_down
        for m in range(4):
            result += nn(gup[r, m * width : (m + 1) * width], w_down[m])
        x[r, :] = result.astype(BF16)
        pltpu.make_async_copy(x.at[r, :], output.at[r, :], tile_a.at[i]).start()
        at_steps(
            i,
            {
                0: [run(take_level, heads_a), run(vec_step, 0)],
                1: [run(take_side, shared), run(vec_step, 1)],
                2: [run(give_side, feeds[1]), run(vec_step, 2)],
                3: [run(take_level, heads_b), run(vec_step, 3)],
            },
        )

    each(count // TILE, output_step)
    def place(n):
        kept = smalls[n][2]
        pair_at, shared_at = HD * c, 2 * HD * (1 - c)
        if n == 1:
            moves = ((0, 128, pair_at), (128, 64, part + pair_at))
        elif n == 2:
            moves = ((0, 64, part + pair_at + 64), (64, 128, 2 * part + pair_at))
        else:
            moves = tuple((k * HD, HD, k * part + shared_at) for k in range(3))
        return [
            pltpu.make_async_copy(
                kept.at[start : start + rows, :], qkv_out.at[ds(where, rows, HD), :], local.at[6 + 2 * n + k]
            )
            for k, (start, rows, where) in enumerate(moves)
        ]

    give_side(proj)
    take_far(heads_a)
    finish(feeds[2], run(place_feed, 2))
    take_level(shared)
    take_far(heads_b)
    give_side(heads_a)
    for i in range(4, len(rounds)):
        vec_step(i)
    pltpu.make_async_copy(vec, vec_out, local.at[7]).start()
    take_far(shared)
    give_side(heads_b)
    finish(feeds[1], run(place_feed, 1))
    give_side(shared)
    finish(proj, place_proj)
    finish(heads_a, run(place, 1))
    finish(heads_b, run(place, 2))
    finish(shared, run(place, 3))

    for i in range(3):
        sent(small_own, small_send.at[i])
    for t in range(tensors):
        ag_sends(t)
    for k, slot in ((1, 0), (2, 1)):
        sent(fp.at[slot], unit_send.at[k, 2])
    for n in range(4):
        for k in (0, 2):
            sent(op.at[4 * n + k], unit_send.at[3 + n, k])
    sent(feeds[2][2].at[own_half(2 * PIECE), :], unit_send.at[2, 8 + rounds_far])
    for unit_of in feeds + smalls:
        unit_sends(unit_of)
    for i in range(count // TILE):
        r = rows_of(i, TILE)
        pltpu.make_async_copy(x.at[r, :], output.at[r, :], tile_a.at[i]).wait()
    for s in range(3):
        for copy in place_feed(s):
            copy.wait()
    place_proj()[0].wait()
    for n in range(1, 4):
        for copy in place(n):
            copy.wait()
    pltpu.make_async_copy(vec, vec_out, local.at[7]).wait()


def per_device(
    dp, tokens, segment, ln1_gain, ln1_bias, w_qkv, b_qv, w_out, b_out, ln2_gain, ln2_bias, w_up, b_up, w_down, b_down,
    cotangent,
):
    mp = 4
    me = lax.axis_index("mp")
    count, width = cotangent.shape
    part = width // mp
    feed = w_up.shape[1]
    bits = dp.bit_length() - 1
    far = bits - 2
    small_own = jnp.pad(b_up.reshape(-1, part), ((8, 0), (0, 0)))
    place = lax.broadcasted_iota(jnp.int32, small_own.shape, 0) * part + lax.broadcasted_iota(
        jnp.int32, small_own.shape, 1
    )
    for i, piece in reversed(list(enumerate((ln1_gain, ln1_bias, b_qv[0], b_qv[1], b_out, ln2_gain, ln2_bias, b_down)))):
        small_own = jnp.where(place < (i + 1) * part, piece[None, :], small_own)
    qkv_own = w_qkv.swapaxes(1, 2)

    def shape(*dims, kind=BF16):
        return jax.ShapeDtypeStruct(dims, kind)

    def room(*dims, kind=BF16):
        return pltpu.VMEM(dims, kind)

    unit_rows = 2 * PIECE
    tensors = 4 + 2 * (feed // PIECE)
    dma = pltpu.SemaphoreType.DMA
    outs = [
        shape(count, width), shape(count, width, kind=F32), shape(feed, width), shape(width, feed), shape(part, width),
        shape(3 * part, width), shape(16, width, kind=F32), shape(count, mp * feed), shape(count, width, kind=F32),
    ]

    def unit_rooms(rows, slots, lead):
        return [
            room(slots, rows, width), room(*lead, rows, width), room(*lead, rows, width),
            room(*lead, rows // 2, width),
        ]

    scratch = [
        room(mp, 8 + mp, part), room(3, width, width), room(width, width), room(mp, width, feed), room(mp, feed, width),
        *[room(count, width) for _ in range(8)],
        room(count, width, kind=F32), room(count, mp * feed), room(2, count, PIECE),
        room(count // LEN, LEN, LEN, kind=F32), room(count // LEN, 128, LEN, kind=F32), room(16, width, kind=F32),
        room(1 + 2 + bits, 16, width, kind=F32),
        *unit_rooms(unit_rows, 8, (3,)), *unit_rooms(part, 16, (4,)),
        dma((tensors,)), dma((tensors, 9)), dma((tensors, 9)), dma((3,)), dma((3,)), dma((15,)), dma((3, 1 + width // PIECE)), dma((2,)), dma((4,)), dma((4,)), dma((4,)),
        dma((7, 9 + max(far, 1))), dma((7, 9 + max(far, 1))), dma((2 + bits,)), dma((2 + bits,)),
        pltpu.SemaphoreType.REGULAR, pltpu.SemaphoreType.REGULAR((7, 3 + max(far, 1))),
    ]
    args = (
        small_own, qkv_own, w_out, w_up, w_down, tokens, cotangent, segment.reshape(-1, LEN),
    )
    results = pl.pallas_call(
        functools.partial(layer_kernel, dp),
        out_shape=outs,
        in_specs=[HBM] * 7 + [VMEM],
        out_specs=[HBM] * len(outs),
        scratch_shapes=scratch,
        compiler_params=pltpu.CompilerParams(
            vmem_limit_bytes=VMEM_LIMIT, collective_id=0, has_side_effects=True
        ),
    )(*args)
    output, grad_x, g_down, g_up, proj, attn, vec = results[:7]
    eight = lax.dynamic_slice_in_dim(vec[:8], me * part, part, 1)
    grad_b_up = lax.dynamic_slice_in_dim(vec, 8 + me, 1, 0).reshape(-1)
    g_qkv = attn.reshape(3, part, width).swapaxes(1, 2).astype(F32)
    return (
        output, grad_x, eight[0], eight[1], g_qkv, eight[2:4], proj.astype(F32), eight[4], eight[5], eight[6],
        g_up.astype(F32), grad_b_up, g_down.astype(F32), eight[7],
    )


def solution(mesh):
    rows = P(("dp", "mp"), None)
    return jax.shard_map(
        functools.partial(per_device, mesh.shape["dp"]),
        mesh=mesh,
        in_specs=(
            P("dp", None), P("dp"), P("mp"), P("mp"), P(None, None, "mp"), P(None, "mp"), P("mp", None), P("mp"),
            P("mp"), P("mp"), P(None, "mp"), P("mp"), P("mp", None), P("mp"), rows,
        ),
        out_specs=(
            rows, rows, P("mp"), P("mp"), P(None, None, "mp"), P(None, "mp"), P("mp", None), P("mp"), P("mp"), P("mp"),
            P(None, "mp"), P("mp"), P("mp", None), P("mp"),
        ),
        check_vma=False,
    )
```

```python
import functools

import jax
import jax.numpy as jnp
from jax import lax
from jax.experimental import pallas as pl
from jax.experimental.pallas import tpu as pltpu
from jax.sharding import PartitionSpec as P

HD = 64
LEN = 512
PIECE = 256
TILE = 256
F32 = jnp.float32
BF16 = jnp.bfloat16
MESH = pl.DeviceIdType.MESH
VMEM_LIMIT = 67043328
HBM = pl.BlockSpec(memory_space=pl.ANY)
VMEM = pl.BlockSpec(memory_space=pltpu.VMEM)


def nn(left, right):
    return jnp.dot(left, right, preferred_element_type=F32)


def nt(left, right):
    return lax.dot_general(left, right, (((1,), (1,)), ((), ())), preferred_element_type=F32)


def tn(left, right):
    return lax.dot_general(left, right, (((0,), (0,)), ((), ())), preferred_element_type=F32)


def ds(start, size, step=None):
    if isinstance(start, int):
        return pl.ds(start, size)
    return pl.ds(pl.multiple_of(start, step or size), size)


def rows_of(index, count):
    return ds(index * count, count)


def normal_of(values):
    centered = values - jnp.mean(values, axis=-1, keepdims=True)
    spread = jnp.mean(centered * centered, axis=-1, keepdims=True)
    inverse = lax.rsqrt(spread + 1e-06)
    return centered * inverse, inverse


def norm_input_back(normal, inverse, scaled):
    inner = jnp.mean(scaled * normal, axis=-1, keepdims=True)
    return inverse * (scaled - jnp.mean(scaled, axis=-1, keepdims=True) - normal * inner)


def column_sum(values):
    return jnp.sum(values, axis=0, keepdims=True)


def each(count, body):
    lax.fori_loop(0, count, lambda i, carry: (body(i), carry)[1], 0)


def at_steps(index, table):
    for step, actions in table.items():

        @pl.when(index == step)
        def _(actions=actions):
            for action in actions:
                action()


def add_into(target, *sources):
    rows = target.shape[0]
    tile = 64 if rows % 64 == 0 else 48

    def step(i):
        r = rows_of(i, tile)
        value = target[r, :].astype(F32)
        for source in sources:
            value += source[r, :].astype(F32)
        target[r, :] = value.astype(BF16)

    each(rows // tile, step)


def layer_kernel(
    dp, small_own, qkv_own, out_own, up_own, down_own, tokens, cot_hbm, segment,
    output, grad_x, down_out, up_out, proj_out, qkv_out, vec_out, act_hbm, hidden_hbm,
    small, wqkv, w_out, w_up, w_down, x, cot, normed, qs, ks, vs, attended, n2, hid, gup, act, bias,
    stat_rows, vec, vec_recv, fp, fcr, fyr, fxr, op, ocr, oyr, oxr,
    ag_local, ag_send, ag_recv, small_send, small_recv, local, feed_done, act_sem, tile_a, tile_b, tile_c, unit_send, unit_recv,
    vec_send, vec_got, credit, ready,
):
    me, d = lax.axis_index("mp"), lax.axis_index("dp")
    y, c = me // 2, me % 2
    count, width = x.shape
    part = width // 4
    half = width // 2
    sequences = count // LEN
    xb, zb = d % 2, (d // 2) % 2

    def across(bit):
        return d + bit - 2 * bit * ((d // bit) % 2)

    partner, above = (d, me + 1 - 2 * c), (d, me + 2 - 4 * y)
    diagonal = (d, 3 - me)
    side, level = (across(1), me), (across(2), me)
    far = [(across(bit), me) for bit in [1 << i for i in range(2, 12)] if bit < dp]
    peers = [partner, above, diagonal, side, level] + far
    barrier = pltpu.get_barrier_semaphore()
    for peer in peers:
        pl.semaphore_signal(barrier, inc=1, device_id=peer, device_id_type=MESH)
    pl.semaphore_wait(barrier, len(peers))

    def remote(source, target, send, recv, device):
        return pltpu.make_async_remote_copy(
            src_ref=source, dst_ref=target, send_sem=send, recv_sem=recv, device_id=device, device_id_type=MESH
        )

    def got(region, recv):
        remote(region, region, recv, recv, partner).wait_recv()

    def sent(region, send):
        remote(region, region, send, send, partner).wait_send()

    quarter = zb * 2 + xb
    q_side, q_level, q_diag = zb * 2 + 1 - xb, (1 - zb) * 2 + xb, 3 - quarter
    tensors = 4 + 2 * (w_up.shape[2] // PIECE)
    q_in, k_in, v_in, o_in = range(4)
    ups, downs = range(4, tensors, 2), range(5, tensors, 2)

    def window(ref, t, q, start):
        piece = (t - 4) // 2 * PIECE
        if t in ups:
            rows = width if q is None else width // 4
            return ref.at[*start, ds(0 if q is None else q * rows, rows), ds(piece, PIECE)]
        rows = PIECE if q is None else PIECE // 4
        return ref.at[*start, ds(piece + (0 if q is None else q * rows), rows, PIECE // 4), :]

    def own(t, q=None):
        if t > o_in:
            return window(up_own if t in ups else down_own, t, q, ())
        rows = ds(0, part) if q is None else rows_of(q, part // 4)
        return out_own.at[rows, :] if t == o_in else qkv_own.at[t, rows, :]

    def region(t, m, q=None):
        if t > o_in:
            return window(w_up if t in ups else w_down, t, q, (m,))
        rows = part if q is None else part // 4
        where = ds(m * part + (0 if q is None else q * rows), rows, part // 4)
        return w_out.at[where, :] if t == o_in else wqkv.at[t, where, :]

    m_core, m_y, m_diag = me + 1 - 2 * c, me + 2 - 4 * y, 3 - me
    through_side = [t in (q_in, v_in) or t in ups for t in range(tensors)]

    for i, peer in enumerate((diagonal, above, partner)):
        remote(small_own, small.at[me], small_send.at[i], small_recv.at[i], peer).start()
    pltpu.make_async_copy(small_own, small.at[me], local.at[0]).start()
    pltpu.make_async_copy(tokens.at[ds(me * count, count), :], x, local.at[1]).start()
    for t in range(tensors):
        remote(own(t, quarter), region(t, me, quarter), ag_send.at[t, 1], ag_recv.at[t, 1], above).start()
        pltpu.make_async_copy(own(t), region(t, me), ag_local.at[t]).start()
        remote(own(t), region(t, me), ag_send.at[t, 0], ag_recv.at[t, 0], partner).start()
    pltpu.make_async_copy(cot_hbm, cot, local.at[2]).start()

    def pass_on(t, q, k, device):
        where = region(t, m_y, q)
        remote(where, where, ag_send.at[t, k], ag_recv.at[t, k], device).start()

    def ag_y(t):
        got(region(t, m_y, quarter), ag_recv.at[t, 1])
        pass_on(t, quarter, 2, side)
        pass_on(t, quarter, 3, level)
        pass_on(t, quarter, 4, partner)

    def ag_side(t):
        got(region(t, m_y, q_side), ag_recv.at[t, 2])
        if not through_side[t]:
            pass_on(t, q_side, 7, level)
        pass_on(t, q_side, 5, partner)

    def ag_level(t):
        got(region(t, m_y, q_level), ag_recv.at[t, 3])
        if through_side[t]:
            pass_on(t, q_level, 7, side)
        pass_on(t, q_level, 6, partner)

    def ag_diag(t):
        got(region(t, m_y, q_diag), ag_recv.at[t, 7])
        pass_on(t, q_diag, 8, partner)

    def ag_near(t):
        pltpu.make_async_copy(own(t), region(t, me), ag_local.at[t]).wait()
        got(region(t, m_core), ag_recv.at[t, 0])

    def ag_rest(t):
        for k, q in ((4, quarter), (5, q_side), (6, q_level), (8, q_diag)):
            got(region(t, m_diag, q), ag_recv.at[t, k])

    def ag_sends(t):
        sent(own(t), ag_send.at[t, 0])
        sent(own(t, quarter), ag_send.at[t, 1])
        for k in range(2, 9):
            sent(own(t, quarter), ag_send.at[t, k])

    vec[...] = jnp.zeros_like(vec)
    for s in range(sequences):
        mine = segment[pl.ds(me * sequences + s, 1), :].astype(F32)
        column = jnp.broadcast_to(mine, (128, LEN)).T[:, :1]
        row_ids = lax.broadcasted_iota(jnp.int32, (LEN, LEN), 0)
        col_ids = lax.broadcasted_iota(jnp.int32, (LEN, LEN), 1)
        allowed = ((column == mine) & (mine != 0.0)) | (row_ids == col_ids)
        bias[s] = jnp.where(allowed, 0.0, -1e30)
        hid[rows_of(s, LEN), :128] = jnp.zeros((LEN, 128), F32)
    pltpu.make_async_copy(small_own, small.at[me], local.at[0]).wait()
    for i, m in enumerate((m_diag, m_y, m_core)):
        got(small.at[m], small_recv.at[i])
    place_row = lax.broadcasted_iota(jnp.int32, (part, width), 0)
    place_column = lax.broadcasted_iota(jnp.int32, (part, width), 1)
    vec_recv[0] = jnp.zeros(vec_recv.shape[1:], F32)
    for m in range(4):
        into = jnp.where(place_column == place_row + m * part, 1.0, 0.0).astype(BF16)
        vec_recv[0, :8, :] += nn(small[m, :8, :], into)
        for owner in range(4):
            vec_recv[0, 8 + owner : 9 + owner, :] += nn(small[owner, 8 + m : 9 + m, :], into)
    vectors = vec_recv[0]
    pltpu.make_async_copy(tokens.at[ds(0, count), :], x, local.at[1]).wait()
    g1, b1, b_query, b_value, b_out, g2, b2, b_down = (vectors[i : i + 1] for i in range(8))

    def ln_one(i):
        r = rows_of(i, TILE)
        normal, _ = normal_of(x[r, :].astype(F32))
        normed[r, :] = (normal * g1 + b1).astype(BF16)

    each(count // TILE, ln_one)
    lane = lax.broadcasted_iota(jnp.int32, (LEN, 128), 1)
    first = lane < HD
    pairs = half // 128

    def project(side_of, table):
        columns = ds(side_of * half, half, 128)

        def step(i):
            r = rows_of(i, LEN)
            value = normed[r, :]
            biases = vec_recv.at[0]
            query = nt(value, wqkv[0, columns, :]) + biases[2:3, columns]
            qs[r, columns] = (query.astype(BF16).astype(F32) * (HD**-0.5)).astype(BF16)
            ks[r, columns] = nt(value, wqkv[1, columns, :]).astype(BF16)
            vs[r, columns] = (nt(value, wqkv[2, columns, :]) + biases[3:4, columns]).astype(BF16)
            at_steps(i, table)

        each(count // LEN, step)

    def attend(side_of, table):
        def step(i):
            s, p = i // pairs, side_of * pairs + i % pairs
            r, cols = rows_of(s, LEN), rows_of(p, 128)
            q2, k2, v2 = qs[r, cols], ks[r, cols], vs[r, cols]
            results = []
            kept = hid[r, :128]
            for part_of in range(2):
                mine = first if part_of == 0 else ~first
                scores = nt(jnp.where(mine, q2, jnp.zeros_like(q2)), k2) + bias[s]
                top = jnp.max(scores, axis=-1, keepdims=True)
                expo = jnp.exp(scores - top)
                total = jnp.sum(expo, axis=-1, keepdims=True)
                results.append(nn(expo.astype(BF16), v2) * (1.0 / total))
                kept = jnp.where(lane == 2 * p + part_of, top + jnp.log(total), kept)
            hid[r, :128] = kept
            attended[r, cols] = jnp.where(first, results[0], results[1]).astype(BF16)
            at_steps(i, table)

        each(sequences * pairs, step)

    def run(function, *args):
        return functools.partial(function, *args)

    def near(t):
        return [run(ag_side, t), run(ag_level, t)]

    for t in (q_in, k_in, v_in):
        ag_near(t)
    ag_y(q_in)
    project(y, {0: [run(ag_y, k_in)], 1: [run(ag_y, v_in)]})
    attend(
        y,
        {
            0: near(q_in),
            2: near(k_in),
            3: [*near(v_in), run(ag_y, ups[0]), run(ag_y, downs[0]), run(ag_y, o_in)],
            4: [run(ag_diag, q_in)],
            5: [run(ag_diag, k_in)],
        },
    )
    ag_diag(v_in)
    for t in (q_in, k_in, v_in):
        ag_rest(t)
    project(1 - y, {0: near(ups[0]), 1: near(downs[0])})
    attend(
        1 - y,
        {
            0: [run(ag_y, ups[1])],
            1: [*near(o_in), run(ag_y, downs[1])],
            3: [run(ag_diag, ups[0])],
            4: [run(ag_diag, downs[0])],
            5: [*near(ups[1]), run(ag_diag, o_in)],
        },
    )
    for s in range(sequences):
        stat_rows[s] = hid[rows_of(s, LEN), :128].T
    ag_near(o_in)
    ag_rest(o_in)

    def out_step(i):
        r = rows_of(i, TILE)
        value = x[r, :].astype(F32) + nn(attended[r, :], w_out[...]) + vec_recv[0, 4:5, :]
        hid[r, :] = value
        pltpu.make_async_copy(hid.at[r, :], hidden_hbm.at[r, :], tile_a.at[i]).start()
        normal, _ = normal_of(value)
        n2[r, :] = (normal * vec_recv[0, 5:6, :] + vec_recv[0, 6:7, :]).astype(BF16)
        at_steps(i, {0: [run(ag_y, ups[2]), run(ag_y, downs[2])], 2: near(downs[1])})

    each(count // TILE, out_step)
    for t in range(o_in + 1, tensors):
        ag_near(t)
    ag_rest(ups[0])
    ag_rest(downs[0])
    pltpu.make_async_copy(cot_hbm, cot, local.at[2]).wait()

    up_bias = vec_recv.at[0]
    feed_slots = 2
    rounds_far = max(len(far), 1)

    def unit(u, kept, cr, yr, xr):
        rows = kept.shape[0]
        return (u, rows, kept, cr, yr, xr)

    level_first = (1,)

    def order_of(unit_of):
        return (level, side, zb, xb) if unit_of[0] in level_first else (side, level, xb, zb)

    def own_half(unit_of):
        rows, (_, _, a, _) = unit_of[1], order_of(unit_of)
        return ds(a * (rows // 2), rows // 2, rows // 4)

    def other_half(unit_of):
        rows, (_, _, a, _) = unit_of[1], order_of(unit_of)
        return ds((1 - a) * (rows // 2), rows // 2, rows // 4)

    def own_quarter(unit_of):
        rows, (_, _, a, b) = unit_of[1], order_of(unit_of)
        return ds(a * (rows // 2) + b * (rows // 4), rows // 4)

    def other_quarter(unit_of):
        rows, (_, _, a, b) = unit_of[1], order_of(unit_of)
        return ds(a * (rows // 2) + (1 - b) * (rows // 4), rows // 4)

    def send_unit(u, k, source, target, device):
        remote(source, target, unit_send.at[u, k], unit_recv.at[u, k], device).start()

    def take_sum(unit_of):
        u, rows, kept, cr, yr, xr = unit_of
        got(cr, unit_recv.at[u, 2])
        got(yr, unit_recv.at[u, 1])
        add_into(kept, cr, yr)
        pl.semaphore_signal(ready.at[u, 2], inc=1, device_id=order_of(unit_of)[1], device_id_type=MESH)
        send_unit(u, 3, kept.at[other_half(unit_of), :], xr, order_of(unit_of)[0])

    def far_room(unit_of, i):
        u, rows, kept, cr, yr, xr = unit_of
        return cr.at[i * (rows // 4) : (i + 1) * (rows // 4), :]

    def send_far(unit_of, i):
        u, rows, kept, cr, yr, xr = unit_of
        pl.semaphore_wait(ready.at[u, 3 + i], 1)
        send_unit(u, 7 + i, kept.at[own_quarter(unit_of), :], far_room(unit_of, i), far[i])

    def take_side(unit_of):
        u, rows, kept, cr, yr, xr = unit_of
        for i in range(len(far)):
            pl.semaphore_signal(ready.at[u, 3 + i], inc=1, device_id=far[i], device_id_type=MESH)
        got(xr, unit_recv.at[u, 3])
        sent(xr, unit_send.at[u, 3])
        pl.semaphore_signal(ready.at[u, 0], inc=1, device_id=order_of(unit_of)[0], device_id_type=MESH)
        add_into(kept.at[own_half(unit_of), :], xr)
        pl.semaphore_wait(ready.at[u, 2], 1)
        send_unit(u, 4, kept.at[other_quarter(unit_of), :], yr.at[: rows // 4, :], order_of(unit_of)[1])

    def give_level(unit_of):
        u, rows, kept, cr, yr, xr = unit_of
        mine = kept.at[own_quarter(unit_of), :]
        pl.semaphore_wait(ready.at[u, 1], 1)
        send_unit(u, 5, mine, mine, order_of(unit_of)[1])
        pl.semaphore_wait(ready.at[u, 0], 1)
        send_unit(u, 6, mine, mine, order_of(unit_of)[0])

    def take_level(unit_of):
        u, rows, kept, cr, yr, xr = unit_of
        landed = yr.at[: rows // 4, :]
        got(landed, unit_recv.at[u, 4])
        sent(landed, unit_send.at[u, 4])
        pl.semaphore_signal(ready.at[u, 1], inc=1, device_id=order_of(unit_of)[1], device_id_type=MESH)
        mine = kept.at[own_quarter(unit_of), :]
        add_into(mine, landed)
        if far:
            send_far(unit_of, 0)
        else:
            give_level(unit_of)

    def take_far(unit_of):
        u, rows, kept, cr, yr, xr = unit_of
        mine = kept.at[own_quarter(unit_of), :]
        for i, _ in enumerate(far):
            landed = far_room(unit_of, i)
            got(landed, unit_recv.at[u, 7 + i])
            sent(mine, unit_send.at[u, 7 + i])
            add_into(mine, landed)
            if i + 1 < len(far):
                send_far(unit_of, i + 1)
        if far:
            give_level(unit_of)

    def give_side(unit_of):
        u, rows, kept, cr, yr, xr = unit_of
        other = kept.at[other_quarter(unit_of), :]
        got(other, unit_recv.at[u, 5])
        send_unit(u, 7 + rounds_far, other, other, order_of(unit_of)[0])

    def finish(unit_of, copies):
        u, rows, kept, cr, yr, xr = unit_of
        got(kept.at[own_quarter(unit_of), :], unit_recv.at[u, 6])
        got(kept.at[own_quarter(unit_of), :], unit_recv.at[u, 7 + rounds_far])
        for copy in copies():
            copy.start()

    def place_feed(sub):
        kept, piece = feeds[sub][2], slice(sub * PIECE, (sub + 1) * PIECE)
        blocks = [slice(k * PIECE, (k + 1) * PIECE) for k in range(width // PIECE)]
        moves = [(kept.at[:PIECE, :], down_out.at[piece, :])]
        moves += [(kept.at[PIECE:, block], up_out.at[block, piece]) for block in blocks]
        return [pltpu.make_async_copy(*move, feed_done.at[sub, k]) for k, move in enumerate(moves)]

    def place_proj():
        return [pltpu.make_async_copy(op.at[3], proj_out, local.at[6])]

    def unit_sends(unit_of):
        u, rows, kept, cr, yr, xr = unit_of
        sent(kept.at[own_half(unit_of), :] if u == 2 else kept, unit_send.at[u, 1])
        for k in (5, 6, 7 + rounds_far):
            sent(kept.at[own_quarter(unit_of), :], unit_send.at[u, k])

    feeds = [
        unit(s, fp.at[feed_slots + 3 + s], fcr.at[s], fyr.at[s], fxr.at[s]) for s in range(3)
    ]
    smalls = [
        unit(3 + n, op.at[4 * n + 3], ocr.at[n], oyr.at[n], oxr.at[n]) for n in range(4)
    ]
    proj, heads_a, heads_b, shared = smalls

    def feed_first(sub, slot):
        send_unit(sub, 0, fp.at[slot], fcr.at[sub], partner)

    def feed_second(sub, slot):
        got(fcr.at[sub], unit_recv.at[sub, 0])
        add_into(fp.at[slot], fcr.at[sub])
        pl.semaphore_signal(credit, inc=1, device_id=partner, device_id_type=MESH)

        @pl.when(sub < 2)
        def _():
            send_unit(sub, 1, fp.at[slot], fyr.at[sub], above)

        @pl.when(sub == 2)
        def _():
            send_unit(2, 8 + rounds_far, fp.at[slot, other_half(feeds[2]), :], fyr.at[2, own_half(feeds[2]), :], order_of(feeds[2])[0])

    def last_other():
        _, rows, _, _, yr, _ = feeds[2]
        passed = fp.at[feed_slots + 2]
        landed = yr.at[other_half(feeds[2]), :]
        got(landed, unit_recv.at[2, 8 + rounds_far])
        add_into(passed.at[own_half(feeds[2]), :], landed)
        send_unit(2, 1, passed.at[own_half(feeds[2]), :], yr.at[own_half(feeds[2]), :], above)

    def last_sum():
        u, rows, kept, cr, _, xr = feeds[2]
        got(cr, unit_recv.at[u, 2])
        add_into(kept, cr)
        for i in range(len(far)):
            pl.semaphore_signal(ready.at[u, 3 + i], inc=1, device_id=far[i], device_id_type=MESH)
        send_unit(u, 3, kept.at[other_half(feeds[2]), :], xr, order_of(feeds[2])[0])

    def last_both():
        u, rows, kept, _, yr, xr = feeds[2]
        mine, landed = kept.at[own_half(feeds[2]), :], yr.at[own_half(feeds[2]), :]
        got(xr, unit_recv.at[u, 3])
        sent(xr, unit_send.at[u, 3])
        pl.semaphore_signal(ready.at[u, 0], inc=1, device_id=order_of(feeds[2])[0], device_id_type=MESH)
        got(landed, unit_recv.at[u, 1])
        add_into(mine, xr, landed)
        pl.semaphore_signal(ready.at[u, 2], inc=1, device_id=order_of(feeds[2])[1], device_id_type=MESH)
        pl.semaphore_wait(ready.at[u, 2], 1)
        send_unit(u, 4, kept.at[other_quarter(feeds[2]), :], yr.at[: rows // 4, :], order_of(feeds[2])[1])

    def feed_third(sub, slot):
        pl.semaphore_wait(credit, 1)
        send_unit(sub, 2, fp.at[slot], fcr.at[sub], partner)

    steps = 12

    def feed_step(i):
        late, odd, sub = i // 6, i % 2, (i % 6) // 2
        m = 2 * jnp.where(late == 0, 1 - y, y) + jnp.where(odd == 0, 1 - c, c)
        slot = jnp.where(odd == 0, (i // 2) % feed_slots, feed_slots + 3 * late + sub)
        cols = rows_of(sub, PIECE)
        whole = rows_of(m * 3 + sub, PIECE)
        wu, wd = w_up[m, :, cols], w_down[m, cols, :]
        piece_bias = up_bias[pl.ds(8 + m, 1), cols]
        buffer = i % 2

        @pl.when(i >= 2)
        def _():
            pltpu.make_async_copy(act.at[buffer], act_hbm.at[:, whole], act_sem.at[buffer]).wait()

        @pl.when((i >= 4) & (odd == 0))
        def _():
            before = i - 4
            sent(fp.at[slot], unit_send.at[(before % 6) // 2, 2 * (before // 6)])

        def rows_step(j):
            r = rows_of(j, LEN)
            up = nn(n2[r, :], wu) + piece_bias
            half_cdf = 0.5 * (1.0 + lax.erf(up * (0.5**0.5)))
            slope = half_cdf + up * (jnp.exp(-0.5 * up * up) * 0.3989422804014327)
            act[buffer, r, :] = (up * half_cdf).astype(BF16)
            grad = (nt(cot[r, :], wd) * slope).astype(BF16)
            gup[r, whole] = grad
            vec[pl.ds(8 + m, 1), cols] += column_sum(grad.astype(F32))

        each(count // LEN, rows_step)
        pltpu.make_async_copy(act.at[buffer], act_hbm.at[:, whole], act_sem.at[buffer]).start()
        fp[slot, :PIECE, :] = tn(act[buffer], cot[...]).astype(BF16)
        product = tn(n2[...], gup[:, whole]).astype(BF16)
        for k in range(width // PIECE):
            fp[slot, PIECE:, k * PIECE : (k + 1) * PIECE] = product[k * PIECE : (k + 1) * PIECE, :]

        @pl.when((late == 0) & (odd == 0))
        def _():
            feed_first(sub, slot)

        @pl.when((late == 0) & (odd == 1))
        def _():
            feed_second(sub, slot)

        @pl.when((late == 1) & (odd == 0))
        def _():
            feed_third(sub, slot)

        at_steps(
            i,
            {
                0: [run(ag_diag, ups[1]), run(ag_diag, downs[1]), *near(ups[2])],
                1: [run(ag_rest, ups[1]), run(ag_rest, downs[1]), *near(downs[2])],
                3: [run(ag_diag, ups[2]), run(ag_diag, downs[2]), run(ag_rest, ups[2]), run(ag_rest, downs[2])],
                8: [run(take_sum, feeds[0])],
                9: [last_other],
            },
        )

    vec[8:16, :] = jnp.zeros_like(vec[8:16, :])
    each(steps, feed_step)
    for buffer in range(2):
        pltpu.make_async_copy(act.at[buffer], act_hbm.at[:, ds(0, PIECE)], act_sem.at[buffer]).wait()
    for i in range(count // TILE):
        r = rows_of(i, TILE)
        pltpu.make_async_copy(hid.at[r, :], hidden_hbm.at[r, :], tile_a.at[i]).wait()

    def hidden_step(i):
        r = rows_of(i, TILE)
        incoming = nt(gup[r, :width], w_up[0])
        for m in range(1, 4):
            incoming += nt(gup[r, m * width : (m + 1) * width], w_up[m])
        normal, inverse = normal_of(hid[r, :])
        wide = cot[r, :].astype(F32)
        grad = wide + norm_input_back(normal, inverse, incoming * vec_recv[0, 5:6, :])
        hid[r, :] = grad
        vec[4:5, :] += column_sum(grad)
        vec[5:6, :] += column_sum(incoming * normal)
        vec[6:7, :] += column_sum(incoming)
        vec[7:8, :] += column_sum(wide)
        narrow = grad.astype(BF16)
        gup[r, 3 * width :] = narrow
        n2[r, :] = nt(narrow, w_out[...]).astype(BF16)
        at_steps(i, {0: [last_sum, run(take_side, feeds[0])], 1: [run(take_sum, feeds[1])], 3: [run(take_level, feeds[0])]})

    each(count // TILE, hidden_step)
    product = tn(attended[...], gup[:, 3 * width :])
    for m in range(4):
        slot = 2 * jnp.where(y == m // 2, 1, 0) + jnp.where(c == m % 2, 1, 0)
        op[slot] = product[m * part : (m + 1) * part, :].astype(BF16)

    def small_first(n):
        send_unit(3 + n, 0, op.at[4 * n], ocr.at[n], partner)

    def small_second(n):
        got(ocr.at[n], unit_recv.at[3 + n, 0])
        add_into(op.at[4 * n + 1], ocr.at[n])
        pl.semaphore_signal(credit, inc=1, device_id=partner, device_id_type=MESH)
        send_unit(3 + n, 1, op.at[4 * n + 1], oyr.at[n], above)

    def small_third(n):
        pl.semaphore_wait(credit, 1)
        send_unit(3 + n, 2, op.at[4 * n + 2], ocr.at[n], partner)

    small_first(0)
    def attend_back(side_of, table):
        def step(i):
            s, p = i % sequences, side_of * pairs + 2 * (i // sequences) % pairs
            r, cols = rows_of(s, LEN), rows_of(p, 128)
            q2, k2, v2, d2 = qs[r, cols], ks[r, cols], vs[r, cols], n2[r, cols]
            rq, rk, rv = 0.0, 0.0, 0.0
            for part_of in range(2):
                mine = first if part_of == 0 else ~first
                qm = jnp.where(mine, q2, jnp.zeros_like(q2))
                km = jnp.where(mine, k2, jnp.zeros_like(k2))
                dm = jnp.where(mine, d2, jnp.zeros_like(d2))
                probs = jnp.exp(nt(k2, qm) + bias[s] - stat_rows[s, pl.ds(2 * p + part_of, 1), :])
                grad_probs = nt(v2, dm)
                inner = jnp.sum(probs * grad_probs, axis=0, keepdims=True)
                grad_scores = (probs * (grad_probs - inner)).astype(BF16)
                rv += nn(probs.astype(BF16), dm)
                rk += nn(grad_scores, qm)
                rq += tn(grad_scores, km)
            gup[r, cols] = (rq * (HD**-0.5)).astype(BF16)
            gup[r, ds(width + p * 128, 128)] = rk.astype(BF16)
            gup[r, ds(2 * width + p * 128, 128)] = rv.astype(BF16)
            at_steps(i, table)

        each(sequences * pairs, step)

    def weight_of_pair(side_of, p):
        first_column = side_of * half + p * 128
        grads = jnp.concatenate([gup[:, ds(k * width + first_column, 128)] for k in range(3)], axis=1)
        return tn(grads, normed[...]).astype(BF16)

    def slot_of(core, late):
        return jnp.where(c == core, 1, 0) + 2 * late

    def weight_of_outer(side_of, late):
        for core, p in ((0, 0), (1, 2)):
            product = weight_of_pair(side_of, p)
            slot = slot_of(core, late)
            op[4 + slot] = product[:part]
            op[8 + slot] = product[part:]

    def weight_of_shared(side_of, late):
        product = weight_of_pair(side_of, 1)
        for core in range(2):
            slot = slot_of(core, late)
            for k in range(3):
                start = k * 128 + core * HD
                op[12 + slot, k * HD : (k + 1) * HD, :] = product[start : start + HD]

    attend_back(
        1 - y,
        {
            0: [run(small_second, 0), run(small_third, 0), last_both],
            3: [
                run(weight_of_outer, 1 - y, 0), run(small_first, 1), run(small_first, 2), run(take_far, feeds[0]),
                run(take_sum, proj),
            ],
            2: [run(take_side, feeds[1])],
            4: [run(small_second, 1), run(small_second, 2), run(take_level, feeds[1])],
            5: [run(take_level, feeds[2])],
        },
    )
    weight_of_shared(1 - y, 0)
    small_first(3)
    attend_back(
        y,
        {
            0: [run(small_second, 3), run(give_side, feeds[0])],
            1: [run(take_side, proj)],
            3: [run(weight_of_outer, y, 1), run(small_third, 1), run(small_third, 2), run(take_far, feeds[1])],
            4: [run(take_sum, heads_a), run(take_level, proj)],
            5: [run(take_sum, heads_b)],
        },
    )
    weight_of_shared(y, 1)
    small_third(3)
    finish(feeds[0], run(place_feed, 0))

    def input_step(i):
        r = rows_of(i, TILE)
        q, k, v = gup[r, :width], gup[r, width : 2 * width], gup[r, 2 * width : 3 * width]
        incoming = nn(q, wqkv[0]) + nn(k, wqkv[1]) + nn(v, wqkv[2])
        normal, inverse = normal_of(x[r, :].astype(F32))
        hid[r, :] += norm_input_back(normal, inverse, incoming * vec_recv[0, 0:1, :])
        vec[0:1, :] += column_sum(incoming * normal)
        vec[1:2, :] += column_sum(incoming)
        vec[2:3, :] += column_sum(q.astype(F32))
        vec[3:4, :] += column_sum(v.astype(F32))
        pltpu.make_async_copy(hid.at[r, :], grad_x.at[r, :], tile_c.at[i]).start()
        pltpu.make_async_copy(act_hbm.at[r, :], gup.at[r, :], tile_b.at[i]).start()
        at_steps(
            i,
            {
                0: [run(take_far, feeds[2]), run(give_side, feeds[1])],
                1: [run(take_sum, shared)],
                2: [run(take_side, heads_a), run(take_far, proj)],
            },
        )

    each(count // TILE, input_step)

    def reload(i):
        r = rows_of(i, TILE)
        pltpu.make_async_copy(hid.at[r, :], grad_x.at[r, :], tile_c.at[i]).wait()
        pltpu.make_async_copy(hidden_hbm.at[r, :], hid.at[r, :], tile_a.at[i]).start()

    each(count // TILE, reload)
    b_down = vec_recv[0, 7:8, :]

    rounds = [partner, above, side, level] + far

    def vec_start(i):
        remote(vec, vec_recv.at[1 + i], vec_send.at[i], vec_got.at[i], rounds[i]).start()

    def vec_step(i):
        got(vec_recv.at[1 + i], vec_got.at[i])
        sent(vec, vec_send.at[i])
        vec[...] += vec_recv[1 + i]
        if i + 1 < len(rounds):
            vec_start(i + 1)

    vec_start(0)

    def output_step(i):
        r = rows_of(i, TILE)
        pltpu.make_async_copy(hidden_hbm.at[r, :], hid.at[r, :], tile_a.at[i]).wait()
        pltpu.make_async_copy(act_hbm.at[r, :], gup.at[r, :], tile_b.at[i]).wait()
        result = hid[r, :] + b_down
        for m in range(4):
            result += nn(gup[r, m * width : (m + 1) * width], w_down[m])
        x[r, :] = result.astype(BF16)
        pltpu.make_async_copy(x.at[r, :], output.at[r, :], tile_a.at[i]).start()
        at_steps(
            i,
            {
                0: [run(take_side, heads_b), run(give_side, feeds[2]), run(vec_step, 0)],
                1: [run(vec_step, 1)],
                2: [run(take_level, heads_a), run(take_side, shared), run(vec_step, 2)],
                3: [run(take_level, heads_b), run(vec_step, 3)],
            },
        )

    each(count // TILE, output_step)
    def place(n):
        kept = smalls[n][2]
        pair_at, shared_at = HD * c, 2 * HD * (1 - c)
        if n == 1:
            moves = ((0, 128, pair_at), (128, 64, part + pair_at))
        elif n == 2:
            moves = ((0, 64, part + pair_at + 64), (64, 128, 2 * part + pair_at))
        else:
            moves = tuple((k * HD, HD, k * part + shared_at) for k in range(3))
        return [
            pltpu.make_async_copy(
                kept.at[start : start + rows, :], qkv_out.at[ds(where, rows, HD), :], local.at[6 + 2 * n + k]
            )
            for k, (start, rows, where) in enumerate(moves)
        ]

    give_side(proj)
    take_far(heads_a)
    finish(feeds[2], run(place_feed, 2))
    take_level(shared)
    take_far(heads_b)
    give_side(heads_a)
    for i in range(4, len(rounds)):
        vec_step(i)
    pltpu.make_async_copy(vec, vec_out, local.at[7]).start()
    take_far(shared)
    give_side(heads_b)
    finish(feeds[1], run(place_feed, 1))
    give_side(shared)
    finish(proj, place_proj)
    finish(heads_a, run(place, 1))
    finish(heads_b, run(place, 2))
    finish(shared, run(place, 3))

    for i in range(3):
        sent(small_own, small_send.at[i])
    for t in range(tensors):
        ag_sends(t)
    for k, slot in ((1, 0), (2, 1)):
        sent(fp.at[slot], unit_send.at[k, 2])
    for n in range(4):
        for k in (0, 2):
            sent(op.at[4 * n + k], unit_send.at[3 + n, k])
    sent(feeds[2][2].at[own_half(feeds[2]), :], unit_send.at[2, 8 + rounds_far])
    for unit_of in feeds + smalls:
        unit_sends(unit_of)
    for i in range(count // TILE):
        r = rows_of(i, TILE)
        pltpu.make_async_copy(x.at[r, :], output.at[r, :], tile_a.at[i]).wait()
    for s in range(3):
        for copy in place_feed(s):
            copy.wait()
    place_proj()[0].wait()
    for n in range(1, 4):
        for copy in place(n):
            copy.wait()
    pltpu.make_async_copy(vec, vec_out, local.at[7]).wait()


def per_device(
    dp, tokens, segment, ln1_gain, ln1_bias, w_qkv, b_qv, w_out, b_out, ln2_gain, ln2_bias, w_up, b_up, w_down, b_down,
    cotangent,
):
    mp = 4
    me = lax.axis_index("mp")
    count, width = cotangent.shape
    part = width // mp
    feed = w_up.shape[1]
    bits = dp.bit_length() - 1
    far = bits - 2
    small_own = jnp.pad(b_up.reshape(-1, part), ((8, 0), (0, 0)))
    place = lax.broadcasted_iota(jnp.int32, small_own.shape, 0) * part + lax.broadcasted_iota(
        jnp.int32, small_own.shape, 1
    )
    for i, piece in reversed(list(enumerate((ln1_gain, ln1_bias, b_qv[0], b_qv[1], b_out, ln2_gain, ln2_bias, b_down)))):
        small_own = jnp.where(place < (i + 1) * part, piece[None, :], small_own)
    qkv_own = w_qkv.swapaxes(1, 2)

    def shape(*dims, kind=BF16):
        return jax.ShapeDtypeStruct(dims, kind)

    def room(*dims, kind=BF16):
        return pltpu.VMEM(dims, kind)

    unit_rows = 2 * PIECE
    tensors = 4 + 2 * (feed // PIECE)
    dma = pltpu.SemaphoreType.DMA
    outs = [
        shape(count, width), shape(count, width, kind=F32), shape(feed, width), shape(width, feed), shape(part, width),
        shape(3 * part, width), shape(16, width, kind=F32), shape(count, mp * feed), shape(count, width, kind=F32),
    ]

    def unit_rooms(rows, slots, lead):
        return [
            room(slots, rows, width), room(*lead, rows, width), room(*lead, rows, width),
            room(*lead, rows // 2, width),
        ]

    scratch = [
        room(mp, 8 + mp, part), room(3, width, width), room(width, width), room(mp, width, feed), room(mp, feed, width),
        *[room(count, width) for _ in range(8)],
        room(count, width, kind=F32), room(count, mp * feed), room(2, count, PIECE),
        room(count // LEN, LEN, LEN, kind=F32), room(count // LEN, 128, LEN, kind=F32), room(16, width, kind=F32),
        room(1 + 2 + bits, 16, width, kind=F32),
        *unit_rooms(unit_rows, 8, (3,)), *unit_rooms(part, 16, (4,)),
        dma((tensors,)), dma((tensors, 9)), dma((tensors, 9)), dma((3,)), dma((3,)), dma((15,)), dma((3, 1 + width // PIECE)), dma((2,)), dma((4,)), dma((4,)), dma((4,)),
        dma((7, 9 + max(far, 1))), dma((7, 9 + max(far, 1))), dma((2 + bits,)), dma((2 + bits,)),
        pltpu.SemaphoreType.REGULAR, pltpu.SemaphoreType.REGULAR((7, 3 + max(far, 1))),
    ]
    args = (
        small_own, qkv_own, w_out, w_up, w_down, tokens, cotangent, segment.reshape(-1, LEN),
    )
    results = pl.pallas_call(
        functools.partial(layer_kernel, dp),
        out_shape=outs,
        in_specs=[HBM] * 7 + [VMEM],
        out_specs=[HBM] * len(outs),
        scratch_shapes=scratch,
        compiler_params=pltpu.CompilerParams(
            vmem_limit_bytes=VMEM_LIMIT, collective_id=0, has_side_effects=True
        ),
    )(*args)
    output, grad_x, g_down, g_up, proj, attn, vec = results[:7]
    eight = lax.dynamic_slice_in_dim(vec[:8], me * part, part, 1)
    grad_b_up = lax.dynamic_slice_in_dim(vec, 8 + me, 1, 0).reshape(-1)
    g_qkv = attn.reshape(3, part, width).swapaxes(1, 2).astype(F32)
    return (
        output, grad_x, eight[0], eight[1], g_qkv, eight[2:4], proj.astype(F32), eight[4], eight[5], eight[6],
        g_up.astype(F32), grad_b_up, g_down.astype(F32), eight[7],
    )


def solution(mesh):
    rows = P(("dp", "mp"), None)
    return jax.shard_map(
        functools.partial(per_device, mesh.shape["dp"]),
        mesh=mesh,
        in_specs=(
            P("dp", None), P("dp"), P("mp"), P("mp"), P(None, None, "mp"), P(None, "mp"), P("mp", None), P("mp"),
            P("mp"), P("mp"), P(None, "mp"), P("mp"), P("mp", None), P("mp"), rows,
        ),
        out_specs=(
            rows, rows, P("mp"), P("mp"), P(None, None, "mp"), P(None, "mp"), P("mp", None), P("mp"), P("mp"), P("mp"),
            P(None, "mp"), P("mp"), P("mp", None), P("mp"),
        ),
        check_vma=False,
    )
```

```python
import functools

import jax
import jax.numpy as jnp
from jax import lax
from jax.experimental import pallas as pl
from jax.experimental.pallas import tpu as pltpu
from jax.sharding import PartitionSpec as P

HD = 64
LEN = 512
PIECE = 256
TILE = 256
F32 = jnp.float32
BF16 = jnp.bfloat16
MESH = pl.DeviceIdType.MESH
VMEM_LIMIT = 67043328
HBM = pl.BlockSpec(memory_space=pl.ANY)
VMEM = pl.BlockSpec(memory_space=pltpu.VMEM)


def nn(left, right):
    return jnp.dot(left, right, preferred_element_type=F32)


def nt(left, right):
    return lax.dot_general(left, right, (((1,), (1,)), ((), ())), preferred_element_type=F32)


def tn(left, right):
    return lax.dot_general(left, right, (((0,), (0,)), ((), ())), preferred_element_type=F32)


def ds(start, size, step=None):
    if isinstance(start, int):
        return pl.ds(start, size)
    return pl.ds(pl.multiple_of(start, step or size), size)


def rows_of(index, count):
    return ds(index * count, count)


def normal_of(values):
    centered = values - jnp.mean(values, axis=-1, keepdims=True)
    spread = jnp.mean(centered * centered, axis=-1, keepdims=True)
    inverse = lax.rsqrt(spread + 1e-06)
    return centered * inverse, inverse


def norm_input_back(normal, inverse, scaled):
    inner = jnp.mean(scaled * normal, axis=-1, keepdims=True)
    return inverse * (scaled - jnp.mean(scaled, axis=-1, keepdims=True) - normal * inner)


def column_sum(values):
    return jnp.sum(values, axis=0, keepdims=True)


def each(count, body):
    lax.fori_loop(0, count, lambda i, carry: (body(i), carry)[1], 0)


def at_steps(index, table):
    for step, actions in table.items():

        @pl.when(index == step)
        def _(actions=actions):
            for action in actions:
                action()


def add_into(target, *sources):
    rows = target.shape[0]
    tile = 64 if rows % 64 == 0 else 48

    def step(i):
        r = rows_of(i, tile)
        value = target[r, :].astype(F32)
        for source in sources:
            value += source[r, :].astype(F32)
        target[r, :] = value.astype(BF16)

    each(rows // tile, step)


def layer_kernel(
    dp, small_own, qkv_own, out_own, up_own, down_own, tokens, cot_hbm, segment,
    output, grad_x, down_out, up_out, proj_out, qkv_out, vec_out, act_hbm, hidden_hbm,
    small, wqkv, w_out, w_up, w_down, x, cot, normed, qs, ks, vs, attended, n2, hid, gup, act, bias,
    stat_rows, vec, vec_recv, fp, fcr, fyr, fxr, op, ocr, oyr, oxr,
    ag_local, ag_send, ag_recv, small_send, small_recv, local, feed_done, act_sem, tile_a, tile_b, tile_c, unit_send, unit_recv,
    vec_send, vec_got, credit, ready,
):
    me, d = lax.axis_index("mp"), lax.axis_index("dp")
    y, c = me // 2, me % 2
    count, width = x.shape
    part = width // 4
    half = width // 2
    sequences = count // LEN
    xb, zb = d % 2, (d // 2) % 2

    def across(bit):
        return d + bit - 2 * bit * ((d // bit) % 2)

    partner, above = (d, me + 1 - 2 * c), (d, me + 2 - 4 * y)
    diagonal = (d, 3 - me)
    side, level = (across(1), me), (across(2), me)
    far = [(across(bit), me) for bit in [1 << i for i in range(2, 12)] if bit < dp]
    peers = [partner, above, diagonal, side, level] + far
    barrier = pltpu.get_barrier_semaphore()
    for peer in peers:
        pl.semaphore_signal(barrier, inc=1, device_id=peer, device_id_type=MESH)
    pl.semaphore_wait(barrier, len(peers))

    def remote(source, target, send, recv, device):
        return pltpu.make_async_remote_copy(
            src_ref=source, dst_ref=target, send_sem=send, recv_sem=recv, device_id=device, device_id_type=MESH
        )

    def got(region, recv):
        remote(region, region, recv, recv, partner).wait_recv()

    def sent(region, send):
        remote(region, region, send, send, partner).wait_send()

    quarter = zb * 2 + xb
    q_side, q_level, q_diag = zb * 2 + 1 - xb, (1 - zb) * 2 + xb, 3 - quarter
    tensors = 4 + 2 * (w_up.shape[2] // PIECE)
    q_in, k_in, v_in, o_in = range(4)
    ups, downs = range(4, tensors, 2), range(5, tensors, 2)

    def window(ref, t, q, start):
        piece = (t - 4) // 2 * PIECE
        if t in ups:
            rows = width if q is None else width // 4
            return ref.at[*start, ds(0 if q is None else q * rows, rows), ds(piece, PIECE)]
        rows = PIECE if q is None else PIECE // 4
        return ref.at[*start, ds(piece + (0 if q is None else q * rows), rows, PIECE // 4), :]

    def own(t, q=None):
        if t > o_in:
            return window(up_own if t in ups else down_own, t, q, ())
        rows = ds(0, part) if q is None else rows_of(q, part // 4)
        return out_own.at[rows, :] if t == o_in else qkv_own.at[t, rows, :]

    def region(t, m, q=None):
        if t > o_in:
            return window(w_up if t in ups else w_down, t, q, (m,))
        rows = part if q is None else part // 4
        where = ds(m * part + (0 if q is None else q * rows), rows, part // 4)
        return w_out.at[where, :] if t == o_in else wqkv.at[t, where, :]

    m_core, m_y, m_diag = me + 1 - 2 * c, me + 2 - 4 * y, 3 - me
    through_side = [t in (q_in, v_in) or t in ups for t in range(tensors)]

    for i, peer in enumerate((diagonal, above, partner)):
        remote(small_own, small.at[me], small_send.at[i], small_recv.at[i], peer).start()
    pltpu.make_async_copy(small_own, small.at[me], local.at[0]).start()
    pltpu.make_async_copy(tokens.at[ds(me * count, count), :], x, local.at[1]).start()
    for t in range(tensors):
        remote(own(t, quarter), region(t, me, quarter), ag_send.at[t, 1], ag_recv.at[t, 1], above).start()
        pltpu.make_async_copy(own(t), region(t, me), ag_local.at[t]).start()
        remote(own(t), region(t, me), ag_send.at[t, 0], ag_recv.at[t, 0], partner).start()
    pltpu.make_async_copy(cot_hbm, cot, local.at[2]).start()

    def pass_on(t, q, k, device):
        where = region(t, m_y, q)
        remote(where, where, ag_send.at[t, k], ag_recv.at[t, k], device).start()

    def ag_y(t):
        got(region(t, m_y, quarter), ag_recv.at[t, 1])
        pass_on(t, quarter, 2, side)
        pass_on(t, quarter, 3, level)
        pass_on(t, quarter, 4, partner)

    def ag_side(t):
        got(region(t, m_y, q_side), ag_recv.at[t, 2])
        if not through_side[t]:
            pass_on(t, q_side, 7, level)
        pass_on(t, q_side, 5, partner)

    def ag_level(t):
        got(region(t, m_y, q_level), ag_recv.at[t, 3])
        if through_side[t]:
            pass_on(t, q_level, 7, side)
        pass_on(t, q_level, 6, partner)

    def ag_diag(t):
        got(region(t, m_y, q_diag), ag_recv.at[t, 7])
        pass_on(t, q_diag, 8, partner)

    def ag_near(t):
        pltpu.make_async_copy(own(t), region(t, me), ag_local.at[t]).wait()
        got(region(t, m_core), ag_recv.at[t, 0])

    def ag_rest(t):
        for k, q in ((4, quarter), (5, q_side), (6, q_level), (8, q_diag)):
            got(region(t, m_diag, q), ag_recv.at[t, k])

    def ag_sends(t):
        sent(own(t), ag_send.at[t, 0])
        sent(own(t, quarter), ag_send.at[t, 1])
        for k in range(2, 9):
            sent(own(t, quarter), ag_send.at[t, k])

    vec[...] = jnp.zeros_like(vec)
    for s in range(sequences):
        mine = segment[pl.ds(me * sequences + s, 1), :].astype(F32)
        column = jnp.broadcast_to(mine, (128, LEN)).T[:, :1]
        row_ids = lax.broadcasted_iota(jnp.int32, (LEN, LEN), 0)
        col_ids = lax.broadcasted_iota(jnp.int32, (LEN, LEN), 1)
        allowed = ((column == mine) & (mine != 0.0)) | (row_ids == col_ids)
        bias[s] = jnp.where(allowed, 0.0, -1e30)
        hid[rows_of(s, LEN), :128] = jnp.zeros((LEN, 128), F32)
    pltpu.make_async_copy(small_own, small.at[me], local.at[0]).wait()
    for i, m in enumerate((m_diag, m_y, m_core)):
        got(small.at[m], small_recv.at[i])
    place_row = lax.broadcasted_iota(jnp.int32, (part, width), 0)
    place_column = lax.broadcasted_iota(jnp.int32, (part, width), 1)
    vec_recv[0] = jnp.zeros(vec_recv.shape[1:], F32)
    for m in range(4):
        into = jnp.where(place_column == place_row + m * part, 1.0, 0.0).astype(BF16)
        vec_recv[0, :8, :] += nn(small[m, :8, :], into)
        for owner in range(4):
            vec_recv[0, 8 + owner : 9 + owner, :] += nn(small[owner, 8 + m : 9 + m, :], into)
    vectors = vec_recv[0]
    pltpu.make_async_copy(tokens.at[ds(0, count), :], x, local.at[1]).wait()
    g1, b1, b_query, b_value, b_out, g2, b2, b_down = (vectors[i : i + 1] for i in range(8))

    def ln_one(i):
        r = rows_of(i, TILE)
        normal, _ = normal_of(x[r, :].astype(F32))
        normed[r, :] = (normal * g1 + b1).astype(BF16)

    each(count // TILE, ln_one)
    lane = lax.broadcasted_iota(jnp.int32, (LEN, 128), 1)
    first = lane < HD
    pairs = half // 128

    def project(side_of, table):
        columns = ds(side_of * half, half, 128)

        def step(i):
            r = rows_of(i, LEN)
            value = normed[r, :]
            biases = vec_recv.at[0]
            query = nt(value, wqkv[0, columns, :]) + biases[2:3, columns]
            qs[r, columns] = (query.astype(BF16).astype(F32) * (HD**-0.5)).astype(BF16)
            ks[r, columns] = nt(value, wqkv[1, columns, :]).astype(BF16)
            vs[r, columns] = (nt(value, wqkv[2, columns, :]) + biases[3:4, columns]).astype(BF16)
            at_steps(i, table)

        each(count // LEN, step)

    def attend(side_of, table):
        def step(i):
            s, p = i // pairs, side_of * pairs + i % pairs
            r, cols = rows_of(s, LEN), rows_of(p, 128)
            q2, k2, v2 = qs[r, cols], ks[r, cols], vs[r, cols]
            results = []
            kept = hid[r, :128]
            for part_of in range(2):
                mine = first if part_of == 0 else ~first
                scores = nt(jnp.where(mine, q2, jnp.zeros_like(q2)), k2) + bias[s]
                top = jnp.max(scores, axis=-1, keepdims=True)
                expo = jnp.exp(scores - top)
                total = jnp.sum(expo, axis=-1, keepdims=True)
                results.append(nn(expo.astype(BF16), v2) * (1.0 / total))
                kept = jnp.where(lane == 2 * p + part_of, top + jnp.log(total), kept)
            hid[r, :128] = kept
            attended[r, cols] = jnp.where(first, results[0], results[1]).astype(BF16)
            at_steps(i, table)

        each(sequences * pairs, step)

    def run(function, *args):
        return functools.partial(function, *args)

    def near(t):
        return [run(ag_side, t), run(ag_level, t)]

    for t in (q_in, k_in, v_in):
        ag_near(t)
    ag_y(q_in)
    project(y, {0: [run(ag_y, k_in)], 1: [run(ag_y, v_in)]})
    attend(
        y,
        {
            0: near(q_in),
            2: near(k_in),
            3: [*near(v_in), run(ag_y, ups[0]), run(ag_y, downs[0]), run(ag_y, o_in)],
            4: [run(ag_diag, q_in)],
            5: [run(ag_diag, k_in)],
        },
    )
    ag_diag(v_in)
    for t in (q_in, k_in, v_in):
        ag_rest(t)
    project(1 - y, {0: near(ups[0]), 1: near(downs[0])})
    attend(
        1 - y,
        {
            0: [run(ag_y, ups[1])],
            1: [*near(o_in), run(ag_y, downs[1])],
            3: [run(ag_diag, ups[0])],
            4: [run(ag_diag, downs[0])],
            5: [*near(ups[1]), run(ag_diag, o_in)],
        },
    )
    for s in range(sequences):
        stat_rows[s] = hid[rows_of(s, LEN), :128].T
    ag_near(o_in)
    ag_rest(o_in)

    def out_step(i):
        r = rows_of(i, TILE)
        value = x[r, :].astype(F32) + nn(attended[r, :], w_out[...]) + vec_recv[0, 4:5, :]
        hid[r, :] = value
        pltpu.make_async_copy(hid.at[r, :], hidden_hbm.at[r, :], tile_a.at[i]).start()
        normal, _ = normal_of(value)
        n2[r, :] = (normal * vec_recv[0, 5:6, :] + vec_recv[0, 6:7, :]).astype(BF16)
        at_steps(i, {0: [run(ag_y, ups[2]), run(ag_y, downs[2])], 2: near(downs[1])})

    each(count // TILE, out_step)
    for t in range(o_in + 1, tensors):
        ag_near(t)
    ag_rest(ups[0])
    ag_rest(downs[0])
    pltpu.make_async_copy(cot_hbm, cot, local.at[2]).wait()

    up_bias = vec_recv.at[0]
    feed_slots = 2
    rounds_far = max(len(far), 1)

    def unit(u, kept, cr, yr, xr):
        rows = kept.shape[0]
        return (u, rows, kept, cr, yr, xr)

    level_first = (1,)

    def order_of(unit_of):
        return (level, side, zb, xb) if unit_of[0] in level_first else (side, level, xb, zb)

    def own_half(unit_of):
        rows, (_, _, a, _) = unit_of[1], order_of(unit_of)
        return ds(a * (rows // 2), rows // 2, rows // 4)

    def other_half(unit_of):
        rows, (_, _, a, _) = unit_of[1], order_of(unit_of)
        return ds((1 - a) * (rows // 2), rows // 2, rows // 4)

    def own_quarter(unit_of):
        rows, (_, _, a, b) = unit_of[1], order_of(unit_of)
        return ds(a * (rows // 2) + b * (rows // 4), rows // 4)

    def other_quarter(unit_of):
        rows, (_, _, a, b) = unit_of[1], order_of(unit_of)
        return ds(a * (rows // 2) + (1 - b) * (rows // 4), rows // 4)

    def send_unit(u, k, source, target, device):
        remote(source, target, unit_send.at[u, k], unit_recv.at[u, k], device).start()

    def take_sum(unit_of):
        u, rows, kept, cr, yr, xr = unit_of
        got(cr, unit_recv.at[u, 2])
        got(yr, unit_recv.at[u, 1])
        add_into(kept, cr, yr)
        pl.semaphore_signal(ready.at[u, 2], inc=1, device_id=order_of(unit_of)[1], device_id_type=MESH)
        send_unit(u, 3, kept.at[other_half(unit_of), :], xr, order_of(unit_of)[0])

    def far_room(unit_of, i):
        u, rows, kept, cr, yr, xr = unit_of
        return cr.at[i * (rows // 4) : (i + 1) * (rows // 4), :]

    def send_far(unit_of, i):
        u, rows, kept, cr, yr, xr = unit_of
        pl.semaphore_wait(ready.at[u, 3 + i], 1)
        send_unit(u, 7 + i, kept.at[own_quarter(unit_of), :], far_room(unit_of, i), far[i])

    def take_side(unit_of):
        u, rows, kept, cr, yr, xr = unit_of
        for i in range(len(far)):
            pl.semaphore_signal(ready.at[u, 3 + i], inc=1, device_id=far[i], device_id_type=MESH)
        got(xr, unit_recv.at[u, 3])
        sent(xr, unit_send.at[u, 3])
        pl.semaphore_signal(ready.at[u, 0], inc=1, device_id=order_of(unit_of)[0], device_id_type=MESH)
        add_into(kept.at[own_half(unit_of), :], xr)
        pl.semaphore_wait(ready.at[u, 2], 1)
        send_unit(u, 4, kept.at[other_quarter(unit_of), :], yr.at[: rows // 4, :], order_of(unit_of)[1])

    def give_level(unit_of):
        u, rows, kept, cr, yr, xr = unit_of
        mine = kept.at[own_quarter(unit_of), :]
        pl.semaphore_wait(ready.at[u, 1], 1)
        send_unit(u, 5, mine, mine, order_of(unit_of)[1])
        pl.semaphore_wait(ready.at[u, 0], 1)
        send_unit(u, 6, mine, mine, order_of(unit_of)[0])

    def take_level(unit_of):
        u, rows, kept, cr, yr, xr = unit_of
        landed = yr.at[: rows // 4, :]
        got(landed, unit_recv.at[u, 4])
        sent(landed, unit_send.at[u, 4])
        pl.semaphore_signal(ready.at[u, 1], inc=1, device_id=order_of(unit_of)[1], device_id_type=MESH)
        mine = kept.at[own_quarter(unit_of), :]
        add_into(mine, landed)
        if far:
            send_far(unit_of, 0)
        else:
            give_level(unit_of)

    def take_far(unit_of):
        u, rows, kept, cr, yr, xr = unit_of
        mine = kept.at[own_quarter(unit_of), :]
        for i, _ in enumerate(far):
            landed = far_room(unit_of, i)
            got(landed, unit_recv.at[u, 7 + i])
            sent(mine, unit_send.at[u, 7 + i])
            add_into(mine, landed)
            if i + 1 < len(far):
                send_far(unit_of, i + 1)
        if far:
            give_level(unit_of)

    def give_side(unit_of):
        u, rows, kept, cr, yr, xr = unit_of
        other = kept.at[other_quarter(unit_of), :]
        got(other, unit_recv.at[u, 5])
        send_unit(u, 7 + rounds_far, other, other, order_of(unit_of)[0])

    def finish(unit_of, copies):
        u, rows, kept, cr, yr, xr = unit_of
        got(kept.at[own_quarter(unit_of), :], unit_recv.at[u, 6])
        got(kept.at[own_quarter(unit_of), :], unit_recv.at[u, 7 + rounds_far])
        for copy in copies():
            copy.start()

    def place_feed(sub):
        kept, piece = feeds[sub][2], slice(sub * PIECE, (sub + 1) * PIECE)
        blocks = [slice(k * PIECE, (k + 1) * PIECE) for k in range(width // PIECE)]
        moves = [(kept.at[:PIECE, :], down_out.at[piece, :])]
        moves += [(kept.at[PIECE:, block], up_out.at[block, piece]) for block in blocks]
        return [pltpu.make_async_copy(*move, feed_done.at[sub, k]) for k, move in enumerate(moves)]

    def place_proj():
        return [pltpu.make_async_copy(op.at[3], proj_out, local.at[6])]

    def unit_sends(unit_of):
        u, rows, kept, cr, yr, xr = unit_of
        sent(kept.at[own_half(unit_of), :] if u == 2 else kept, unit_send.at[u, 1])
        for k in (5, 6, 7 + rounds_far):
            sent(kept.at[own_quarter(unit_of), :], unit_send.at[u, k])

    feeds = [
        unit(s, fp.at[feed_slots + 3 + s], fcr.at[s], fyr.at[s], fxr.at[s]) for s in range(3)
    ]
    smalls = [
        unit(3 + n, op.at[4 * n + 3], ocr.at[n], oyr.at[n], oxr.at[n]) for n in range(4)
    ]
    proj, heads_a, heads_b, shared = smalls

    def feed_first(sub, slot):
        send_unit(sub, 0, fp.at[slot], fcr.at[sub], partner)

    def feed_second(sub, slot):
        got(fcr.at[sub], unit_recv.at[sub, 0])
        add_into(fp.at[slot], fcr.at[sub])
        pl.semaphore_signal(credit, inc=1, device_id=partner, device_id_type=MESH)

        @pl.when(sub < 2)
        def _():
            send_unit(sub, 1, fp.at[slot], fyr.at[sub], above)

        @pl.when(sub == 2)
        def _():
            send_unit(2, 8 + rounds_far, fp.at[slot, other_half(feeds[2]), :], fyr.at[2, own_half(feeds[2]), :], order_of(feeds[2])[0])

    def last_other():
        _, rows, _, _, yr, _ = feeds[2]
        passed = fp.at[feed_slots + 2]
        landed = yr.at[other_half(feeds[2]), :]
        got(landed, unit_recv.at[2, 8 + rounds_far])
        add_into(passed.at[own_half(feeds[2]), :], landed)
        send_unit(2, 1, passed.at[own_half(feeds[2]), :], yr.at[own_half(feeds[2]), :], above)

    def last_sum():
        u, rows, kept, cr, _, xr = feeds[2]
        got(cr, unit_recv.at[u, 2])
        add_into(kept, cr)
        for i in range(len(far)):
            pl.semaphore_signal(ready.at[u, 3 + i], inc=1, device_id=far[i], device_id_type=MESH)
        send_unit(u, 3, kept.at[other_half(feeds[2]), :], xr, order_of(feeds[2])[0])

    def last_both():
        u, rows, kept, _, yr, xr = feeds[2]
        mine, landed = kept.at[own_half(feeds[2]), :], yr.at[own_half(feeds[2]), :]
        got(xr, unit_recv.at[u, 3])
        sent(xr, unit_send.at[u, 3])
        pl.semaphore_signal(ready.at[u, 0], inc=1, device_id=order_of(feeds[2])[0], device_id_type=MESH)
        got(landed, unit_recv.at[u, 1])
        add_into(mine, xr, landed)
        pl.semaphore_signal(ready.at[u, 2], inc=1, device_id=order_of(feeds[2])[1], device_id_type=MESH)
        pl.semaphore_wait(ready.at[u, 2], 1)
        send_unit(u, 4, kept.at[other_quarter(feeds[2]), :], yr.at[: rows // 4, :], order_of(feeds[2])[1])

    def feed_third(sub, slot):
        pl.semaphore_wait(credit, 1)
        send_unit(sub, 2, fp.at[slot], fcr.at[sub], partner)

    steps = 12

    def feed_step(i):
        late, odd, sub = i // 6, i % 2, (i % 6) // 2
        m = 2 * jnp.where(late == 0, 1 - y, y) + jnp.where(odd == 0, 1 - c, c)
        slot = jnp.where(odd == 0, (i // 2) % feed_slots, feed_slots + 3 * late + sub)
        cols = rows_of(sub, PIECE)
        whole = rows_of(m * 3 + sub, PIECE)
        wu, wd = w_up[m, :, cols], w_down[m, cols, :]
        piece_bias = up_bias[pl.ds(8 + m, 1), cols]
        buffer = i % 2

        @pl.when(i >= 2)
        def _():
            pltpu.make_async_copy(act.at[buffer], act_hbm.at[:, whole], act_sem.at[buffer]).wait()

        @pl.when((i >= 4) & (odd == 0))
        def _():
            before = i - 4
            sent(fp.at[slot], unit_send.at[(before % 6) // 2, 2 * (before // 6)])

        def rows_step(j):
            r = rows_of(j, LEN)
            up = nn(n2[r, :], wu) + piece_bias
            half_cdf = 0.5 * (1.0 + lax.erf(up * (0.5**0.5)))
            slope = half_cdf + up * (jnp.exp(-0.5 * up * up) * 0.3989422804014327)
            act[buffer, r, :] = (up * half_cdf).astype(BF16)
            grad = (nt(cot[r, :], wd) * slope).astype(BF16)
            gup[r, whole] = grad
            vec[pl.ds(8 + m, 1), cols] += column_sum(grad.astype(F32))

        each(count // LEN, rows_step)
        pltpu.make_async_copy(act.at[buffer], act_hbm.at[:, whole], act_sem.at[buffer]).start()
        fp[slot, :PIECE, :] = tn(act[buffer], cot[...]).astype(BF16)
        product = tn(n2[...], gup[:, whole]).astype(BF16)
        for k in range(width // PIECE):
            fp[slot, PIECE:, k * PIECE : (k + 1) * PIECE] = product[k * PIECE : (k + 1) * PIECE, :]

        @pl.when((late == 0) & (odd == 0))
        def _():
            feed_first(sub, slot)

        @pl.when((late == 0) & (odd == 1))
        def _():
            feed_second(sub, slot)

        @pl.when((late == 1) & (odd == 0))
        def _():
            feed_third(sub, slot)

        at_steps(
            i,
            {
                0: [run(ag_diag, ups[1]), run(ag_diag, downs[1]), *near(ups[2])],
                1: [run(ag_rest, ups[1]), run(ag_rest, downs[1]), *near(downs[2])],
                3: [run(ag_diag, ups[2]), run(ag_diag, downs[2]), run(ag_rest, ups[2]), run(ag_rest, downs[2])],
                8: [run(take_sum, feeds[0])],
                9: [last_other],
            },
        )

    vec[8:16, :] = jnp.zeros_like(vec[8:16, :])
    each(steps, feed_step)
    for buffer in range(2):
        pltpu.make_async_copy(act.at[buffer], act_hbm.at[:, ds(0, PIECE)], act_sem.at[buffer]).wait()
    for i in range(count // TILE):
        r = rows_of(i, TILE)
        pltpu.make_async_copy(hid.at[r, :], hidden_hbm.at[r, :], tile_a.at[i]).wait()

    def hidden_step(i):
        r = rows_of(i, TILE)
        incoming = nt(gup[r, :width], w_up[0])
        for m in range(1, 4):
            incoming += nt(gup[r, m * width : (m + 1) * width], w_up[m])
        normal, inverse = normal_of(hid[r, :])
        wide = cot[r, :].astype(F32)
        grad = wide + norm_input_back(normal, inverse, incoming * vec_recv[0, 5:6, :])
        hid[r, :] = grad
        vec[4:5, :] += column_sum(grad)
        vec[5:6, :] += column_sum(incoming * normal)
        vec[6:7, :] += column_sum(incoming)
        vec[7:8, :] += column_sum(wide)
        narrow = grad.astype(BF16)
        gup[r, 3 * width :] = narrow
        n2[r, :] = nt(narrow, w_out[...]).astype(BF16)
        at_steps(i, {0: [last_sum, run(take_side, feeds[0])], 1: [run(take_sum, feeds[1])], 3: [run(take_level, feeds[0])]})

    each(count // TILE, hidden_step)
    product = tn(attended[...], gup[:, 3 * width :])
    for m in range(4):
        slot = 2 * jnp.where(y == m // 2, 1, 0) + jnp.where(c == m % 2, 1, 0)
        op[slot] = product[m * part : (m + 1) * part, :].astype(BF16)

    def small_first(n):
        send_unit(3 + n, 0, op.at[4 * n], ocr.at[n], partner)

    def small_second(n):
        got(ocr.at[n], unit_recv.at[3 + n, 0])
        add_into(op.at[4 * n + 1], ocr.at[n])
        pl.semaphore_signal(credit, inc=1, device_id=partner, device_id_type=MESH)
        send_unit(3 + n, 1, op.at[4 * n + 1], oyr.at[n], above)

    def small_third(n):
        pl.semaphore_wait(credit, 1)
        send_unit(3 + n, 2, op.at[4 * n + 2], ocr.at[n], partner)

    small_first(0)
    def attend_back(side_of, table):
        def step(i):
            s, p = i % sequences, side_of * pairs + 2 * (i // sequences) % pairs
            r, cols = rows_of(s, LEN), rows_of(p, 128)
            q2, k2, v2, d2 = qs[r, cols], ks[r, cols], vs[r, cols], n2[r, cols]
            rq, rk, rv = 0.0, 0.0, 0.0
            for part_of in range(2):
                mine = first if part_of == 0 else ~first
                qm = jnp.where(mine, q2, jnp.zeros_like(q2))
                km = jnp.where(mine, k2, jnp.zeros_like(k2))
                dm = jnp.where(mine, d2, jnp.zeros_like(d2))
                probs = jnp.exp(nt(k2, qm) + bias[s] - stat_rows[s, pl.ds(2 * p + part_of, 1), :])
                grad_probs = nt(v2, dm)
                inner = jnp.sum(probs * grad_probs, axis=0, keepdims=True)
                grad_scores = (probs * (grad_probs - inner)).astype(BF16)
                rv += nn(probs.astype(BF16), dm)
                rk += nn(grad_scores, qm)
                rq += tn(grad_scores, km)
            gup[r, cols] = (rq * (HD**-0.5)).astype(BF16)
            gup[r, ds(width + p * 128, 128)] = rk.astype(BF16)
            gup[r, ds(2 * width + p * 128, 128)] = rv.astype(BF16)
            at_steps(i, table)

        each(sequences * pairs, step)

    def weight_of_pair(side_of, p):
        first_column = side_of * half + p * 128
        grads = jnp.concatenate([gup[:, ds(k * width + first_column, 128)] for k in range(3)], axis=1)
        return tn(grads, normed[...]).astype(BF16)

    def slot_of(core, late):
        return jnp.where(c == core, 1, 0) + 2 * late

    def weight_of_outer(side_of, late):
        for core, p in ((0, 0), (1, 2)):
            product = weight_of_pair(side_of, p)
            slot = slot_of(core, late)
            op[4 + slot] = product[:part]
            op[8 + slot] = product[part:]

    def weight_of_shared(side_of, late):
        product = weight_of_pair(side_of, 1)
        for core in range(2):
            slot = slot_of(core, late)
            for k in range(3):
                start = k * 128 + core * HD
                op[12 + slot, k * HD : (k + 1) * HD, :] = product[start : start + HD]

    attend_back(
        1 - y,
        {
            0: [run(small_second, 0), run(small_third, 0), last_both],
            3: [
                run(weight_of_outer, 1 - y, 0), run(small_first, 1), run(small_first, 2), run(take_far, feeds[0]),
                run(take_sum, proj),
            ],
            2: [run(take_side, feeds[1])],
            4: [run(small_second, 1), run(small_second, 2), run(take_level, feeds[1])],
            5: [run(take_level, feeds[2])],
        },
    )
    weight_of_shared(1 - y, 0)
    small_first(3)
    attend_back(
        y,
        {
            0: [run(small_second, 3), run(give_side, feeds[0])],
            1: [run(take_side, proj)],
            3: [run(weight_of_outer, y, 1), run(small_third, 1), run(small_third, 2), run(take_far, feeds[1])],
            4: [run(take_sum, heads_a), run(take_level, proj)],
            5: [run(take_sum, heads_b)],
        },
    )
    weight_of_shared(y, 1)
    small_third(3)
    finish(feeds[0], run(place_feed, 0))

    def input_step(i):
        r = rows_of(i, TILE)
        q, k, v = gup[r, :width], gup[r, width : 2 * width], gup[r, 2 * width : 3 * width]
        incoming = nn(q, wqkv[0]) + nn(k, wqkv[1]) + nn(v, wqkv[2])
        normal, inverse = normal_of(x[r, :].astype(F32))
        hid[r, :] += norm_input_back(normal, inverse, incoming * vec_recv[0, 0:1, :])
        vec[0:1, :] += column_sum(incoming * normal)
        vec[1:2, :] += column_sum(incoming)
        vec[2:3, :] += column_sum(q.astype(F32))
        vec[3:4, :] += column_sum(v.astype(F32))
        pltpu.make_async_copy(hid.at[r, :], grad_x.at[r, :], tile_c.at[i]).start()
        pltpu.make_async_copy(act_hbm.at[r, :], gup.at[r, :], tile_b.at[i]).start()
        at_steps(
            i,
            {
                0: [run(take_far, feeds[2]), run(give_side, feeds[1])],
                1: [run(take_sum, shared)],
                2: [run(take_side, heads_a), run(take_far, proj)],
            },
        )

    each(count // TILE, input_step)

    def reload(i):
        r = rows_of(i, TILE)
        pltpu.make_async_copy(hid.at[r, :], grad_x.at[r, :], tile_c.at[i]).wait()
        pltpu.make_async_copy(hidden_hbm.at[r, :], hid.at[r, :], tile_a.at[i]).start()

    each(count // TILE, reload)
    b_down = vec_recv[0, 7:8, :]

    rounds = [partner, above, side, level] + far

    def vec_start(i):
        remote(vec, vec_recv.at[1 + i], vec_send.at[i], vec_got.at[i], rounds[i]).start()

    def vec_step(i):
        got(vec_recv.at[1 + i], vec_got.at[i])
        sent(vec, vec_send.at[i])
        vec[...] += vec_recv[1 + i]
        if i + 1 < len(rounds):
            vec_start(i + 1)

    vec_start(0)

    def output_step(i):
        r = rows_of(i, TILE)
        pltpu.make_async_copy(hidden_hbm.at[r, :], hid.at[r, :], tile_a.at[i]).wait()
        pltpu.make_async_copy(act_hbm.at[r, :], gup.at[r, :], tile_b.at[i]).wait()
        result = hid[r, :] + b_down
        for m in range(4):
            result += nn(gup[r, m * width : (m + 1) * width], w_down[m])
        x[r, :] = result.astype(BF16)
        pltpu.make_async_copy(x.at[r, :], output.at[r, :], tile_a.at[i]).start()
        at_steps(
            i,
            {
                0: [run(take_side, heads_b), run(give_side, feeds[2]), run(vec_step, 0)],
                1: [run(vec_step, 1)],
                2: [run(take_level, heads_a), run(take_side, shared), run(vec_step, 2)],
                3: [run(take_level, heads_b), run(vec_step, 3)],
            },
        )

    each(count // TILE, output_step)
    def place(n):
        kept = smalls[n][2]
        pair_at, shared_at = HD * c, 2 * HD * (1 - c)
        if n == 1:
            moves = ((0, 128, pair_at), (128, 64, part + pair_at))
        elif n == 2:
            moves = ((0, 64, part + pair_at + 64), (64, 128, 2 * part + pair_at))
        else:
            moves = tuple((k * HD, HD, k * part + shared_at) for k in range(3))
        return [
            pltpu.make_async_copy(
                kept.at[start : start + rows, :], qkv_out.at[ds(where, rows, HD), :], local.at[6 + 2 * n + k]
            )
            for k, (start, rows, where) in enumerate(moves)
        ]

    give_side(proj)
    take_far(heads_a)
    finish(feeds[2], run(place_feed, 2))
    take_level(shared)
    take_far(heads_b)
    give_side(heads_a)
    for i in range(4, len(rounds)):
        vec_step(i)
    pltpu.make_async_copy(vec, vec_out, local.at[7]).start()
    take_far(shared)
    give_side(heads_b)
    finish(feeds[1], run(place_feed, 1))
    give_side(shared)
    finish(proj, place_proj)
    finish(heads_a, run(place, 1))
    finish(heads_b, run(place, 2))
    finish(shared, run(place, 3))

    for i in range(3):
        sent(small_own, small_send.at[i])
    for t in range(tensors):
        ag_sends(t)
    for k, slot in ((1, 0), (2, 1)):
        sent(fp.at[slot], unit_send.at[k, 2])
    for n in range(4):
        for k in (0, 2):
            sent(op.at[4 * n + k], unit_send.at[3 + n, k])
    sent(feeds[2][2].at[own_half(feeds[2]), :], unit_send.at[2, 8 + rounds_far])
    for unit_of in feeds + smalls:
        unit_sends(unit_of)
    for i in range(count // TILE):
        r = rows_of(i, TILE)
        pltpu.make_async_copy(x.at[r, :], output.at[r, :], tile_a.at[i]).wait()
    for s in range(3):
        for copy in place_feed(s):
            copy.wait()
    place_proj()[0].wait()
    for n in range(1, 4):
        for copy in place(n):
            copy.wait()
    pltpu.make_async_copy(vec, vec_out, local.at[7]).wait()


def per_device(
    dp, tokens, segment, ln1_gain, ln1_bias, w_qkv, b_qv, w_out, b_out, ln2_gain, ln2_bias, w_up, b_up, w_down, b_down,
    cotangent,
):
    mp = 4
    me = lax.axis_index("mp")
    count, width = cotangent.shape
    part = width // mp
    feed = w_up.shape[1]
    bits = dp.bit_length() - 1
    far = bits - 2
    small_own = jnp.pad(b_up.reshape(-1, part), ((8, 0), (0, 0)))
    place = lax.broadcasted_iota(jnp.int32, small_own.shape, 0) * part + lax.broadcasted_iota(
        jnp.int32, small_own.shape, 1
    )
    pieces = [
        ln1_gain[None], ln1_bias[None], b_qv[:1], b_qv[1:], b_out[None], ln2_gain[None], ln2_bias[None], b_down[None],
    ]
    for i, piece in reversed(list(enumerate(pieces))):
        small_own = jnp.where(place < (i + 1) * part, piece, small_own)
    qkv_own = w_qkv.swapaxes(1, 2)

    def shape(*dims, kind=BF16):
        return jax.ShapeDtypeStruct(dims, kind)

    def room(*dims, kind=BF16):
        return pltpu.VMEM(dims, kind)

    unit_rows = 2 * PIECE
    tensors = 4 + 2 * (feed // PIECE)
    dma = pltpu.SemaphoreType.DMA
    outs = [
        shape(count, width), shape(count, width, kind=F32), shape(feed, width), shape(width, feed), shape(part, width),
        shape(3 * part, width), shape(16, width, kind=F32), shape(count, mp * feed), shape(count, width, kind=F32),
    ]

    def unit_rooms(rows, slots, lead):
        return [
            room(slots, rows, width), room(*lead, rows, width), room(*lead, rows, width),
            room(*lead, rows // 2, width),
        ]

    scratch = [
        room(mp, 8 + mp, part), room(3, width, width), room(width, width), room(mp, width, feed), room(mp, feed, width),
        *[room(count, width) for _ in range(8)],
        room(count, width, kind=F32), room(count, mp * feed), room(2, count, PIECE),
        room(count // LEN, LEN, LEN, kind=F32), room(count // LEN, 128, LEN, kind=F32), room(16, width, kind=F32),
        room(1 + 2 + bits, 16, width, kind=F32),
        *unit_rooms(unit_rows, 8, (3,)), *unit_rooms(part, 16, (4,)),
        dma((tensors,)), dma((tensors, 9)), dma((tensors, 9)), dma((3,)), dma((3,)), dma((15,)), dma((3, 1 + width // PIECE)), dma((2,)), dma((4,)), dma((4,)), dma((4,)),
        dma((7, 9 + max(far, 1))), dma((7, 9 + max(far, 1))), dma((2 + bits,)), dma((2 + bits,)),
        pltpu.SemaphoreType.REGULAR, pltpu.SemaphoreType.REGULAR((7, 3 + max(far, 1))),
    ]
    args = (
        small_own, qkv_own, w_out, w_up, w_down, tokens, cotangent, segment.reshape(-1, LEN),
    )
    results = pl.pallas_call(
        functools.partial(layer_kernel, dp),
        out_shape=outs,
        in_specs=[HBM] * 7 + [VMEM],
        out_specs=[HBM] * len(outs),
        scratch_shapes=scratch,
        compiler_params=pltpu.CompilerParams(
            vmem_limit_bytes=VMEM_LIMIT, collective_id=0, has_side_effects=True
        ),
    )(*args)
    output, grad_x, g_down, g_up, proj, attn, vec = results[:7]
    eight = lax.dynamic_slice(vec, (0, me * part), (8, part))
    grad_b_up = lax.dynamic_slice_in_dim(vec, 8 + me, 1, 0).reshape(-1)
    g_qkv = attn.reshape(3, part, width).swapaxes(1, 2).astype(F32)
    return (
        output, grad_x, eight[0], eight[1], g_qkv, eight[2:4], proj.astype(F32), eight[4], eight[5], eight[6],
        g_up.astype(F32), grad_b_up, g_down.astype(F32), eight[7],
    )


def solution(mesh):
    rows = P(("dp", "mp"), None)
    return jax.shard_map(
        functools.partial(per_device, mesh.shape["dp"]),
        mesh=mesh,
        in_specs=(
            P("dp", None), P("dp"), P("mp"), P("mp"), P(None, None, "mp"), P(None, "mp"), P("mp", None), P("mp"),
            P("mp"), P("mp"), P(None, "mp"), P("mp"), P("mp", None), P("mp"), rows,
        ),
        out_specs=(
            rows, rows, P("mp"), P("mp"), P(None, None, "mp"), P(None, "mp"), P("mp", None), P("mp"), P("mp"), P("mp"),
            P(None, "mp"), P("mp"), P("mp", None), P("mp"),
        ),
        check_vma=False,
    )
```
